128 devices in a mesh: bead: 32 (over x, z, core), space: 4 (over y).
Axes of the slice: x: 4, y: 4, z: 4, core: 2. Of those that a mesh axis runs over, the one named last changes fastest.
Arguments:
- positions: float32 [32, 3, 1024], P('bead', None, 'space'), may hold values from -9 to 9
- momenta: float32 [32, 3, 1024], P('bead', None, 'space'), may hold values from -6 to 6
- species: int32 [1024], P('space'), may hold values from 0 to 1
- neighbours: int32 [32, 48, 1024], P('bead', None, 'space'), may hold values from 0 to 767
- counts: int32 [32, 1024], P('bead', 'space'), may hold values from 24 to 48
- exports: int32 [32, 4, 4, 128], P('bead', 'space'), may hold values from 0 to 255, as said below
- embed: float32 [2, 32], replicated, may hold values from -6 to 6
- radial_one_in: float32 [8, 64], replicated, may hold values from -2 to 2
- radial_one_out: float32 [64, 96], replicated, may hold values from -0.75 to 0.75
- mix_one: float32 [96, 32], replicated, may hold values from -0.625 to 0.625
- radial_two_in: float32 [8, 64], replicated, may hold values from -2 to 2
- radial_two_out: float32 [64, 96], replicated, may hold values from -0.75 to 0.75
- readout: float32 [96, 64], replicated, may hold values from -0.625 to 0.625
- energy_w: float32 [64], replicated, may hold values from -0.75 to 0.75
Outputs:
- new_positions: float32 [32, 3, 1024], P('bead', None, 'space')
- new_momenta: float32 [32, 3, 1024], P('bead', None, 'space')
The draws below stay inside these ranges and needn't reach their ends.
Inputs may be any that keep to these rules, and one draw needn't show every extreme that they name: `neighbours`: entries index the domain's slots: its 256 own atoms, then 128 ghost copies from each of the 4 source domains in order; entries at or past an atom's count are padding. `counts`: live slots of an atom. `exports`: for each bead, source and destination domain: 128 distinct rows of the source domain's atoms, in the order the destination stores them.
All inputs are finite; a program needn't handle non-finite values.
Results may differ from the reference program's by a relative error of at most 0.0003.
Values sent between devices are 32-bit elements; how exact they have to be, the bound alone decides.
A program may use at most 128 MiB of HBM per device.

```python
import math
import jax
import jax.numpy as jnp
from jax import lax

ATOMS_DEV = 256
NEIGH = 48
CH = 32
RAD_H = 64
NBASIS = 8
KINDS = 2
BEADS = 32
SPACE = 4
GHOST = 128
ATOMS = 1024


def draw_exports(key, part):
    row_keys = jax.random.split(key, BEADS * SPACE * SPACE)

    def one_row(row_key):
        return jax.random.permutation(row_key, ATOMS_DEV)[:GHOST]
    chosen = jax.vmap(one_row)(row_keys)
    return chosen.reshape(BEADS, SPACE, SPACE, GHOST).astype(jnp.int32)


def place_ends(values, key, low, largest):
    longest = values.shape.index(max(values.shape))
    spots = []
    for shift in (0, 1):
        where = [jax.random.randint(jax.random.fold_in(key, axis), (), 0, length) for axis, length in enumerate(values.shape)]
        where[longest] = (where[longest] + shift) % values.shape[longest]
        spots.append(tuple(where))
    return values.at[spots[0]].set(low).at[spots[1]].set(largest)


def block_levels(own_key, extent, shards, low, largest):
    gain, own = 1.0, jax.random.fold_in(own_key, 6)
    for position, shards_of in shards:
        draws = jnp.exp(jax.random.uniform(jax.random.fold_in(own, position), (shards_of,), jnp.float32, low / len(shards), largest / len(shards)))
        gain = gain * jnp.repeat(draws, extent[position] // shards_of).reshape([-1 if axis == position else 1 for axis in range(len(extent))])
    return gain


def gaussian(rng, shape, deviation, most, cuts=(), kind=jnp.bfloat16):
    values = deviation * jax.random.normal(rng, shape, jnp.float32)
    if cuts:
        values = values * block_levels(rng, shape, cuts, -0.22, 0.18)
    return jnp.clip(values, -most, most).astype(kind)


def setup_inputs(seed: int = 0) -> dict:
    keys = jax.random.split(jax.random.key(seed), 15)
    positions = gaussian(keys[0], (BEADS, 3, ATOMS), 1.5, 9.0, ((0, 32), (2, 4)), jnp.float32)
    momenta = gaussian(keys[1], (BEADS, 3, ATOMS), 1.0, 6.0, ((0, 32), (2, 4)), jnp.float32)
    species = place_ends(jax.random.randint(keys[2], (ATOMS,), 0, 2), jax.random.fold_in(keys[2], 1), 0, 1).astype(jnp.int32)
    neighbours = place_ends(jax.random.randint(keys[3], (BEADS, NEIGH, ATOMS), 0, ATOMS_DEV + SPACE * GHOST), jax.random.fold_in(keys[3], 1), 0, (ATOMS_DEV + SPACE * GHOST) - 1).astype(jnp.int32)
    counts = place_ends(jax.random.randint(keys[4], (BEADS, ATOMS), NEIGH // 2, NEIGH + 1), jax.random.fold_in(keys[4], 1), NEIGH // 2, NEIGH).astype(jnp.int32)
    exports = draw_exports(jax.random.fold_in(keys[14], 71), 0)
    embed = gaussian(keys[6], (KINDS, CH), 1.0, 6.0, (), jnp.float32)
    radial_one_in = gaussian(keys[7], (NBASIS, RAD_H), NBASIS ** -0.5, 2.0, (), jnp.float32)
    radial_one_out = gaussian(keys[8], (RAD_H, 3 * CH), RAD_H ** -0.5, 0.75, (), jnp.float32)
    mix_one = gaussian(keys[9], (3 * CH, CH), (3 * CH) ** -0.5, 0.625, (), jnp.float32)
    radial_two_in = gaussian(keys[10], (NBASIS, RAD_H), NBASIS ** -0.5, 2.0, (), jnp.float32)
    radial_two_out = gaussian(keys[11], (RAD_H, 3 * CH), RAD_H ** -0.5, 0.75, (), jnp.float32)
    readout = gaussian(keys[12], (3 * CH, RAD_H), (3 * CH) ** -0.5, 0.625, (), jnp.float32)
    energy_w = gaussian(keys[13], (RAD_H,), RAD_H ** -0.5, 0.75, (), jnp.float32)
    return {"positions": positions, "momenta": momenta, "species": species, "neighbours": neighbours, "counts": counts, "exports": exports, "embed": embed, "radial_one_in": radial_one_in, "radial_one_out": radial_one_out, "mix_one": mix_one, "radial_two_in": radial_two_in, "radial_two_out": radial_two_out, "readout": readout, "energy_w": energy_w}


rcut = 6.0
cycle_freq = 1.5
mass_oxygen = 15.999
mass_hydrogen = 1.008
highest = lax.Precision.HIGHEST

def harmonics(direction):
    comp_x, comp_y, comp_z = (direction[0], direction[1], direction[2])
    length_sq = comp_x * comp_x + comp_y * comp_y + comp_z * comp_z
    root_three = math.sqrt(3.0)
    root_fifteen = math.sqrt(15.0)
    root_five = math.sqrt(5.0)
    return jnp.stack([jnp.ones_like(comp_x), root_three * comp_x, root_three * comp_y, root_three * comp_z, root_fifteen * comp_x * comp_y, root_fifteen * comp_y * comp_z, root_fifteen * comp_x * comp_z, 0.5 * root_fifteen * (comp_x * comp_x - comp_y * comp_y), 0.5 * root_five * (3.0 * comp_z * comp_z - length_sq)], axis=0)

def invariants(center, slot_pos, slot_feat, indices, live_count, radial_in, radial_out):
    neigh_depth, breadth = indices.shape
    channels = slot_feat.shape[0]
    flat_index = indices.reshape(-1)
    nearby = jnp.take(slot_pos, flat_index, axis=1).reshape(3, neigh_depth, breadth)
    offset = nearby - center[:, None, :]
    distance = jnp.sqrt(lax.optimization_barrier(jnp.sum(offset * offset, axis=0)) + 1.0)
    direction = offset / distance[None]
    present = (lax.broadcasted_iota(jnp.int32, (neigh_depth, breadth), 0) < live_count[None, :]).astype(jnp.float32)
    scaled = jnp.clip(distance / rcut, 0.0, 1.0)
    envelope = (1.0 - scaled * scaled) ** 2 * present
    orders = jnp.arange(1, radial_in.shape[0] + 1).astype(jnp.float32)
    radial_basis = jnp.sin(orders[:, None, None] * math.pi * scaled[None]) / distance[None] * envelope[None]
    hidden = jax.nn.silu(jnp.einsum('nh,nkb->hkb', radial_in, radial_basis, precision=highest))
    radial = jnp.einsum('hw,hkb->wkb', radial_out, hidden, precision=highest)
    gathered = jnp.take(slot_feat, flat_index, axis=1).reshape(channels, neigh_depth, breadth)
    harmonic = harmonics(direction)
    norm_scale = 1.0 / math.sqrt(neigh_depth)
    pieces = []
    for degree, bounds in enumerate(((0, 1), (1, 4), (4, 9))):
        weighted = radial[degree * channels:(degree + 1) * channels] * gathered
        amplitude = jnp.einsum('ckb,mkb->cmb', weighted, harmonic[bounds[0]:bounds[1]], precision=highest) * norm_scale
        pieces.append(lax.optimization_barrier(jnp.sum(amplitude * amplitude, axis=1)))
    return jnp.concatenate(pieces, axis=0)

def domain_invariants(slot_pos, slot_feat, indices, live_count, radial_in, radial_out):
    atom_count = indices.shape[1]
    block_size = min(512, atom_count)
    block_count = atom_count // block_size
    centers = slot_pos[:, :atom_count].reshape(3, block_count, block_size).transpose(1, 0, 2)
    row_blocks = indices.reshape(indices.shape[0], block_count, block_size).transpose(1, 0, 2)
    alive_blocks = live_count.reshape(block_count, block_size)

    def one_block(inputs):
        return invariants(inputs[0], slot_pos, slot_feat, inputs[1], inputs[2], radial_in, radial_out)
    result = lax.map(jax.checkpoint(one_block), (centers, row_blocks, alive_blocks))
    return result.transpose(1, 0, 2).reshape(result.shape[1], atom_count)

def first_layer(invar, own_embed, mix_one):
    return own_embed + jax.nn.silu(jnp.dot(mix_one.T, invar, precision=highest))

def atom_energy(invar, readout, energy_w):
    return jnp.dot(energy_w, jax.nn.silu(jnp.dot(readout.T, invar, precision=highest)), precision=highest)

def atom_mass(species):
    return jnp.where(species == 0, mass_oxygen, mass_hydrogen).astype(jnp.float32)

def embed_of(species, embed):
    kinds_hot = (species[None, :] == jnp.arange(embed.shape[0], dtype=jnp.int32)[:, None]).astype(jnp.float32)
    return jnp.dot(embed.T, kinds_hot, precision=highest)

def mode_table(rows, bead_count):
    modes = jnp.arange(bead_count, dtype=jnp.int32)
    phase = rows[:, None] * modes[None, :] % bead_count
    angle = 2.0 * math.pi * phase.astype(jnp.float32) / bead_count
    half_beads = bead_count // 2
    table = jnp.where(modes[None] < half_beads, math.sqrt(2.0 / bead_count) * jnp.cos(angle), math.sqrt(2.0 / bead_count) * jnp.sin(angle))
    table = jnp.where(modes[None] == 0, 1.0 / math.sqrt(bead_count), table)
    table = jnp.where(modes[None] == half_beads, jnp.cos(angle) / math.sqrt(bead_count), table)
    return table

def time_step(bead_count):
    return bead_count / 3.0

def mode_rotation(bead_count):
    step_dt = time_step(bead_count)
    modes = jnp.arange(bead_count, dtype=jnp.int32)
    frequency = 2.0 * cycle_freq * jnp.sin(math.pi * modes.astype(jnp.float32) / bead_count)
    cosine = jnp.cos(frequency * step_dt)
    sine = jnp.sin(frequency * step_dt)
    reach = jnp.where(modes == 0, step_dt, sine / jnp.where(modes == 0, 1.0, frequency))
    stiffness = frequency * sine
    return (cosine, reach, stiffness)

def build_slots(values, export):
    feats = values.shape[0]
    blocks = values.reshape(feats, SPACE, ATOMS_DEV)

    def take_block(block_vals, export_rows):
        return jnp.take(block_vals, export_rows.reshape(-1), axis=1).reshape(feats, SPACE, GHOST)
    ghosts = jax.vmap(take_block, in_axes=(1, 0))(blocks, export)
    ghosts = jnp.transpose(ghosts, (2, 1, 0, 3)).reshape(SPACE, feats, SPACE * GHOST)
    return jnp.concatenate([jnp.transpose(blocks, (1, 0, 2)), ghosts], axis=2)

def bead_energy(pos, species, neigh, count, export, embed, radial_one_in, radial_one_out, mix_one, radial_two_in, radial_two_out, readout, energy_w):
    pos_slots = build_slots(pos, export)
    embed_slots = build_slots(embed_of(species, embed), export)
    neigh_domains = neigh.reshape(neigh.shape[0], SPACE, ATOMS_DEV).transpose(1, 0, 2)
    count_domains = count.reshape(SPACE, ATOMS_DEV)

    def first_pass(inputs):
        invar = domain_invariants(inputs[0], inputs[1], inputs[2], inputs[3], radial_one_in, radial_one_out)
        return first_layer(invar, inputs[1][:, :ATOMS_DEV], mix_one)
    layer_one = lax.map(first_pass, (pos_slots, embed_slots, neigh_domains, count_domains))
    channels = layer_one.shape[1]
    feat_slots = build_slots(layer_one.transpose(1, 0, 2).reshape(channels, SPACE * ATOMS_DEV), export)

    def second_pass(inputs):
        invar = domain_invariants(inputs[0], inputs[1], inputs[2], inputs[3], radial_two_in, radial_two_out)
        return jnp.sum(atom_energy(invar, readout, energy_w))
    return jnp.sum(lax.map(second_pass, (pos_slots, feat_slots, neigh_domains, count_domains)))

def reference(positions, momenta, species, neighbours, counts, exports, embed, radial_one_in, radial_one_out, mix_one, radial_two_in, radial_two_out, readout, energy_w):

    def bead_grad(inputs):
        return jax.grad(bead_energy)(inputs[0], species, inputs[1], inputs[2], inputs[3], embed, radial_one_in, radial_one_out, mix_one, radial_two_in, radial_two_out, readout, energy_w)
    grads = lax.map(bead_grad, (positions, neighbours, counts, exports))
    kicked = momenta - 0.5 * time_step(BEADS) * grads
    table = mode_table(jnp.arange(BEADS, dtype=jnp.int32), BEADS)
    cosine, reach, stiffness = mode_rotation(BEADS)
    mass = atom_mass(species)
    mode_q = jnp.einsum('bk,bcn->kcn', table, positions, precision=highest)
    mode_p = jnp.einsum('bk,bcn->kcn', table, kicked, precision=highest)
    next_q = cosine[:, None, None] * mode_q + reach[:, None, None] * mode_p / mass
    next_p = -stiffness[:, None, None] * mass * mode_q + cosine[:, None, None] * mode_p
    new_positions = jnp.einsum('bk,kcn->bcn', table, next_q, precision=highest)
    new_momenta = jnp.einsum('bk,kcn->bcn', table, next_p, precision=highest)
    return (new_positions, new_momenta)
```

```python
import functools
import math

import jax
import jax.numpy as jnp
import numpy as np
from jax import lax
from jax.experimental import pallas as pl
from jax.experimental.pallas import tpu as pltpu
from jax.sharding import PartitionSpec as P

RCUT = 6.0
CYCLE_FREQ = 1.5
MASS_OXYGEN = 15.999
MASS_HYDROGEN = 1.008
LANES = 128
F32 = jnp.float32
BF16 = jnp.bfloat16
MESH = pl.DeviceIdType.MESH
ROOT3 = math.sqrt(3.0)
ROOT5 = math.sqrt(5.0)
ROOT15 = math.sqrt(15.0)
DEGREE = (0, 1, 1, 1, 2, 2, 2, 2, 2)


def circulant_weights(beads):
    dt = beads / 3.0
    k = np.arange(beads)
    w = 2.0 * CYCLE_FREQ * np.sin(np.pi * k / beads)
    cosine = np.cos(w * dt)
    sine = np.sin(w * dt)
    reach = np.where(k == 0, dt, sine / np.where(k == 0, 1.0, w))
    stiff = w * sine
    d = np.arange(beads)
    waves = np.cos(2.0 * np.pi * d[:, None] * k[None, :] / beads) / beads
    return [(waves @ f).astype(np.float32) for f in (cosine, reach, stiff)]


def split(x):
    hi = x.astype(BF16)
    lo = (x - hi.astype(F32)).astype(BF16)
    return hi, lo


def rhs3(x):
    hi, lo = split(x)
    return jnp.concatenate([hi, lo, hi], axis=0)


def lhs3(w):
    hi = w.astype(BF16).astype(F32)
    lo = w - hi
    return jnp.concatenate([hi, hi, lo], axis=1).astype(BF16)


def mm(a, b):
    return jnp.dot(a, b, preferred_element_type=F32)


def mm_nt(a, b):
    return lax.dot_general(a, b, (((1,), (1,)), ((), ())), preferred_element_type=F32)


def lane_take(table, index):
    return jnp.take_along_axis(table, index, axis=1)


def silu_parts(x):
    sig = 0.5 * jnp.tanh(0.5 * x) + 0.5
    val = x * sig
    return val, sig + val * (1.0 - sig)


def rows_to_tile(parts, sub):
    low = sub < 4
    quads = []
    for j in range(4):
        a, b = parts[j], parts[j + 4]
        quads.append(jnp.where(low, a, b) + pltpu.roll(jnp.where(low, b, a), 4, 0))
    even2 = (sub & 2) == 0
    pairs = []
    for j in range(2):
        a, b = quads[j], quads[j + 2]
        pairs.append(jnp.where(even2, a + pltpu.roll(a, 6, 0), b + pltpu.roll(b, 2, 0)))
    even1 = (sub & 1) == 0
    a, b = pairs
    return jnp.where(even1, a + pltpu.roll(a, 7, 0), b + pltpu.roll(b, 1, 0))


def kernel(
    beads,
    domains,
    pos_ref,
    mom_ref,
    kind_ref,
    neigh_ref,
    count_ref,
    exp_ref,
    embed_ref,
    w1i_ref,
    w1o_ref,
    mix_ref,
    w2i_ref,
    w2o_ref,
    read_ref,
    ew_ref,
    newq_ref,
    newp_ref,
    qtile,
    qall,
    ptile,
    pall,
    psend,
    slots,
    fsend,
    ftab,
    gsend,
    gback,
    xsend,
    xback,
    bas,
    dbas,
    ylm,
    geo,
    doff,
    kindd,
    lowd,
    tabd,
    rad1,
    hd1,
    rad2,
    hd2,
    feat2,
    amp1,
    amp2,
    onehot,
    onehot_exp,
    lhs_g,
    acc_g,
    lhs_x,
    acc_x,
    bas_grad,
    ylm_grad,
    send_sem,
    recv_sem,
    bsend_sem,
    brecv_sem,
):
    bead = lax.axis_index("bead")
    dom = lax.axis_index("space")
    depth, atoms = neigh_ref.shape
    chans = embed_ref.shape[1]
    tables = atoms // LANES + domains
    own_tabs = atoms // LANES
    norm = 1.0 / depth

    barrier = pltpu.get_barrier_semaphore()
    for d in range(1, domains):
        pl.semaphore_signal(
            barrier, inc=1, device_id=(bead, lax.rem(dom + d, domains)), device_id_type=MESH
        )

    def greet(d, carry):
        pl.semaphore_signal(
            barrier, inc=1, device_id=(lax.rem(bead + d, beads), dom), device_id_type=MESH
        )
        return carry

    lax.fori_loop(1, beads, greet, 0)

    def space_copy(stage, d, src, dst):
        peer = lax.rem(dom + d, domains)
        return pltpu.make_async_remote_copy(
            src_ref=src.at[peer],
            dst_ref=dst.at[dom],
            send_sem=send_sem.at[stage, d],
            recv_sem=recv_sem.at[stage, d],
            device_id=(bead, peer),
            device_id_type=MESH,
        )

    def space_start(stage, src, dst):
        for d in range(1, domains):
            space_copy(stage, d, src, dst).start()

    def space_wait(stage, src, dst):
        for d in range(1, domains):
            space_copy(stage, d, src, dst).wait()

    def bead_copy(stage, d, src, dst):
        return pltpu.make_async_remote_copy(
            src_ref=src,
            dst_ref=dst.at[d],
            send_sem=bsend_sem.at[stage, d],
            recv_sem=brecv_sem.at[stage, d],
            device_id=(lax.rem(bead + d, beads), dom),
            device_id_type=MESH,
        )

    own = pos_ref[...]
    kind_row = kind_ref[...].astype(F32)
    zero_row = jnp.zeros((1, LANES), F32)
    for h in range(own_tabs):
        lanes = slice(h * LANES, (h + 1) * LANES)
        slots_h = jnp.concatenate(
            [own[:, lanes], kind_row[:, lanes], zero_row, zero_row, zero_row, zero_row], axis=0
        )
        slots[domains + h] = slots_h
        qtile[4 * h : 4 * h + 4] = slots_h[0:4]
    for t in range(domains):
        row = jnp.broadcast_to(exp_ref[t : t + 1, :], (8, LANES))
        low = row & (LANES - 1)
        picked = lane_take(slots[domains], low)
        for h in range(1, own_tabs):
            picked = jnp.where(
                (row >> 7) == h, lane_take(slots[domains + h], low), picked
            )
        psend[t] = picked

    pl.semaphore_wait(barrier, domains - 1 + beads - 1)
    space_start(0, psend, slots)

    def start_q(d, carry):
        bead_copy(0, d, qtile, qall).start()
        return carry

    lax.fori_loop(1, beads, start_q, 0)
    qall[0] = qtile[...]

    w1i = w1i_ref[...]
    w1o = w1o_ref[...]
    w2i = w2i_ref[...]
    w2o = w2o_ref[...]
    nbasis, hidden = w1i.shape

    def in_lhs(w):
        wt = w.T
        hi = wt.astype(BF16).astype(F32)
        lo = wt - hi
        return jnp.concatenate([hi, hi, lo, jnp.zeros_like(hi)], axis=1).astype(BF16)

    f1i, f1o = in_lhs(w1i), lhs3(w1o.T)
    b1i, b1o = lhs3(w1i), lhs3(w1o)
    f2i, f2o = in_lhs(w2i), lhs3(w2o.T)
    b2i, b2o = lhs3(w2i), lhs3(w2o)
    mix_f, mix_b = lhs3(mix_ref[...].T), lhs3(mix_ref[...])
    read_f, read_b = lhs3(read_ref[...].T), lhs3(read_ref[...])
    embed_t = embed_ref[...].T
    energy_t = ew_ref[...].T

    slots[dom] = psend[dom]
    for t in range(domains):
        onehot_exp[:, t * LANES : (t + 1) * LANES] = (
            (lax.broadcasted_iota(jnp.int32, (atoms, LANES), 0) == exp_ref[t : t + 1, :])
            .astype(F32)
            .astype(BF16)
        )
    space_wait(0, psend, slots)

    def table_of(index):
        t = index >> 7
        return jnp.where(t < own_tabs, t + domains, t - own_tabs)

    idx = neigh_ref[...]
    low_all = idx & (LANES - 1)
    tab_all = table_of(idx)
    planes = []
    for comp in range(4):
        halves = []
        for h in range(own_tabs):
            lanes = slice(h * LANES, (h + 1) * LANES)
            low, tab = low_all[:, lanes], tab_all[:, lanes]
            out = None
            for t in range(tables):
                source = jnp.broadcast_to(slots[t, comp : comp + 1, :], (depth, LANES))
                got = lane_take(source, low)
                out = got if out is None else jnp.where(tab == t, got, out)
            halves.append(out)
        planes.append(jnp.concatenate(halves, axis=1))
    for h in range(own_tabs):
        lanes = slice(h * LANES, (h + 1) * LANES)
        kindd[h] = planes[3][:, lanes]
        lowd[h] = low_all[:, lanes]
        tabd[h] = tab_all[:, lanes]

    def plane_row(ref, k, h):
        return ref[h, pl.ds(k, 1), :]

    def whole_row(ref, k):
        return jnp.concatenate([plane_row(ref, k, h) for h in range(own_tabs)], axis=1)


    def geometry():
        off = [planes[c] - own[c : c + 1, :] for c in range(3)]
        dist = jnp.sqrt(off[0] * off[0] + off[1] * off[1] + off[2] * off[2] + 1.0)
        inv = 1.0 / dist
        return [o * inv for o in off], dist, inv

    u, dist, inv = geometry()
    present = (
        lax.broadcasted_iota(jnp.int32, (depth, atoms), 0) < count_ref[...]
    ).astype(F32)
    scaled = jnp.minimum(dist * (1.0 / RCUT), 1.0)
    arg = math.pi * (scaled - 0.5)
    sq = arg * arg
    cos_y = 1.0
    for n in range(7, 0, -1):
        cos_y = 1.0 - cos_y * sq * (1.0 / ((2 * n - 1) * (2 * n)))
    sin_y = 1.0
    for n in range(6, 0, -1):
        sin_y = 1.0 - sin_y * sq * (1.0 / ((2 * n) * (2 * n + 1)))
    sin_y = sin_y * arg
    sines, cosines = {1: cos_y}, {1: -sin_y}
    for n in range(2, nbasis + 1):
        a, b = n // 2, n - n // 2
        sines[n] = sines[a] * cosines[b] + cosines[a] * sines[b]
        cosines[n] = cosines[a] * cosines[b] - sines[a] * sines[b]
    gap = 1.0 - scaled * scaled
    env = gap * gap * present * inv
    slope = -(4.0 / RCUT) * scaled * gap * present * inv - env * inv

    def strided_put(ref, j, plane):
        for h in range(own_tabs):
            ref[h, pl.ds(j, depth, stride=8), :] = plane[:, h * LANES : (h + 1) * LANES]

    def strided_get(ref, j):
        return jnp.concatenate(
            [ref[h, pl.ds(j, depth, stride=8), :] for h in range(own_tabs)], axis=1
        )

    def rows_get(ref, k):
        rows = pl.ds(pl.multiple_of(k * 8, 8), 8)
        return jnp.concatenate([ref[h, rows, :] for h in range(own_tabs)], axis=1)

    def rows_put(ref, k, value, add):
        rows = pl.ds(pl.multiple_of(k * 8, 8), 8)
        for h in range(own_tabs):
            part = value[:, h * LANES : (h + 1) * LANES]
            ref[h, rows, :] = ref[h, rows, :] + part if add else part

    for n in range(1, nbasis + 1):
        strided_put(bas, n - 1, sines[n] * env)
    ux, uy, uz = u
    harmonic = [
        ROOT3 * ux,
        ROOT3 * uy,
        ROOT3 * uz,
        ROOT15 * ux * uy,
        ROOT15 * uy * uz,
        ROOT15 * ux * uz,
        0.5 * ROOT15 * (ux * ux - uy * uy),
        0.5 * ROOT5 * (2.0 * uz * uz - ux * ux - uy * uy),
    ]
    for m in range(8):
        strided_put(ylm, m, harmonic[m])
    for n in range(1, nbasis + 1):
        dbas[n - 1] = (n * math.pi / RCUT) * cosines[n] * env + sines[n] * slope
    for c in range(3):
        geo[c] = u[c]
    geo[3] = inv

    def radial_net(w_in, w_out, rad, hd):
        def step(k, carry):
            x = rows_get(bas, k)
            hi = x.astype(BF16).astype(F32)
            x3 = jnp.concatenate([hi, x - hi, hi, jnp.zeros_like(hi)], axis=0).astype(BF16)
            val, slope_h = silu_parts(mm(w_in, x3))
            hd[k] = slope_h
            rad[k] = mm(w_out, rhs3(val))
            return carry

        lax.fori_loop(0, depth, step, 0, unroll=2)

    group = 16

    def y_row(k, m, h):
        return ylm[h, pl.ds(k * 8 + m - 1, 1), :]

    def amplitudes(amp, rad, feature):
        invs = [[[None] * own_tabs for _ in range(chans // group)] for _ in range(3)]
        for h in range(own_tabs):
            lanes = slice(h * LANES, (h + 1) * LANES)
            for g in range(chans // group):

                def step(k, acc):
                    f = feature(k, g, h)
                    ws = [
                        rad[k, deg * chans + g * group : deg * chans + (g + 1) * group, lanes] * f
                        for deg in range(3)
                    ]
                    out = [acc[0] + ws[0]]
                    for m in range(1, 9):
                        out.append(acc[m] + ws[DEGREE[m]] * y_row(k, m, h))
                    return tuple(out)

                start = tuple(jnp.zeros((group, LANES), F32) for _ in range(9))
                acc = lax.fori_loop(0, depth, step, start, unroll=2)
                sums = [0.0, 0.0, 0.0]
                for m in range(9):
                    amp[m, g * group : (g + 1) * group, lanes] = acc[m]
                    sums[DEGREE[m]] = sums[DEGREE[m]] + acc[m] * acc[m]
                for deg in range(3):
                    invs[deg][g][h] = sums[deg] * norm
        rows = []
        for deg in range(3):
            for g in range(chans // group):
                rows.append(jnp.concatenate(invs[deg][g], axis=1))
        return jnp.concatenate(rows, axis=0)

    def scale_amp(amp, d_inv):
        for m in range(9):
            deg = DEGREE[m]
            amp[m] = amp[m] * d_inv[deg * chans : (deg + 1) * chans] * (2.0 * norm)

    def kind_feature(k, g, h):
        row = plane_row(kindd, k, h)
        rows = slice(g * group, (g + 1) * group)
        return jnp.where(row > 0.5, embed_t[rows, 1:2], embed_t[rows, 0:1])

    def slot_feature(k, g, h):
        return feat2[k, g * group : (g + 1) * group, h * LANES : (h + 1) * LANES]

    radial_net(f1i, f1o, rad1, hd1)
    inv1 = amplitudes(amp1, rad1, kind_feature)
    act1, slope1 = silu_parts(mm(mix_f, rhs3(inv1)))
    own_embed = jnp.where(kind_row > 0.5, embed_t[:, 1:2], embed_t[:, 0:1])
    layer_one = own_embed + act1
    for h in range(own_tabs):
        ftab[domains + h] = layer_one[:, h * LANES : (h + 1) * LANES]
    for t in range(domains):
        row = jnp.broadcast_to(exp_ref[t : t + 1, :], (chans, LANES))
        low = row & (LANES - 1)
        picked = lane_take(ftab[domains], low)
        for h in range(1, own_tabs):
            picked = jnp.where((row >> 7) == h, lane_take(ftab[domains + h], low), picked)
        fsend[t] = picked
    space_start(1, fsend, ftab)
    ftab[dom] = fsend[dom]

    radial_net(f2i, f2o, rad2, hd2)
    space_wait(1, fsend, ftab)

    def gather_step(k, carry):
        low_row = whole_row(lowd, k)
        tab_row = whole_row(tabd, k)
        for h in range(own_tabs):
            lanes = slice(h * LANES, (h + 1) * LANES)
            low = jnp.broadcast_to(low_row[:, lanes], (chans, LANES))
            out = lane_take(ftab[0], low)
            for t in range(1, tables):
                out = jnp.where(tab_row[:, lanes] == t, lane_take(ftab[t], low), out)
            feat2[k, :, lanes] = out
        onehot[k] = (
            lax.broadcasted_iota(jnp.int32, (LANES, atoms), 0) == low_row
        ).astype(F32).astype(BF16)
        return carry

    lax.fori_loop(0, depth, gather_step, 0)

    inv2 = amplitudes(amp2, rad2, slot_feature)
    unused, slope_r = silu_parts(mm(read_f, rhs3(inv2)))
    scale_amp(amp2, mm(read_b, rhs3(slope_r * energy_t)))

    sub = lax.broadcasted_iota(jnp.int32, (8, LANES), 0)

    def backward(k, amp, rad, hd, w_out, w_in, feature, want_feat):
        d_rads, d_feats, d_ylms = [], [], []
        for h in range(own_tabs):
            lanes = slice(h * LANES, (h + 1) * LANES)
            f = jnp.concatenate([feature(k, g, h) for g in range(chans // group)], axis=0)
            rads = [rad[k, deg * chans : (deg + 1) * chans, lanes] for deg in range(3)]
            ws = [r * f for r in rads]
            d_ws = [amp[0, :, lanes], None, None]
            parts = []
            for m in range(1, 9):
                deg = DEGREE[m]
                da = amp[m, :, lanes]
                term = da * y_row(k, m, h)
                d_ws[deg] = term if d_ws[deg] is None else d_ws[deg] + term
                prod = da * ws[deg]
                parts.append(prod[0:8] + prod[8:16] + prod[16:24] + prod[24:32])
            d_ylms.append(rows_to_tile(parts, sub))
            d_rads.append(jnp.concatenate([d * f for d in d_ws], axis=0))
            if want_feat:
                d_feats.append(d_ws[0] * rads[0] + d_ws[1] * rads[1] + d_ws[2] * rads[2])
        d_rad = jnp.concatenate(d_rads, axis=1)
        d_pre = mm(w_out, rhs3(d_rad)) * hd[k]
        d_bas = mm(w_in, rhs3(d_pre))
        d_ylm = jnp.concatenate(d_ylms, axis=1)
        d_feat = jnp.concatenate(d_feats, axis=1) if want_feat else None
        return d_bas, d_ylm, d_feat

    acc_g[...] = jnp.zeros_like(acc_g)
    per = 4

    def second_back(kb, carry):
        for j in range(per):
            k = kb * per + j
            d_bas, d_ylm, d_feat = backward(k, amp2, rad2, hd2, b2o, b2i, slot_feature, True)
            rows_put(bas_grad, k, d_bas, False)
            rows_put(ylm_grad, k, d_ylm, False)
            hi, lo = split(d_feat)
            both = jnp.concatenate([hi, lo], axis=0)
            tab_row = whole_row(tabd, k)
            for t in range(tables):
                hit = (tab_row == t).astype(F32).astype(BF16)
                lhs_g[t * 2 * chans : (t + 1) * 2 * chans, j * atoms : (j + 1) * atoms] = both * hit
        hot = jnp.concatenate([onehot[kb * per + j] for j in range(per)], axis=1)
        acc_g[...] += mm_nt(lhs_g[...], hot)
        return carry

    lax.fori_loop(0, depth // per, second_back, 0)

    def table_grad(t):
        base = t * 2 * chans
        return acc_g[base : base + chans, :] + acc_g[base + chans : base + 2 * chans, :]

    for t in range(domains):
        gsend[t] = table_grad(t)
    space_start(2, gsend, gback)
    gback[dom] = gsend[dom]
    own_grad = jnp.concatenate([table_grad(domains + h) for h in range(own_tabs)], axis=1)
    space_wait(2, gsend, gback)

    def to_owner(back):
        rows = back.shape[1]
        flat = jnp.concatenate([back[t] for t in range(domains)], axis=1)
        hi = flat.astype(BF16).astype(F32)
        both = jnp.concatenate([hi, flat - hi], axis=0).astype(BF16)
        out = mm_nt(both, onehot_exp[...])
        return out[:rows] + out[rows:]

    d_layer = own_grad + to_owner(gback)
    scale_amp(amp1, mm(mix_b, rhs3(d_layer * slope1)))

    def first_back(k, carry):
        d_bas, d_ylm, unused_feat = backward(k, amp1, rad1, hd1, b1o, b1i, kind_feature, False)
        rows_put(bas_grad, k, d_bas, True)
        rows_put(ylm_grad, k, d_ylm, True)
        return carry

    lax.fori_loop(0, depth, first_back, 0)

    ux, uy, uz = geo[0], geo[1], geo[2]
    d_r = None
    for n in range(nbasis):
        term = strided_get(bas_grad, n) * dbas[n]
        d_r = term if d_r is None else d_r + term
    dy = [strided_get(ylm_grad, m) for m in range(8)]
    dux = ROOT3 * dy[0] + ROOT15 * (uy * dy[3] + uz * dy[5] + ux * dy[6]) - ROOT5 * (ux * dy[7])
    duy = ROOT3 * dy[1] + ROOT15 * (ux * dy[3] + uz * dy[4] - uy * dy[6]) - ROOT5 * (uy * dy[7])
    duz = ROOT3 * dy[2] + ROOT15 * (uy * dy[4] + ux * dy[5]) + (2.0 * ROOT5) * (uz * dy[7])
    along = d_r - geo[3] * (ux * dux + uy * duy + uz * duz)
    d_off = [geo[3] * d + v * along for d, v in ((dux, ux), (duy, uy), (duz, uz))]
    centre = jnp.concatenate([jnp.sum(d, axis=0, keepdims=True) for d in d_off], axis=0)
    for c in range(3):
        for h in range(own_tabs):
            doff[c, h] = d_off[c][:, h * LANES : (h + 1) * LANES]

    acc_x[...] = jnp.zeros_like(acc_x)

    def force_step(kb, carry):
        for j in range(per):
            k = kb * per + j
            tab_row = whole_row(tabd, k)
            hit = tab_row == lax.broadcasted_iota(jnp.int32, (8, atoms), 0)
            rows = [jnp.where(hit, whole_row(doff.at[c], k), 0.0) for c in range(3)]
            full = jnp.concatenate(rows, axis=0)
            hi = full.astype(BF16).astype(F32)
            lhs_x[:, j * atoms : (j + 1) * atoms] = jnp.concatenate(
                [hi, full - hi], axis=0
            ).astype(BF16)
        hot = jnp.concatenate([onehot[kb * per + j] for j in range(per)], axis=1)
        acc_x[...] += mm_nt(lhs_x[...], hot)
        return carry

    lax.fori_loop(0, depth // per, force_step, 0)
    table_force = [acc_x[c * 8 : (c + 1) * 8, :] + acc_x[24 + c * 8 : 32 + c * 8, :] for c in range(3)]
    pad = jnp.zeros((5, LANES), F32)
    for t in range(domains):
        xsend[t] = jnp.concatenate([f[t : t + 1] for f in table_force] + [pad], axis=0)
    space_start(3, xsend, xback)
    xback[dom] = xsend[dom]
    own_force = jnp.concatenate(
        [
            jnp.concatenate([f[domains + h : domains + h + 1] for f in table_force], axis=0)
            for h in range(own_tabs)
        ],
        axis=1,
    )

    def wait_q(d, carry):
        bead_copy(0, d, qtile, qall).wait()
        return carry

    lax.fori_loop(1, beads, wait_q, 0)
    half_step = 0.5 * beads / 3.0
    partial = mom_ref[...] - half_step * (own_force - centre)
    wqq, wqp, wpq = circulant_weights(beads)
    q_q = sum(float(wqq[d]) * qall[d] for d in range(beads))
    p_q = sum(float(wpq[d]) * qall[d] for d in range(beads))
    space_wait(3, xsend, xback)
    kicked = partial - half_step * to_owner(xback)[0:3]
    for h in range(own_tabs):
        ptile[4 * h : 4 * h + 3] = kicked[:, h * LANES : (h + 1) * LANES]
        ptile[4 * h + 3 : 4 * h + 4] = zero_row

    def start_p(d, carry):
        bead_copy(1, d, ptile, pall).start()
        return carry

    lax.fori_loop(1, beads, start_p, 0)
    pall[0] = ptile[...]
    mass = jnp.concatenate(
        [
            jnp.broadcast_to(
                jnp.where(kind_row[:, h * LANES : (h + 1) * LANES] > 0.5, MASS_HYDROGEN, MASS_OXYGEN),
                (4, LANES),
            )
            for h in range(own_tabs)
        ],
        axis=0,
    )

    def wait_p(d, carry):
        bead_copy(1, d, ptile, pall).wait()
        return carry

    lax.fori_loop(1, beads, wait_p, 0)
    q_p = sum(float(wqp[d]) * pall[d] for d in range(beads))
    p_p = sum(float(wqq[d]) * pall[d] for d in range(beads))
    new_q = q_q + q_p / mass
    new_p = p_p - mass * p_q
    for h in range(own_tabs):
        lanes = slice(h * LANES, (h + 1) * LANES)
        newq_ref[:, lanes] = new_q[4 * h : 4 * h + 3]
        newp_ref[:, lanes] = new_p[4 * h : 4 * h + 3]


def shards(
    positions,
    momenta,
    species,
    neighbours,
    counts,
    exports,
    embed,
    radial_one_in,
    radial_one_out,
    mix_one,
    radial_two_in,
    radial_two_out,
    readout,
    energy_w,
):
    beads = lax.axis_size("bead")
    domains = lax.axis_size("space")
    depth, atoms = neighbours.shape[1:]
    chans = embed.shape[1]
    nbasis, hidden = radial_one_in.shape
    tables = atoms // LANES + domains
    per = 4
    vmem = pltpu.VMEM
    scratch = [
        vmem((8, LANES), F32),
        vmem((beads, 8, LANES), F32),
        vmem((8, LANES), F32),
        vmem((beads, 8, LANES), F32),
        vmem((domains, 8, LANES), F32),
        vmem((tables, 8, LANES), F32),
        vmem((domains, chans, LANES), F32),
        vmem((tables, chans, LANES), F32),
        vmem((domains, chans, LANES), F32),
        vmem((domains, chans, LANES), F32),
        vmem((domains, 8, LANES), F32),
        vmem((domains, 8, LANES), F32),
        vmem((2, depth * 8, LANES), F32),
        vmem((nbasis, depth, atoms), F32),
        vmem((2, depth * 8, LANES), F32),
        vmem((4, depth, atoms), F32),
        vmem((3, 2, depth, LANES), F32),
        vmem((2, depth, LANES), F32),
        vmem((2, depth, LANES), jnp.int32),
        vmem((2, depth, LANES), jnp.int32),
        vmem((depth, 3 * chans, atoms), F32),
        vmem((depth, hidden, atoms), F32),
        vmem((depth, 3 * chans, atoms), F32),
        vmem((depth, hidden, atoms), F32),
        vmem((depth, chans, atoms), F32),
        vmem((9, chans, atoms), F32),
        vmem((9, chans, atoms), F32),
        vmem((depth, LANES, atoms), BF16),
        vmem((atoms, domains * LANES), BF16),
        vmem((tables * 2 * chans, per * atoms), BF16),
        vmem((tables * 2 * chans, LANES), F32),
        vmem((48, per * atoms), BF16),
        vmem((48, LANES), F32),
        vmem((2, depth * 8, LANES), F32),
        vmem((2, depth * 8, LANES), F32),
        pltpu.SemaphoreType.DMA((4, domains)),
        pltpu.SemaphoreType.DMA((4, domains)),
        pltpu.SemaphoreType.DMA((2, beads)),
        pltpu.SemaphoreType.DMA((2, beads)),
    ]
    whole = pl.BlockSpec(memory_space=pltpu.VMEM)
    new_q, new_p = pl.pallas_call(
        functools.partial(kernel, beads, domains),
        out_shape=(
            jax.ShapeDtypeStruct((3, atoms), F32),
            jax.ShapeDtypeStruct((3, atoms), F32),
        ),
        in_specs=[whole] * 14,
        out_specs=(whole, whole),
        scratch_shapes=scratch,
        compiler_params=pltpu.CompilerParams(
            collective_id=0, has_side_effects=True, vmem_limit_bytes=56 * 1024 * 1024
        ),
    )(
        positions[0],
        momenta[0],
        species.reshape(1, atoms),
        neighbours[0],
        counts,
        exports[0, 0],
        embed,
        radial_one_in,
        radial_one_out,
        mix_one,
        radial_two_in,
        radial_two_out,
        readout,
        energy_w.reshape(1, hidden),
    )
    return new_q[None], new_p[None]


def solution(mesh):
    placed = (
        P("bead", None, "space"),
        P("bead", None, "space"),
        P("space"),
        P("bead", None, "space"),
        P("bead", "space"),
        P("bead", "space", None, None),
        P(),
        P(),
        P(),
        P(),
        P(),
        P(),
        P(),
        P(),
    )
    return jax.shard_map(
        shards,
        mesh=mesh,
        in_specs=placed,
        out_specs=(P("bead", None, "space"), P("bead", None, "space")),
        check_vma=False,
    )
```

```python
import functools
import math

import jax
import jax.numpy as jnp
import numpy as np
from jax import lax
from jax.experimental import pallas as pl
from jax.experimental.pallas import tpu as pltpu
from jax.sharding import PartitionSpec as P

RCUT = 6.0
CYCLE_FREQ = 1.5
MASS_OXYGEN = 15.999
MASS_HYDROGEN = 1.008
LANES = 128
F32 = jnp.float32
BF16 = jnp.bfloat16
MESH = pl.DeviceIdType.MESH
ROOT3 = math.sqrt(3.0)
ROOT5 = math.sqrt(5.0)
ROOT15 = math.sqrt(15.0)
DEGREE = (0, 1, 1, 1, 2, 2, 2, 2, 2)


def circulant_weights(beads):
    dt = beads / 3.0
    k = np.arange(beads)
    w = 2.0 * CYCLE_FREQ * np.sin(np.pi * k / beads)
    cosine = np.cos(w * dt)
    sine = np.sin(w * dt)
    reach = np.where(k == 0, dt, sine / np.where(k == 0, 1.0, w))
    stiff = w * sine
    d = np.arange(beads)
    waves = np.cos(2.0 * np.pi * d[:, None] * k[None, :] / beads) / beads
    return [(waves @ f).astype(np.float32) for f in (cosine, reach, stiff)]


def split(x):
    hi = x.astype(BF16)
    lo = (x - hi.astype(F32)).astype(BF16)
    return hi, lo


def rhs3(x):
    hi, lo = split(x)
    return jnp.concatenate([hi, lo, hi], axis=0)


def lhs3(w):
    hi = w.astype(BF16).astype(F32)
    lo = w - hi
    return jnp.concatenate([hi, hi, lo], axis=1).astype(BF16)


def mm(a, b):
    return jnp.dot(a, b, preferred_element_type=F32)


def mm_nt(a, b):
    return lax.dot_general(a, b, (((1,), (1,)), ((), ())), preferred_element_type=F32)


def lane_take(table, index):
    return jnp.take_along_axis(table, index, axis=1)


def silu_parts(x):
    sig = 0.5 * jnp.tanh(0.5 * x) + 0.5
    val = x * sig
    return val, sig + val * (1.0 - sig)


def rows_to_tile(parts, sub):
    low = sub < 4
    quads = []
    for j in range(4):
        a, b = parts[j], parts[j + 4]
        quads.append(jnp.where(low, a, b) + pltpu.roll(jnp.where(low, b, a), 4, 0))
    even2 = (sub & 2) == 0
    pairs = []
    for j in range(2):
        a, b = quads[j], quads[j + 2]
        pairs.append(jnp.where(even2, a + pltpu.roll(a, 6, 0), b + pltpu.roll(b, 2, 0)))
    even1 = (sub & 1) == 0
    a, b = pairs
    return jnp.where(even1, a + pltpu.roll(a, 7, 0), b + pltpu.roll(b, 1, 0))


def kernel(
    beads,
    domains,
    pos_ref,
    mom_ref,
    kind_ref,
    neigh_ref,
    count_ref,
    exp_ref,
    embed_ref,
    w1i_ref,
    w1o_ref,
    mix_ref,
    w2i_ref,
    w2o_ref,
    read_ref,
    ew_ref,
    newq_ref,
    newp_ref,
    qtile,
    qall,
    ptile,
    pall,
    psend,
    slots,
    fsend,
    ftab,
    gsend,
    gback,
    xsend,
    xback,
    bas,
    dbas,
    ylm,
    geo,
    doff,
    kindd,
    lowd,
    tabd,
    embeds,
    rad1,
    hd1,
    rad2,
    hd2,
    feat2,
    amp1,
    amp2,
    onehot,
    onehot_exp,
    lhs_g,
    acc_g,
    lhs_x,
    acc_x,
    bas_grad,
    ylm_grad,
    send_sem,
    recv_sem,
    bsend_sem,
    brecv_sem,
):
    bead = lax.axis_index("bead")
    dom = lax.axis_index("space")
    depth, atoms = neigh_ref.shape
    chans = embed_ref.shape[1]
    tables = atoms // LANES + domains
    own_tabs = atoms // LANES
    norm = 1.0 / depth

    barrier = pltpu.get_barrier_semaphore()
    for d in range(1, domains):
        pl.semaphore_signal(
            barrier, inc=1, device_id=(bead, lax.rem(dom + d, domains)), device_id_type=MESH
        )

    def greet(d, carry):
        pl.semaphore_signal(
            barrier, inc=1, device_id=(lax.rem(bead + d, beads), dom), device_id_type=MESH
        )
        return carry

    lax.fori_loop(1, beads, greet, 0)

    def space_copy(stage, d, src, dst):
        peer = lax.rem(dom + d, domains)
        return pltpu.make_async_remote_copy(
            src_ref=src.at[peer],
            dst_ref=dst.at[dom],
            send_sem=send_sem.at[stage, d],
            recv_sem=recv_sem.at[stage, d],
            device_id=(bead, peer),
            device_id_type=MESH,
        )

    def space_start(stage, src, dst):
        for d in range(1, domains):
            space_copy(stage, d, src, dst).start()

    def space_wait(stage, src, dst):
        for d in range(1, domains):
            space_copy(stage, d, src, dst).wait()

    def bead_copy(stage, d, src, dst):
        return pltpu.make_async_remote_copy(
            src_ref=src,
            dst_ref=dst.at[d],
            send_sem=bsend_sem.at[stage, d],
            recv_sem=brecv_sem.at[stage, d],
            device_id=(lax.rem(bead + d, beads), dom),
            device_id_type=MESH,
        )

    own = pos_ref[...].reshape(3, atoms)
    kind_row = kind_ref[...].astype(F32)
    zero_row = jnp.zeros((1, LANES), F32)
    for h in range(own_tabs):
        lanes = slice(h * LANES, (h + 1) * LANES)
        slots_h = jnp.concatenate(
            [own[:, lanes], kind_row[:, lanes], zero_row, zero_row, zero_row, zero_row], axis=0
        )
        slots[domains + h] = slots_h
        qtile[4 * h : 4 * h + 4] = slots_h[0:4]
    for t in range(domains):
        row = jnp.broadcast_to(exp_ref[t : t + 1, :], (8, LANES))
        low = row & (LANES - 1)
        picked = lane_take(slots[domains], low)
        for h in range(1, own_tabs):
            picked = jnp.where(
                (row >> 7) == h, lane_take(slots[domains + h], low), picked
            )
        psend[t] = picked

    pl.semaphore_wait(barrier, domains - 1 + beads - 1)
    space_start(0, psend, slots)

    def start_q(d, carry):
        bead_copy(0, d, qtile, qall).start()
        return carry

    lax.fori_loop(1, beads, start_q, 0)
    qall[0] = qtile[...]

    w1i = w1i_ref[...]
    w1o = w1o_ref[...]
    w2i = w2i_ref[...]
    w2o = w2o_ref[...]
    nbasis, hidden = w1i.shape

    def in_lhs(w):
        wt = w.T
        hi = wt.astype(BF16).astype(F32)
        lo = wt - hi
        return jnp.concatenate([hi, hi, lo, jnp.zeros_like(hi)], axis=1).astype(BF16)

    f1i, f1o = in_lhs(w1i), lhs3(w1o.T)
    b1i, b1o = lhs3(w1i), lhs3(w1o)
    f2i, f2o = in_lhs(w2i), lhs3(w2o.T)
    b2i, b2o = lhs3(w2i), lhs3(w2o)
    mix_f, mix_b = lhs3(mix_ref[...]), lhs3(mix_ref[...].T)
    read_f, read_b = lhs3(read_ref[...]), lhs3(read_ref[...].T)
    embed_t = embed_ref[...].T
    for kind in range(2):
        embeds[kind] = jnp.broadcast_to(embed_t[:, kind : kind + 1], (chans, LANES))
    energy_t = ew_ref[...].T

    slots[dom] = psend[dom]
    for t in range(domains):
        onehot_exp[:, t * LANES : (t + 1) * LANES] = (
            (lax.broadcasted_iota(jnp.int32, (atoms, LANES), 0) == exp_ref[t : t + 1, :])
            .astype(F32)
            .astype(BF16)
        )
    space_wait(0, psend, slots)

    def table_of(index):
        t = index >> 7
        return jnp.where(t < own_tabs, t + domains, t - own_tabs)

    idx = neigh_ref[...]
    low_all = idx & (LANES - 1)
    tab_all = table_of(idx)
    planes = []
    for comp in range(4):
        halves = []
        for h in range(own_tabs):
            lanes = slice(h * LANES, (h + 1) * LANES)
            low, tab = low_all[:, lanes], tab_all[:, lanes]
            out = None
            for t in range(tables):
                source = jnp.broadcast_to(slots[t, comp : comp + 1, :], (depth, LANES))
                got = lane_take(source, low)
                out = got if out is None else jnp.where(tab == t, got, out)
            halves.append(out)
        planes.append(jnp.concatenate(halves, axis=1))
    for h in range(own_tabs):
        lanes = slice(h * LANES, (h + 1) * LANES)
        kindd[h] = planes[3][:, lanes]
        lowd[h] = low_all[:, lanes]
        tabd[h] = tab_all[:, lanes]

    def plane_row(ref, k, h):
        return ref[h, pl.ds(k, 1), :]

    def whole_row(ref, k):
        return jnp.concatenate([plane_row(ref, k, h) for h in range(own_tabs)], axis=1)


    def geometry():
        off = [planes[c] - own[c : c + 1, :] for c in range(3)]
        dist = jnp.sqrt(off[0] * off[0] + off[1] * off[1] + off[2] * off[2] + 1.0)
        inv = 1.0 / dist
        return [o * inv for o in off], dist, inv

    u, dist, inv = geometry()
    present = (
        lax.broadcasted_iota(jnp.int32, (depth, atoms), 0) < count_ref[...]
    ).astype(F32)
    scaled = jnp.minimum(dist * (1.0 / RCUT), 1.0)
    arg = math.pi * (scaled - 0.5)
    sq = arg * arg
    cos_y = 1.0
    for n in range(7, 0, -1):
        cos_y = 1.0 - cos_y * sq * (1.0 / ((2 * n - 1) * (2 * n)))
    sin_y = 1.0
    for n in range(6, 0, -1):
        sin_y = 1.0 - sin_y * sq * (1.0 / ((2 * n) * (2 * n + 1)))
    sin_y = sin_y * arg
    sines, cosines = {1: cos_y}, {1: -sin_y}
    for n in range(2, nbasis + 1):
        a, b = n // 2, n - n // 2
        sines[n] = sines[a] * cosines[b] + cosines[a] * sines[b]
        cosines[n] = cosines[a] * cosines[b] - sines[a] * sines[b]
    gap = 1.0 - scaled * scaled
    env = gap * gap * present * inv
    slope = -(4.0 / RCUT) * scaled * gap * present * inv - env * inv

    def strided_put(ref, j, plane):
        for h in range(own_tabs):
            ref[h, pl.ds(j, depth, stride=8), :] = plane[:, h * LANES : (h + 1) * LANES]

    def strided_get(ref, j):
        return jnp.concatenate(
            [ref[h, pl.ds(j, depth, stride=8), :] for h in range(own_tabs)], axis=1
        )

    def rows_get(ref, k):
        rows = pl.ds(pl.multiple_of(k * 8, 8), 8)
        return jnp.concatenate([ref[h, rows, :] for h in range(own_tabs)], axis=1)

    def rows_put(ref, k, value, add):
        rows = pl.ds(pl.multiple_of(k * 8, 8), 8)
        for h in range(own_tabs):
            part = value[:, h * LANES : (h + 1) * LANES]
            ref[h, rows, :] = ref[h, rows, :] + part if add else part

    for n in range(1, nbasis + 1):
        strided_put(bas, n - 1, sines[n] * env)
    ux, uy, uz = u
    harmonic = [
        ROOT3 * ux,
        ROOT3 * uy,
        ROOT3 * uz,
        ROOT15 * ux * uy,
        ROOT15 * uy * uz,
        ROOT15 * ux * uz,
        0.5 * ROOT15 * (ux * ux - uy * uy),
        0.5 * ROOT5 * (2.0 * uz * uz - ux * ux - uy * uy),
    ]
    for m in range(8):
        strided_put(ylm, m, harmonic[m])
    for n in range(1, nbasis + 1):
        dbas[n - 1] = (n * math.pi / RCUT) * cosines[n] * env + sines[n] * slope
    for c in range(3):
        geo[c] = u[c]
    geo[3] = inv

    def radial_net(w_in, w_out, rad, hd):
        def step(k, carry):
            x = rows_get(bas, k)
            hi = x.astype(BF16).astype(F32)
            x3 = jnp.concatenate([hi, x - hi, hi, jnp.zeros_like(hi)], axis=0).astype(BF16)
            val, slope_h = silu_parts(mm(w_in, x3))
            hd[k] = slope_h
            rad[k] = mm(w_out, rhs3(val))
            return carry

        lax.fori_loop(0, depth, step, 0, unroll=8)

    group = 16

    def y_row(k, m, h):
        return ylm[h, pl.ds(k * 8 + m - 1, 1), :]

    def amplitudes(amp, rad, feature):
        invs = [[[None] * own_tabs for _ in range(chans // group)] for _ in range(3)]
        for h in range(own_tabs):
            lanes = slice(h * LANES, (h + 1) * LANES)
            for g in range(chans // group):

                def step(k, acc):
                    f = feature(k, g, h)
                    ws = [
                        rad[k, deg * chans + g * group : deg * chans + (g + 1) * group, lanes] * f
                        for deg in range(3)
                    ]
                    out = [acc[0] + ws[0]]
                    for m in range(1, 9):
                        out.append(acc[m] + ws[DEGREE[m]] * y_row(k, m, h))
                    return tuple(out)

                start = tuple(jnp.zeros((group, LANES), F32) for _ in range(9))
                acc = lax.fori_loop(0, depth, step, start, unroll=4)
                sums = [0.0, 0.0, 0.0]
                for m in range(9):
                    amp[m, g * group : (g + 1) * group, lanes] = acc[m]
                    sums[DEGREE[m]] = sums[DEGREE[m]] + acc[m] * acc[m]
                for deg in range(3):
                    invs[deg][g][h] = sums[deg] * norm
        rows = []
        for deg in range(3):
            for g in range(chans // group):
                rows.append(jnp.concatenate(invs[deg][g], axis=1))
        return jnp.concatenate(rows, axis=0)

    def scale_amp(amp, d_inv):
        for m in range(9):
            deg = DEGREE[m]
            amp[m] = amp[m] * d_inv[deg * chans : (deg + 1) * chans] * (2.0 * norm)

    def kind_feature(k, g, h):
        row = plane_row(kindd, k, h)
        rows = slice(g * group, (g + 1) * group)
        return jnp.where(row > 0.5, embeds[1, rows, :], embeds[0, rows, :])

    def slot_feature(k, g, h):
        return feat2[k, g * group : (g + 1) * group, h * LANES : (h + 1) * LANES]

    radial_net(f1i, f1o, rad1, hd1)
    inv1 = amplitudes(amp1, rad1, kind_feature)
    act1, slope1 = silu_parts(mm(mix_f, rhs3(inv1)))
    own_embed = jnp.where(kind_row > 0.5, embed_t[:, 1:2], embed_t[:, 0:1])
    layer_one = own_embed + act1
    for h in range(own_tabs):
        ftab[domains + h] = layer_one[:, h * LANES : (h + 1) * LANES]
    for t in range(domains):
        row = jnp.broadcast_to(exp_ref[t : t + 1, :], (chans, LANES))
        low = row & (LANES - 1)
        picked = lane_take(ftab[domains], low)
        for h in range(1, own_tabs):
            picked = jnp.where((row >> 7) == h, lane_take(ftab[domains + h], low), picked)
        fsend[t] = picked
    space_start(1, fsend, ftab)
    ftab[dom] = fsend[dom]

    radial_net(f2i, f2o, rad2, hd2)
    space_wait(1, fsend, ftab)

    def gather_step(k, carry):
        low_row = whole_row(lowd, k)
        tab_row = whole_row(tabd, k)
        for h in range(own_tabs):
            lanes = slice(h * LANES, (h + 1) * LANES)
            low = jnp.broadcast_to(low_row[:, lanes], (chans, LANES))
            out = lane_take(ftab[0], low)
            for t in range(1, tables):
                out = jnp.where(tab_row[:, lanes] == t, lane_take(ftab[t], low), out)
            feat2[k, :, lanes] = out
        onehot[k] = (
            lax.broadcasted_iota(jnp.int32, (LANES, atoms), 0) == low_row
        ).astype(F32).astype(BF16)
        return carry

    lax.fori_loop(0, depth, gather_step, 0, unroll=4)

    inv2 = amplitudes(amp2, rad2, slot_feature)
    unused, slope_r = silu_parts(mm(read_f, rhs3(inv2)))
    scale_amp(amp2, mm(read_b, rhs3(slope_r * energy_t)))

    sub = lax.broadcasted_iota(jnp.int32, (8, LANES), 0)

    def backward(k, amp, rad, hd, w_out, w_in, feature, want_feat):
        d_rads, d_feats, d_ylms = [], [], []
        for h in range(own_tabs):
            lanes = slice(h * LANES, (h + 1) * LANES)
            f = jnp.concatenate([feature(k, g, h) for g in range(chans // group)], axis=0)
            rads = [rad[k, deg * chans : (deg + 1) * chans, lanes] for deg in range(3)]
            ws = [r * f for r in rads]
            d_ws = [amp[0, :, lanes], None, None]
            parts = []
            for m in range(1, 9):
                deg = DEGREE[m]
                da = amp[m, :, lanes]
                term = da * y_row(k, m, h)
                d_ws[deg] = term if d_ws[deg] is None else d_ws[deg] + term
                prod = da * ws[deg]
                parts.append(prod[0:8] + prod[8:16] + prod[16:24] + prod[24:32])
            d_ylms.append(rows_to_tile(parts, sub))
            d_rads.append(jnp.concatenate([d * f for d in d_ws], axis=0))
            if want_feat:
                d_feats.append(d_ws[0] * rads[0] + d_ws[1] * rads[1] + d_ws[2] * rads[2])
        d_rad = jnp.concatenate(d_rads, axis=1)
        d_pre = mm(w_out, rhs3(d_rad)) * hd[k]
        d_bas = mm(w_in, rhs3(d_pre))
        d_ylm = jnp.concatenate(d_ylms, axis=1)
        d_feat = jnp.concatenate(d_feats, axis=1) if want_feat else None
        return d_bas, d_ylm, d_feat

    acc_g[...] = jnp.zeros_like(acc_g)
    per = 4

    def second_back(kb, carry):
        for j in range(per):
            k = kb * per + j
            d_bas, d_ylm, d_feat = backward(k, amp2, rad2, hd2, b2o, b2i, slot_feature, True)
            rows_put(bas_grad, k, d_bas, False)
            rows_put(ylm_grad, k, d_ylm, False)
            hi, lo = split(d_feat)
            both = jnp.concatenate([hi, lo], axis=0)
            tab_row = whole_row(tabd, k)
            for t in range(tables):
                hit = (tab_row == t).astype(F32).astype(BF16)
                lhs_g[t * 2 * chans : (t + 1) * 2 * chans, j * atoms : (j + 1) * atoms] = both * hit
        hot = jnp.concatenate([onehot[kb * per + j] for j in range(per)], axis=1)
        acc_g[...] += mm_nt(lhs_g[...], hot)
        return carry

    lax.fori_loop(0, depth // per, second_back, 0)

    def table_grad(t):
        base = t * 2 * chans
        return acc_g[base : base + chans, :] + acc_g[base + chans : base + 2 * chans, :]

    for t in range(domains):
        gsend[t] = table_grad(t)
    space_start(2, gsend, gback)
    gback[dom] = gsend[dom]
    own_grad = jnp.concatenate([table_grad(domains + h) for h in range(own_tabs)], axis=1)
    space_wait(2, gsend, gback)

    def to_owner(back):
        rows = back.shape[1]
        flat = jnp.concatenate([back[t] for t in range(domains)], axis=1)
        hi = flat.astype(BF16).astype(F32)
        both = jnp.concatenate([hi, flat - hi], axis=0).astype(BF16)
        out = mm_nt(both, onehot_exp[...])
        return out[:rows] + out[rows:]

    d_layer = own_grad + to_owner(gback)
    scale_amp(amp1, mm(mix_b, rhs3(d_layer * slope1)))

    def first_back(k, carry):
        d_bas, d_ylm, unused_feat = backward(k, amp1, rad1, hd1, b1o, b1i, kind_feature, False)
        rows_put(bas_grad, k, d_bas, True)
        rows_put(ylm_grad, k, d_ylm, True)
        return carry

    lax.fori_loop(0, depth, first_back, 0, unroll=4)

    ux, uy, uz = geo[0], geo[1], geo[2]
    d_r = None
    for n in range(nbasis):
        term = strided_get(bas_grad, n) * dbas[n]
        d_r = term if d_r is None else d_r + term
    dy = [strided_get(ylm_grad, m) for m in range(8)]
    dux = ROOT3 * dy[0] + ROOT15 * (uy * dy[3] + uz * dy[5] + ux * dy[6]) - ROOT5 * (ux * dy[7])
    duy = ROOT3 * dy[1] + ROOT15 * (ux * dy[3] + uz * dy[4] - uy * dy[6]) - ROOT5 * (uy * dy[7])
    duz = ROOT3 * dy[2] + ROOT15 * (uy * dy[4] + ux * dy[5]) + (2.0 * ROOT5) * (uz * dy[7])
    along = d_r - geo[3] * (ux * dux + uy * duy + uz * duz)
    d_off = [geo[3] * d + v * along for d, v in ((dux, ux), (duy, uy), (duz, uz))]
    centre = jnp.concatenate([jnp.sum(d, axis=0, keepdims=True) for d in d_off], axis=0)
    for c in range(3):
        for h in range(own_tabs):
            doff[c, h] = d_off[c][:, h * LANES : (h + 1) * LANES]

    acc_x[...] = jnp.zeros_like(acc_x)

    def force_step(kb, carry):
        for j in range(per):
            k = kb * per + j
            tab_row = whole_row(tabd, k)
            hit = tab_row == lax.broadcasted_iota(jnp.int32, (8, atoms), 0)
            rows = [jnp.where(hit, whole_row(doff.at[c], k), 0.0) for c in range(3)]
            full = jnp.concatenate(rows, axis=0)
            hi = full.astype(BF16).astype(F32)
            lhs_x[:, j * atoms : (j + 1) * atoms] = jnp.concatenate(
                [hi, full - hi], axis=0
            ).astype(BF16)
        hot = jnp.concatenate([onehot[kb * per + j] for j in range(per)], axis=1)
        acc_x[...] += mm_nt(lhs_x[...], hot)
        return carry

    lax.fori_loop(0, depth // per, force_step, 0)
    table_force = [acc_x[c * 8 : (c + 1) * 8, :] + acc_x[24 + c * 8 : 32 + c * 8, :] for c in range(3)]
    pad = jnp.zeros((5, LANES), F32)
    for t in range(domains):
        xsend[t] = jnp.concatenate([f[t : t + 1] for f in table_force] + [pad], axis=0)
    space_start(3, xsend, xback)
    xback[dom] = xsend[dom]
    own_force = jnp.concatenate(
        [
            jnp.concatenate([f[domains + h : domains + h + 1] for f in table_force], axis=0)
            for h in range(own_tabs)
        ],
        axis=1,
    )

    def wait_q(d, carry):
        bead_copy(0, d, qtile, qall).wait()
        return carry

    lax.fori_loop(1, beads, wait_q, 0)
    half_step = 0.5 * beads / 3.0
    partial = mom_ref[...].reshape(3, atoms) - half_step * (own_force - centre)
    wqq, wqp, wpq = circulant_weights(beads)
    q_q = sum(float(wqq[d]) * qall[d] for d in range(beads))
    p_q = sum(float(wpq[d]) * qall[d] for d in range(beads))
    space_wait(3, xsend, xback)
    kicked = partial - half_step * to_owner(xback)[0:3]
    for h in range(own_tabs):
        ptile[4 * h : 4 * h + 3] = kicked[:, h * LANES : (h + 1) * LANES]
        ptile[4 * h + 3 : 4 * h + 4] = zero_row

    def start_p(d, carry):
        bead_copy(1, d, ptile, pall).start()
        return carry

    lax.fori_loop(1, beads, start_p, 0)
    pall[0] = ptile[...]
    mass = jnp.concatenate(
        [
            jnp.broadcast_to(
                jnp.where(kind_row[:, h * LANES : (h + 1) * LANES] > 0.5, MASS_HYDROGEN, MASS_OXYGEN),
                (4, LANES),
            )
            for h in range(own_tabs)
        ],
        axis=0,
    )

    def wait_p(d, carry):
        bead_copy(1, d, ptile, pall).wait()
        return carry

    lax.fori_loop(1, beads, wait_p, 0)
    q_p = sum(float(wqp[d]) * pall[d] for d in range(beads))
    p_p = sum(float(wqq[d]) * pall[d] for d in range(beads))
    new_q = q_q + q_p / mass
    new_p = p_p - mass * p_q
    for h in range(own_tabs):
        lanes = slice(h * LANES, (h + 1) * LANES)
        newq_ref[:, 0, lanes] = new_q[4 * h : 4 * h + 3]
        newp_ref[:, 0, lanes] = new_p[4 * h : 4 * h + 3]


def shards(
    positions,
    momenta,
    species,
    neighbours,
    counts,
    exports,
    embed,
    radial_one_in,
    radial_one_out,
    mix_one,
    radial_two_in,
    radial_two_out,
    readout,
    energy_w,
):
    beads = lax.axis_size("bead")
    domains = lax.axis_size("space")
    depth, atoms = neighbours.shape[1:]
    chans = embed.shape[1]
    nbasis, hidden = radial_one_in.shape
    tables = atoms // LANES + domains
    per = 4
    vmem = pltpu.VMEM
    scratch = [
        vmem((8, LANES), F32),
        vmem((beads, 8, LANES), F32),
        vmem((8, LANES), F32),
        vmem((beads, 8, LANES), F32),
        vmem((domains, 8, LANES), F32),
        vmem((tables, 8, LANES), F32),
        vmem((domains, chans, LANES), F32),
        vmem((tables, chans, LANES), F32),
        vmem((domains, chans, LANES), F32),
        vmem((domains, chans, LANES), F32),
        vmem((domains, 8, LANES), F32),
        vmem((domains, 8, LANES), F32),
        vmem((2, depth * 8, LANES), F32),
        vmem((nbasis, depth, atoms), F32),
        vmem((2, depth * 8, LANES), F32),
        vmem((4, depth, atoms), F32),
        vmem((3, 2, depth, LANES), F32),
        vmem((2, depth, LANES), F32),
        vmem((2, depth, LANES), jnp.int32),
        vmem((2, depth, LANES), jnp.int32),
        vmem((2, chans, LANES), F32),
        vmem((depth, 3 * chans, atoms), F32),
        vmem((depth, hidden, atoms), F32),
        vmem((depth, 3 * chans, atoms), F32),
        vmem((depth, hidden, atoms), F32),
        vmem((depth, chans, atoms), F32),
        vmem((9, chans, atoms), F32),
        vmem((9, chans, atoms), F32),
        vmem((depth, LANES, atoms), BF16),
        vmem((atoms, domains * LANES), BF16),
        vmem((tables * 2 * chans, per * atoms), BF16),
        vmem((tables * 2 * chans, LANES), F32),
        vmem((48, per * atoms), BF16),
        vmem((48, LANES), F32),
        vmem((2, depth * 8, LANES), F32),
        vmem((2, depth * 8, LANES), F32),
        pltpu.SemaphoreType.DMA((4, domains)),
        pltpu.SemaphoreType.DMA((4, domains)),
        pltpu.SemaphoreType.DMA((2, beads)),
        pltpu.SemaphoreType.DMA((2, beads)),
    ]
    whole = pl.BlockSpec(memory_space=pltpu.VMEM)
    new_q, new_p = pl.pallas_call(
        functools.partial(kernel, beads, domains),
        out_shape=(
            jax.ShapeDtypeStruct((3, 1, atoms), F32),
            jax.ShapeDtypeStruct((3, 1, atoms), F32),
        ),
        in_specs=[whole] * 14,
        out_specs=(whole, whole),
        scratch_shapes=scratch,
        compiler_params=pltpu.CompilerParams(
            collective_id=0, has_side_effects=True, vmem_limit_bytes=56 * 1024 * 1024
        ),
    )(
        positions.transpose(1, 0, 2),
        momenta.transpose(1, 0, 2),
        species.reshape(1, atoms),
        neighbours[0],
        counts,
        exports[0, 0],
        embed,
        radial_one_in,
        radial_one_out,
        mix_one.T,
        radial_two_in,
        radial_two_out,
        readout.T,
        energy_w.reshape(1, hidden),
    )
    return new_q.transpose(1, 0, 2), new_p.transpose(1, 0, 2)


def solution(mesh):
    placed = (
        P("bead", None, "space"),
        P("bead", None, "space"),
        P("space"),
        P("bead", None, "space"),
        P("bead", "space"),
        P("bead", "space", None, None),
        P(),
        P(),
        P(),
        P(),
        P(),
        P(),
        P(),
        P(),
    )
    return jax.shard_map(
        shards,
        mesh=mesh,
        in_specs=placed,
        out_specs=(P("bead", None, "space"), P("bead", None, "space")),
        check_vma=False,
    )
```

```python
import functools
import math

import jax
import jax.numpy as jnp
import numpy as np
from jax import lax
from jax.experimental import pallas as pl
from jax.experimental.pallas import tpu as pltpu
from jax.sharding import PartitionSpec as P

RCUT = 6.0
CYCLE_FREQ = 1.5
MASS_OXYGEN = 15.999
MASS_HYDROGEN = 1.008
LANES = 128
F32 = jnp.float32
BF16 = jnp.bfloat16
MESH = pl.DeviceIdType.MESH
ROOT3 = math.sqrt(3.0)
ROOT5 = math.sqrt(5.0)
ROOT15 = math.sqrt(15.0)
DEGREE = (0, 1, 1, 1, 2, 2, 2, 2, 2)


def circulant_weights(beads):
    dt = beads / 3.0
    k = np.arange(beads)
    w = 2.0 * CYCLE_FREQ * np.sin(np.pi * k / beads)
    cosine = np.cos(w * dt)
    sine = np.sin(w * dt)
    reach = np.where(k == 0, dt, sine / np.where(k == 0, 1.0, w))
    stiff = w * sine
    d = np.arange(beads)
    waves = np.cos(2.0 * np.pi * d[:, None] * k[None, :] / beads) / beads
    return [(waves @ f).astype(np.float32) for f in (cosine, reach, stiff)]


def split(x):
    hi = x.astype(BF16)
    lo = (x - hi.astype(F32)).astype(BF16)
    return hi, lo


def rhs3(x):
    hi, lo = split(x)
    return jnp.concatenate([hi, lo, hi], axis=0)


def lhs3(w):
    hi = w.astype(BF16).astype(F32)
    lo = w - hi
    return jnp.concatenate([hi, hi, lo], axis=1).astype(BF16)


def mm(a, b):
    return jnp.dot(a, b, preferred_element_type=F32)


def mm_nt(a, b):
    return lax.dot_general(a, b, (((1,), (1,)), ((), ())), preferred_element_type=F32)


def lane_take(table, index):
    return jnp.take_along_axis(table, index, axis=1)


def silu_parts(x):
    sig = 0.5 * jnp.tanh(0.5 * x) + 0.5
    val = x * sig
    return val, sig + val * (1.0 - sig)


def rows_to_tile(parts, sub):
    low = sub < 4
    quads = []
    for j in range(4):
        a, b = parts[j], parts[j + 4]
        quads.append(jnp.where(low, a, b) + pltpu.roll(jnp.where(low, b, a), 4, 0))
    even2 = (sub & 2) == 0
    pairs = []
    for j in range(2):
        a, b = quads[j], quads[j + 2]
        pairs.append(jnp.where(even2, a + pltpu.roll(a, 6, 0), b + pltpu.roll(b, 2, 0)))
    even1 = (sub & 1) == 0
    a, b = pairs
    return jnp.where(even1, a + pltpu.roll(a, 7, 0), b + pltpu.roll(b, 1, 0))


def kernel(
    beads,
    domains,
    pos_ref,
    mom_ref,
    kind_ref,
    neigh_ref,
    count_ref,
    exp_ref,
    embed_ref,
    w1i_ref,
    w1o_ref,
    mix_ref,
    w2i_ref,
    w2o_ref,
    read_ref,
    ew_ref,
    newq_ref,
    newp_ref,
    qtile,
    qall,
    ptile,
    pall,
    psend,
    slots,
    fsend,
    ftab,
    gsend,
    gback,
    xsend,
    xback,
    bas,
    dbas,
    ylm,
    geo,
    doff,
    kindd,
    lowd,
    tabd,
    embeds,
    rad1,
    rad1s,
    rad2,
    rad2s,
    feat2,
    amp1,
    amp2,
    onehot,
    onehot_exp,
    lhs_a,
    lhs_b,
    acc_g,
    lhs_x,
    acc_x,
    r_grad,
    ylm_grad,
    act3a,
    act3b,
    send_sem,
    recv_sem,
    bsend_sem,
    brecv_sem,
):
    bead = lax.axis_index("bead")
    dom = lax.axis_index("space")
    depth, atoms = neigh_ref.shape
    chans = embed_ref.shape[1]
    tables = atoms // LANES + domains
    own_tabs = atoms // LANES
    norm = 1.0 / depth
    per = act3a.shape[1] // (2 * atoms)
    blocks = depth // per

    barrier = pltpu.get_barrier_semaphore()
    for d in range(1, domains):
        pl.semaphore_signal(
            barrier, inc=1, device_id=(bead, lax.rem(dom + d, domains)), device_id_type=MESH
        )

    def greet(d, carry):
        pl.semaphore_signal(
            barrier, inc=1, device_id=(lax.rem(bead + d, beads), dom), device_id_type=MESH
        )
        return carry

    lax.fori_loop(1, beads, greet, 0)

    def space_copy(stage, d, src, dst):
        peer = lax.rem(dom + d, domains)
        return pltpu.make_async_remote_copy(
            src_ref=src.at[peer],
            dst_ref=dst.at[dom],
            send_sem=send_sem.at[stage, d],
            recv_sem=recv_sem.at[stage, d],
            device_id=(bead, peer),
            device_id_type=MESH,
        )

    def space_start(stage, src, dst):
        for d in range(1, domains):
            space_copy(stage, d, src, dst).start()

    def space_wait(stage, src, dst):
        for d in range(1, domains):
            space_copy(stage, d, src, dst).wait()

    def bead_copy(stage, d, src, dst):
        return pltpu.make_async_remote_copy(
            src_ref=src,
            dst_ref=dst.at[d],
            send_sem=bsend_sem.at[stage, d],
            recv_sem=brecv_sem.at[stage, d],
            device_id=(lax.rem(bead + d, beads), dom),
            device_id_type=MESH,
        )

    own = pos_ref[...].reshape(3, atoms)
    kind_row = kind_ref[...].astype(F32)
    zero_row = jnp.zeros((1, LANES), F32)
    for h in range(own_tabs):
        lanes = slice(h * LANES, (h + 1) * LANES)
        slots_h = jnp.concatenate(
            [own[:, lanes], kind_row[:, lanes], zero_row, zero_row, zero_row, zero_row], axis=0
        )
        slots[domains + h] = slots_h
        qtile[4 * h : 4 * h + 4] = slots_h[0:4]
    for t in range(domains):
        row = jnp.broadcast_to(exp_ref[t : t + 1, :], (8, LANES))
        low = row & (LANES - 1)
        picked = lane_take(slots[domains], low)
        for h in range(1, own_tabs):
            picked = jnp.where(
                (row >> 7) == h, lane_take(slots[domains + h], low), picked
            )
        psend[t] = picked

    pl.semaphore_wait(barrier, domains - 1 + beads - 1)
    space_start(0, psend, slots)

    def start_q(d, carry):
        bead_copy(0, d, qtile, qall).start()
        return carry

    lax.fori_loop(1, beads, start_q, 0)
    qall[0] = qtile[...]

    w1i = w1i_ref[...]
    w1o = w1o_ref[...]
    w2i = w2i_ref[...]
    w2o = w2o_ref[...]
    nbasis, hidden = w1i.shape

    def in_lhs(w):
        wt = w.T
        hi = wt.astype(BF16).astype(F32)
        wide = jnp.concatenate([hi, hi, wt - hi], axis=1)
        none = jnp.zeros_like(wide)
        return jnp.concatenate(
            [jnp.concatenate([wide, none], axis=1), jnp.concatenate([none, wide], axis=1)], axis=0
        ).astype(BF16)

    f1i, f1o = in_lhs(w1i), lhs3(w1o.T)
    f2i, f2o = in_lhs(w2i), lhs3(w2o.T)
    mix_f, mix_b = lhs3(mix_ref[...]), lhs3(mix_ref[...].T)
    read_f, read_b = lhs3(read_ref[...]), lhs3(read_ref[...].T)
    embed_t = embed_ref[...].T
    for kind in range(2):
        embeds[kind] = jnp.broadcast_to(embed_t[:, kind : kind + 1], (chans, LANES))
    energy_t = ew_ref[...].T

    slots[dom] = psend[dom]
    for t in range(domains):
        onehot_exp[:, t * LANES : (t + 1) * LANES] = (
            (lax.broadcasted_iota(jnp.int32, (atoms, LANES), 0) == exp_ref[t : t + 1, :])
            .astype(F32)
            .astype(BF16)
        )
    low_all = neigh_ref[...] & (LANES - 1)
    for h in range(own_tabs):
        lowd[h] = low_all[:, h * LANES : (h + 1) * LANES]
    slot_iota = lax.broadcasted_iota(jnp.int32, (LANES, atoms), 0).astype(F32).astype(BF16)

    def hot_step(k, carry):
        row = jnp.concatenate([lowd[h, pl.ds(k, 1), :] for h in range(own_tabs)], axis=1)
        row = row.astype(F32).astype(BF16)
        onehot[k] = jnp.where(slot_iota == row, jnp.ones_like(slot_iota), jnp.zeros_like(slot_iota))
        return carry

    lax.fori_loop(0, depth, hot_step, 0, unroll=4)
    space_wait(0, psend, slots)

    def table_of(index):
        t = index >> 7
        return jnp.where(t < own_tabs, t + domains, t - own_tabs)

    idx = neigh_ref[...]
    tab_all = table_of(idx)
    planes = []
    for comp in range(4):
        halves = []
        for h in range(own_tabs):
            lanes = slice(h * LANES, (h + 1) * LANES)
            low, tab = low_all[:, lanes], tab_all[:, lanes]
            out = None
            for t in range(tables):
                source = jnp.broadcast_to(slots[t, comp : comp + 1, :], (depth, LANES))
                got = lane_take(source, low)
                out = got if out is None else jnp.where(tab == t, got, out)
            halves.append(out)
        planes.append(jnp.concatenate(halves, axis=1))
    for h in range(own_tabs):
        lanes = slice(h * LANES, (h + 1) * LANES)
        kindd[h] = planes[3][:, lanes]
        tabd[h] = tab_all[:, lanes]

    def plane_row(ref, k, h):
        return ref[h, pl.ds(k, 1), :]

    def whole_row(ref, k):
        return jnp.concatenate([plane_row(ref, k, h) for h in range(own_tabs)], axis=1)


    def geometry():
        off = [planes[c] - own[c : c + 1, :] for c in range(3)]
        dist = jnp.sqrt(off[0] * off[0] + off[1] * off[1] + off[2] * off[2] + 1.0)
        inv = 1.0 / dist
        return [o * inv for o in off], dist, inv

    u, dist, inv = geometry()
    present = (
        lax.broadcasted_iota(jnp.int32, (depth, atoms), 0) < count_ref[...]
    ).astype(F32)
    scaled = jnp.minimum(dist * (1.0 / RCUT), 1.0)
    arg = math.pi * (scaled - 0.5)
    sq = arg * arg
    cos_y = 1.0
    for n in range(7, 0, -1):
        cos_y = 1.0 - cos_y * sq * (1.0 / ((2 * n - 1) * (2 * n)))
    sin_y = 1.0
    for n in range(6, 0, -1):
        sin_y = 1.0 - sin_y * sq * (1.0 / ((2 * n) * (2 * n + 1)))
    sin_y = sin_y * arg
    sines, cosines = {1: cos_y}, {1: -sin_y}
    for n in range(2, nbasis + 1):
        a, b = n // 2, n - n // 2
        sines[n] = sines[a] * cosines[b] + cosines[a] * sines[b]
        cosines[n] = cosines[a] * cosines[b] - sines[a] * sines[b]
    gap = 1.0 - scaled * scaled
    env = gap * gap * present * inv
    slope = -(4.0 / RCUT) * scaled * gap * present * inv - env * inv

    def strided_put(ref, j, plane):
        for h in range(own_tabs):
            ref[h, pl.ds(j, depth, stride=8), :] = plane[:, h * LANES : (h + 1) * LANES]

    def strided_get(ref, j):
        return jnp.concatenate(
            [ref[h, pl.ds(j, depth, stride=8), :] for h in range(own_tabs)], axis=1
        )

    def rows_get(ref, k):
        rows = pl.ds(pl.multiple_of(k * 8, 8), 8)
        return jnp.concatenate([ref[h, rows, :] for h in range(own_tabs)], axis=1)

    def rows_put(ref, k, value, add):
        rows = pl.ds(pl.multiple_of(k * 8, 8), 8)
        for h in range(own_tabs):
            part = value[:, h * LANES : (h + 1) * LANES]
            ref[h, rows, :] = ref[h, rows, :] + part if add else part

    for n in range(1, nbasis + 1):
        strided_put(bas, n - 1, sines[n] * env)
    ux, uy, uz = u
    harmonic = [
        ROOT3 * ux,
        ROOT3 * uy,
        ROOT3 * uz,
        ROOT15 * ux * uy,
        ROOT15 * uy * uz,
        ROOT15 * ux * uz,
        0.5 * ROOT15 * (ux * ux - uy * uy),
        0.5 * ROOT5 * (2.0 * uz * uz - ux * ux - uy * uy),
    ]
    for m in range(8):
        strided_put(ylm, m, harmonic[m])
    for n in range(1, nbasis + 1):
        strided_put(dbas, n - 1, (n * math.pi / RCUT) * cosines[n] * env + sines[n] * slope)
    for c in range(3):
        geo[c] = u[c]
    geo[3] = inv

    act3b[...] = jnp.zeros_like(act3b)

    def hi_lo_hi(x):
        hi = x.astype(BF16).astype(F32)
        return [hi, x - hi, hi]

    def radial_in(kb, w_in, act):
        xs = []
        for j in range(per):
            k = kb * per + j
            rows = hi_lo_hi(rows_get(bas, k)) + hi_lo_hi(rows_get(dbas, k))
            xs.append(jnp.concatenate(rows, axis=0).astype(BF16))
        for j in range(per):
            pre = mm(w_in, xs[j])
            val, steep = silu_parts(pre[:hidden])
            base = 2 * j * atoms
            act[:, base : base + atoms] = rhs3(val)
            act[:, base + atoms : base + 2 * atoms] = rhs3(steep * pre[hidden:])

    def radial_out(kb, w_out, act, rad, slopes, feature):
        for j in range(per):
            k = kb * per + j
            out = mm(w_out, act[:, 2 * j * atoms : 2 * (j + 1) * atoms])
            val, steep = out[:, :atoms], out[:, atoms:]
            if feature is not None:
                f = jnp.concatenate([feature(k, h) for h in range(own_tabs)], axis=1)
                f = jnp.concatenate([f, f, f], axis=0)
                val, steep = val * f, steep * f
            rad[k] = val
            slopes[k] = steep

    def radial_net(w_in, w_out, rad, slopes, feature):
        def step(p, carry):
            radial_out(jnp.maximum(2 * p - 1, 0), w_out, act3b, rad, slopes, feature)
            radial_in(2 * p, w_in, act3a)
            radial_out(2 * p, w_out, act3a, rad, slopes, feature)
            radial_in(2 * p + 1, w_in, act3b)
            return carry

        lax.fori_loop(0, blocks // 2, step, 0)
        radial_out(blocks - 1, w_out, act3b, rad, slopes, feature)

    group = 16

    def y_row(k, m, h):
        return ylm[h, pl.ds(k * 8 + m - 1, 1), :]

    def amplitudes(amp, rad, feature):
        invs = [[[None] * own_tabs for _ in range(chans // group)] for _ in range(3)]
        for h in range(own_tabs):
            lanes = slice(h * LANES, (h + 1) * LANES)
            for g in range(chans // group):

                def step(k, acc):
                    ws = [
                        rad[k, deg * chans + g * group : deg * chans + (g + 1) * group, lanes]
                        for deg in range(3)
                    ]
                    if feature is not None:
                        f = feature(k, g, h)
                        ws = [w * f for w in ws]
                    out = [acc[0] + ws[0]]
                    for m in range(1, 9):
                        out.append(acc[m] + ws[DEGREE[m]] * y_row(k, m, h))
                    return tuple(out)

                start = tuple(jnp.zeros((group, LANES), F32) for _ in range(9))
                acc = lax.fori_loop(0, depth, step, start, unroll=4)
                sums = [0.0, 0.0, 0.0]
                for m in range(9):
                    amp[m, g * group : (g + 1) * group, lanes] = acc[m]
                    sums[DEGREE[m]] = sums[DEGREE[m]] + acc[m] * acc[m]
                for deg in range(3):
                    invs[deg][g][h] = sums[deg] * norm
        rows = []
        for deg in range(3):
            for g in range(chans // group):
                rows.append(jnp.concatenate(invs[deg][g], axis=1))
        return jnp.concatenate(rows, axis=0)

    def scale_amp(amp, d_inv):
        for m in range(9):
            deg = DEGREE[m]
            amp[m] = amp[m] * d_inv[deg * chans : (deg + 1) * chans] * (2.0 * norm)

    def kind_feature(k, h):
        return jnp.where(plane_row(kindd, k, h) > 0.5, embeds[1], embeds[0])

    def slot_feature(k, g, h):
        return feat2[k, g * group : (g + 1) * group, h * LANES : (h + 1) * LANES]

    radial_net(f1i, f1o, rad1, rad1s, kind_feature)
    inv1 = amplitudes(amp1, rad1, None)
    act1, slope1 = silu_parts(mm(mix_f, rhs3(inv1)))
    own_embed = jnp.where(kind_row > 0.5, embed_t[:, 1:2], embed_t[:, 0:1])
    layer_one = own_embed + act1
    for h in range(own_tabs):
        ftab[domains + h] = layer_one[:, h * LANES : (h + 1) * LANES]
    for t in range(domains):
        row = jnp.broadcast_to(exp_ref[t : t + 1, :], (chans, LANES))
        low = row & (LANES - 1)
        picked = lane_take(ftab[domains], low)
        for h in range(1, own_tabs):
            picked = jnp.where((row >> 7) == h, lane_take(ftab[domains + h], low), picked)
        fsend[t] = picked
    space_start(1, fsend, ftab)
    ftab[dom] = fsend[dom]

    radial_net(f2i, f2o, rad2, rad2s, None)
    space_wait(1, fsend, ftab)

    def gather_step(k, carry):
        low_row = whole_row(lowd, k)
        tab_row = whole_row(tabd, k)
        for h in range(own_tabs):
            lanes = slice(h * LANES, (h + 1) * LANES)
            low = jnp.broadcast_to(low_row[:, lanes], (chans, LANES))
            out = lane_take(ftab[0], low)
            for t in range(1, tables):
                out = jnp.where(tab_row[:, lanes] == t, lane_take(ftab[t], low), out)
            feat2[k, :, lanes] = out
        return carry

    lax.fori_loop(0, depth, gather_step, 0, unroll=4)

    inv2 = amplitudes(amp2, rad2, slot_feature)
    unused, slope_r = silu_parts(mm(read_f, rhs3(inv2)))
    scale_amp(amp2, mm(read_b, rhs3(slope_r * energy_t)))

    sub = lax.broadcasted_iota(jnp.int32, (8, LANES), 0)

    def edge_pass(k, amp, rad, slopes, feature):
        d_ylms, d_rs, d_feats = [], [], []
        for h in range(own_tabs):
            lanes = slice(h * LANES, (h + 1) * LANES)
            rads = [rad[k, deg * chans : (deg + 1) * chans, lanes] for deg in range(3)]
            steep = [slopes[k, deg * chans : (deg + 1) * chans, lanes] for deg in range(3)]
            ws = rads
            if feature is not None:
                f = jnp.concatenate([feature(k, g, h) for g in range(chans // group)], axis=0)
                ws = [r * f for r in rads]
            d_ws = [amp[0, :, lanes], None, None]
            parts = []
            for m in range(1, 9):
                deg = DEGREE[m]
                da = amp[m, :, lanes]
                term = da * y_row(k, m, h)
                d_ws[deg] = term if d_ws[deg] is None else d_ws[deg] + term
                parts.append(fold(da * ws[deg]))
            d_ylms.append(rows_to_tile(parts, sub))
            by_r = d_ws[0] * steep[0] + d_ws[1] * steep[1] + d_ws[2] * steep[2]
            if feature is not None:
                by_r = by_r * f
                d_feats.append(d_ws[0] * rads[0] + d_ws[1] * rads[1] + d_ws[2] * rads[2])
            d_rs.append(fold(by_r))
        d_feat = jnp.concatenate(d_feats, axis=1) if d_feats else None
        return jnp.concatenate(d_ylms, axis=1), d_rs, d_feat

    def fold(x):
        return (x[0:8] + x[8:16]) + (x[16:24] + x[24:32])

    def distances_put(p, d_rs, add):
        rows = pl.ds(pl.multiple_of(p * 8, 8), 8)
        for h in range(own_tabs):
            tile = rows_to_tile([d[h] for d in d_rs], sub)
            r_grad[h, rows, :] = r_grad[h, rows, :] + tile if add else tile

    acc_g[...] = jnp.zeros_like(acc_g)
    lhs_b[...] = jnp.zeros_like(lhs_b)

    def second_edges(kb, lhs):
        d_rs = []
        for j in range(per):
            k = kb * per + j
            d_ylm, d_r_k, d_feat = edge_pass(k, amp2, rad2, rad2s, slot_feature)
            rows_put(ylm_grad, k, d_ylm, False)
            d_rs.append(d_r_k)
            hi, lo = split(d_feat)
            both = jnp.concatenate([hi, lo], axis=0)
            tab_row = whole_row(tabd, k)
            for t in range(tables):
                hit = (tab_row == t).astype(F32).astype(BF16)
                lhs[t * 2 * chans : (t + 1) * 2 * chans, j * atoms : (j + 1) * atoms] = both * hit
        return d_rs

    def scatter_block(kb, lhs):
        hot = jnp.concatenate([onehot[kb * per + j] for j in range(per)], axis=1)
        acc_g[...] += mm_nt(lhs[...], hot)

    def second_back(p, carry):
        scatter_block(jnp.maximum(2 * p - 1, 0), lhs_b)
        d_rs = second_edges(2 * p, lhs_a)
        scatter_block(2 * p, lhs_a)
        d_rs = d_rs + second_edges(2 * p + 1, lhs_b)
        distances_put(p, d_rs, False)
        return carry

    lax.fori_loop(0, blocks // 2, second_back, 0)
    scatter_block(blocks - 1, lhs_b)

    def table_grad(t):
        base = t * 2 * chans
        return acc_g[base : base + chans, :] + acc_g[base + chans : base + 2 * chans, :]

    for t in range(domains):
        gsend[t] = table_grad(t)
    space_start(2, gsend, gback)
    gback[dom] = gsend[dom]
    own_grad = jnp.concatenate([table_grad(domains + h) for h in range(own_tabs)], axis=1)
    space_wait(2, gsend, gback)

    def to_owner(back):
        rows = back.shape[1]
        flat = jnp.concatenate([back[t] for t in range(domains)], axis=1)
        hi = flat.astype(BF16).astype(F32)
        both = jnp.concatenate([hi, flat - hi], axis=0).astype(BF16)
        out = mm_nt(both, onehot_exp[...])
        return out[:rows] + out[rows:]

    d_layer = own_grad + to_owner(gback)
    scale_amp(amp1, mm(mix_b, rhs3(d_layer * slope1)))

    def first_back(p, carry):
        d_rs = []
        for j in range(8):
            k = p * 8 + j
            d_ylm, d_r_k, unused_feat = edge_pass(k, amp1, rad1, rad1s, None)
            rows_put(ylm_grad, k, d_ylm, True)
            d_rs.append(d_r_k)
        distances_put(p, d_rs, True)
        return carry

    lax.fori_loop(0, depth // 8, first_back, 0)

    ux, uy, uz = geo[0], geo[1], geo[2]
    d_r = jnp.concatenate([r_grad[h] for h in range(own_tabs)], axis=1)
    dy = [strided_get(ylm_grad, m) for m in range(8)]
    dux = ROOT3 * dy[0] + ROOT15 * (uy * dy[3] + uz * dy[5] + ux * dy[6]) - ROOT5 * (ux * dy[7])
    duy = ROOT3 * dy[1] + ROOT15 * (ux * dy[3] + uz * dy[4] - uy * dy[6]) - ROOT5 * (uy * dy[7])
    duz = ROOT3 * dy[2] + ROOT15 * (uy * dy[4] + ux * dy[5]) + (2.0 * ROOT5) * (uz * dy[7])
    along = d_r - geo[3] * (ux * dux + uy * duy + uz * duz)
    d_off = [geo[3] * d + v * along for d, v in ((dux, ux), (duy, uy), (duz, uz))]
    centre = jnp.concatenate([jnp.sum(d, axis=0, keepdims=True) for d in d_off], axis=0)
    for c in range(3):
        for h in range(own_tabs):
            doff[c, h] = d_off[c][:, h * LANES : (h + 1) * LANES]

    acc_x[...] = jnp.zeros_like(acc_x)

    def force_step(kb, carry):
        for j in range(per):
            k = kb * per + j
            tab_row = whole_row(tabd, k)
            hit = tab_row == lax.broadcasted_iota(jnp.int32, (8, atoms), 0)
            rows = [jnp.where(hit, whole_row(doff.at[c], k), 0.0) for c in range(3)]
            full = jnp.concatenate(rows, axis=0)
            hi = full.astype(BF16).astype(F32)
            lhs_x[:, j * atoms : (j + 1) * atoms] = jnp.concatenate(
                [hi, full - hi], axis=0
            ).astype(BF16)
        hot = jnp.concatenate([onehot[kb * per + j] for j in range(per)], axis=1)
        acc_x[...] += mm_nt(lhs_x[...], hot)
        return carry

    lax.fori_loop(0, depth // per, force_step, 0)
    table_force = [acc_x[c * 8 : (c + 1) * 8, :] + acc_x[24 + c * 8 : 32 + c * 8, :] for c in range(3)]
    pad = jnp.zeros((5, LANES), F32)
    for t in range(domains):
        xsend[t] = jnp.concatenate([f[t : t + 1] for f in table_force] + [pad], axis=0)
    space_start(3, xsend, xback)
    xback[dom] = xsend[dom]
    own_force = jnp.concatenate(
        [
            jnp.concatenate([f[domains + h : domains + h + 1] for f in table_force], axis=0)
            for h in range(own_tabs)
        ],
        axis=1,
    )

    def wait_q(d, carry):
        bead_copy(0, d, qtile, qall).wait()
        return carry

    lax.fori_loop(1, beads, wait_q, 0)
    half_step = 0.5 * beads / 3.0
    partial = mom_ref[...].reshape(3, atoms) - half_step * (own_force - centre)
    wqq, wqp, wpq = circulant_weights(beads)
    q_q = sum(float(wqq[d]) * qall[d] for d in range(beads))
    p_q = sum(float(wpq[d]) * qall[d] for d in range(beads))
    space_wait(3, xsend, xback)
    kicked = partial - half_step * to_owner(xback)[0:3]
    for h in range(own_tabs):
        ptile[4 * h : 4 * h + 3] = kicked[:, h * LANES : (h + 1) * LANES]
        ptile[4 * h + 3 : 4 * h + 4] = zero_row

    def start_p(d, carry):
        bead_copy(1, d, ptile, pall).start()
        return carry

    lax.fori_loop(1, beads, start_p, 0)
    pall[0] = ptile[...]
    mass = jnp.concatenate(
        [
            jnp.broadcast_to(
                jnp.where(kind_row[:, h * LANES : (h + 1) * LANES] > 0.5, MASS_HYDROGEN, MASS_OXYGEN),
                (4, LANES),
            )
            for h in range(own_tabs)
        ],
        axis=0,
    )

    def wait_p(d, carry):
        bead_copy(1, d, ptile, pall).wait()
        return carry

    lax.fori_loop(1, beads, wait_p, 0)
    q_p = sum(float(wqp[d]) * pall[d] for d in range(beads))
    p_p = sum(float(wqq[d]) * pall[d] for d in range(beads))
    new_q = q_q + q_p / mass
    new_p = p_p - mass * p_q
    for h in range(own_tabs):
        lanes = slice(h * LANES, (h + 1) * LANES)
        newq_ref[:, 0, lanes] = new_q[4 * h : 4 * h + 3]
        newp_ref[:, 0, lanes] = new_p[4 * h : 4 * h + 3]


def shards(
    positions,
    momenta,
    species,
    neighbours,
    counts,
    exports,
    embed,
    radial_one_in,
    radial_one_out,
    mix_one,
    radial_two_in,
    radial_two_out,
    readout,
    energy_w,
):
    beads = lax.axis_size("bead")
    domains = lax.axis_size("space")
    depth, atoms = neighbours.shape[1:]
    chans = embed.shape[1]
    nbasis, hidden = radial_one_in.shape
    tables = atoms // LANES + domains
    per = 4
    vmem = pltpu.VMEM
    scratch = [
        vmem((8, LANES), F32),
        vmem((beads, 8, LANES), F32),
        vmem((8, LANES), F32),
        vmem((beads, 8, LANES), F32),
        vmem((domains, 8, LANES), F32),
        vmem((tables, 8, LANES), F32),
        vmem((domains, chans, LANES), F32),
        vmem((tables, chans, LANES), F32),
        vmem((domains, chans, LANES), F32),
        vmem((domains, chans, LANES), F32),
        vmem((domains, 8, LANES), F32),
        vmem((domains, 8, LANES), F32),
        vmem((2, depth * 8, LANES), F32),
        vmem((2, depth * 8, LANES), F32),
        vmem((2, depth * 8, LANES), F32),
        vmem((4, depth, atoms), F32),
        vmem((3, 2, depth, LANES), F32),
        vmem((2, depth, LANES), F32),
        vmem((2, depth, LANES), jnp.int32),
        vmem((2, depth, LANES), jnp.int32),
        vmem((2, chans, LANES), F32),
        vmem((depth, 3 * chans, atoms), F32),
        vmem((depth, 3 * chans, atoms), F32),
        vmem((depth, 3 * chans, atoms), F32),
        vmem((depth, 3 * chans, atoms), F32),
        vmem((depth, chans, atoms), F32),
        vmem((9, chans, atoms), F32),
        vmem((9, chans, atoms), F32),
        vmem((depth, LANES, atoms), BF16),
        vmem((atoms, domains * LANES), BF16),
        vmem((tables * 2 * chans, per * atoms), BF16),
        vmem((tables * 2 * chans, per * atoms), BF16),
        vmem((tables * 2 * chans, LANES), F32),
        vmem((48, per * atoms), BF16),
        vmem((48, LANES), F32),
        vmem((2, depth, LANES), F32),
        vmem((2, depth * 8, LANES), F32),
        vmem((3 * hidden, 2 * per * atoms), BF16),
        vmem((3 * hidden, 2 * per * atoms), BF16),
        pltpu.SemaphoreType.DMA((4, domains)),
        pltpu.SemaphoreType.DMA((4, domains)),
        pltpu.SemaphoreType.DMA((2, beads)),
        pltpu.SemaphoreType.DMA((2, beads)),
    ]
    whole = pl.BlockSpec(memory_space=pltpu.VMEM)
    new_q, new_p = pl.pallas_call(
        functools.partial(kernel, beads, domains),
        out_shape=(
            jax.ShapeDtypeStruct((3, 1, atoms), F32),
            jax.ShapeDtypeStruct((3, 1, atoms), F32),
        ),
        in_specs=[whole] * 14,
        out_specs=(whole, whole),
        scratch_shapes=scratch,
        compiler_params=pltpu.CompilerParams(
            collective_id=0, has_side_effects=True, vmem_limit_bytes=56 * 1024 * 1024
        ),
    )(
        positions.transpose(1, 0, 2),
        momenta.transpose(1, 0, 2),
        species.reshape(1, atoms),
        neighbours[0],
        counts,
        exports[0, 0],
        embed,
        radial_one_in,
        radial_one_out,
        mix_one.T,
        radial_two_in,
        radial_two_out,
        readout.T,
        energy_w.reshape(1, hidden),
    )
    return new_q.transpose(1, 0, 2), new_p.transpose(1, 0, 2)


def solution(mesh):
    placed = (
        P("bead", None, "space"),
        P("bead", None, "space"),
        P("space"),
        P("bead", None, "space"),
        P("bead", "space"),
        P("bead", "space", None, None),
        P(),
        P(),
        P(),
        P(),
        P(),
        P(),
        P(),
        P(),
    )
    return jax.shard_map(
        shards,
        mesh=mesh,
        in_specs=placed,
        out_specs=(P("bead", None, "space"), P("bead", None, "space")),
        check_vma=False,
    )
```

```python
import functools
import math

import jax
import jax.numpy as jnp
import numpy as np
from jax import lax
from jax.experimental import pallas as pl
from jax.experimental.pallas import tpu as pltpu
from jax.sharding import PartitionSpec as P

RCUT = 6.0
CYCLE_FREQ = 1.5
MASS_OXYGEN = 15.999
MASS_HYDROGEN = 1.008
LANES = 128
F32 = jnp.float32
BF16 = jnp.bfloat16
MESH = pl.DeviceIdType.MESH
ROOT3 = math.sqrt(3.0)
ROOT5 = math.sqrt(5.0)
ROOT15 = math.sqrt(15.0)
DEGREE = (0, 1, 1, 1, 2, 2, 2, 2, 2)


def circulant_weights(beads):
    dt = beads / 3.0
    k = np.arange(beads)
    w = 2.0 * CYCLE_FREQ * np.sin(np.pi * k / beads)
    cosine = np.cos(w * dt)
    sine = np.sin(w * dt)
    reach = np.where(k == 0, dt, sine / np.where(k == 0, 1.0, w))
    stiff = w * sine
    d = np.arange(beads)
    waves = np.cos(2.0 * np.pi * d[:, None] * k[None, :] / beads) / beads
    return [(waves @ f).astype(np.float32) for f in (cosine, reach, stiff)]


def split(x):
    hi = x.astype(BF16)
    lo = (x - hi.astype(F32)).astype(BF16)
    return hi, lo


def rhs3(x):
    hi, lo = split(x)
    return jnp.concatenate([hi, lo, hi], axis=0)


def lhs3(w):
    hi = w.astype(BF16).astype(F32)
    lo = w - hi
    return jnp.concatenate([hi, hi, lo], axis=1).astype(BF16)


def mm(a, b):
    return jnp.dot(a, b, preferred_element_type=F32)


def mm_nt(a, b):
    return lax.dot_general(a, b, (((1,), (1,)), ((), ())), preferred_element_type=F32)


def lane_take(table, index):
    return jnp.take_along_axis(table, index, axis=1)


def silu_parts(x):
    sig = 0.5 * jnp.tanh(0.5 * x) + 0.5
    val = x * sig
    return val, sig + val * (1.0 - sig)


def rows_to_tile(parts, sub):
    low = sub < 4
    quads = []
    for j in range(4):
        a, b = parts[j], parts[j + 4]
        quads.append(jnp.where(low, a, b) + pltpu.roll(jnp.where(low, b, a), 4, 0))
    even2 = (sub & 2) == 0
    pairs = []
    for j in range(2):
        a, b = quads[j], quads[j + 2]
        pairs.append(jnp.where(even2, a + pltpu.roll(a, 6, 0), b + pltpu.roll(b, 2, 0)))
    even1 = (sub & 1) == 0
    a, b = pairs
    return jnp.where(even1, a + pltpu.roll(a, 7, 0), b + pltpu.roll(b, 1, 0))


def kernel(
    beads,
    domains,
    pos_ref,
    mom_ref,
    kind_ref,
    neigh_ref,
    count_ref,
    exp_ref,
    embed_ref,
    w1i_ref,
    w1o_ref,
    mix_ref,
    w2i_ref,
    w2o_ref,
    read_ref,
    ew_ref,
    out_ref,
    qtile,
    qall,
    ptile,
    pall,
    psend,
    slots,
    fsend,
    ftab,
    gsend,
    gback,
    xsend,
    xback,
    bas,
    dbas,
    ylm,
    geo,
    doff,
    kindd,
    lowd,
    tabd,
    embeds,
    rad1,
    rad1s,
    rad2,
    rad2s,
    wgrad,
    feat2,
    amp1,
    amp2,
    onehot,
    onehot_exp,
    lhs_a,
    lhs_b,
    acc_g,
    lhs_x,
    acc_x,
    r_grad,
    ylm_grad,
    act3a,
    act3b,
    send_sem,
    recv_sem,
):
    bead = lax.axis_index("bead")
    dom = lax.axis_index("space")
    depth, atoms = neigh_ref.shape
    chans = embed_ref.shape[1]
    tables = atoms // LANES + domains
    own_tabs = atoms // LANES
    norm = 1.0 / depth
    per = act3a.shape[1] // (2 * atoms)
    blocks = depth // per

    barrier = pltpu.get_barrier_semaphore()
    for d in range(1, domains):
        pl.semaphore_signal(
            barrier, inc=1, device_id=(bead, lax.rem(dom + d, domains)), device_id_type=MESH
        )

    def greet(d, carry):
        pl.semaphore_signal(
            barrier, inc=1, device_id=(lax.rem(bead + d, beads), dom), device_id_type=MESH
        )
        return carry

    lax.fori_loop(1, beads, greet, 0)

    def space_copy(stage, src, dst, peer):
        return pltpu.make_async_remote_copy(
            src_ref=src,
            dst_ref=dst,
            send_sem=send_sem.at[stage],
            recv_sem=recv_sem.at[stage],
            device_id=(bead, peer),
            device_id_type=MESH,
        )

    def space_start(stage, src, dst):
        for d in range(1, domains):
            peer = lax.rem(dom + d, domains)
            space_copy(stage, src.at[peer], dst.at[dom], peer).start()

    def space_wait(stage, src, dst):
        most = pl.ds(0, domains - 1)
        space_copy(stage, src.at[most], dst.at[most], lax.rem(dom + 1, domains)).wait()

    def bead_copy(stage, src, dst, d):
        return pltpu.make_async_remote_copy(
            src_ref=src,
            dst_ref=dst,
            send_sem=send_sem.at[domains + stage],
            recv_sem=recv_sem.at[domains + stage],
            device_id=(lax.rem(bead + d, beads), dom),
            device_id_type=MESH,
        )

    def bead_wait(stage, dst):
        most = pl.ds(1, beads - 1)
        bead_copy(stage, dst.at[most], dst.at[most], 1).wait()

    own = pos_ref[...].reshape(3, atoms)
    kind_row = kind_ref[...].astype(F32)
    zero_row = jnp.zeros((1, LANES), F32)
    for h in range(own_tabs):
        lanes = slice(h * LANES, (h + 1) * LANES)
        slots_h = jnp.concatenate(
            [own[:, lanes], kind_row[:, lanes], zero_row, zero_row, zero_row, zero_row], axis=0
        )
        slots[domains + h] = slots_h
        qtile[4 * h : 4 * h + 4] = slots_h[0:4]
    for t in range(domains):
        row = jnp.broadcast_to(exp_ref[t : t + 1, :], (8, LANES))
        low = row & (LANES - 1)
        picked = lane_take(slots[domains], low)
        for h in range(1, own_tabs):
            picked = jnp.where(
                (row >> 7) == h, lane_take(slots[domains + h], low), picked
            )
        psend[t] = picked

    pl.semaphore_wait(barrier, domains - 1 + beads - 1)
    space_start(0, psend, slots)

    def start_q(d, carry):
        bead_copy(0, qtile, qall.at[d], d).start()
        return carry

    lax.fori_loop(1, beads, start_q, 0)
    qall[0] = qtile[...]

    w1i = w1i_ref[...]
    w1o = w1o_ref[...]
    w2i = w2i_ref[...]
    w2o = w2o_ref[...]
    nbasis, hidden = w1i.shape

    def in_lhs(w):
        wt = w.T
        hi = wt.astype(BF16).astype(F32)
        wide = jnp.concatenate([hi, hi, wt - hi], axis=1)
        none = jnp.zeros_like(wide)
        return jnp.concatenate(
            [jnp.concatenate([wide, none], axis=1), jnp.concatenate([none, wide], axis=1)], axis=0
        ).astype(BF16)

    f1i, f1o = in_lhs(w1i), lhs3(w1o.T)
    f2i, f2o = in_lhs(w2i), lhs3(w2o.T)
    mix_f, mix_b = lhs3(mix_ref[...]), lhs3(mix_ref[...].T)
    read_f, read_b = lhs3(read_ref[...]), lhs3(read_ref[...].T)
    embed_t = embed_ref[...].T
    for kind in range(2):
        embeds[kind] = jnp.broadcast_to(embed_t[:, kind : kind + 1], (chans, LANES))
    energy_t = ew_ref[...].T

    slots[dom] = psend[dom]
    for t in range(domains):
        onehot_exp[:, t * LANES : (t + 1) * LANES] = (
            (lax.broadcasted_iota(jnp.int32, (atoms, LANES), 0) == exp_ref[t : t + 1, :])
            .astype(F32)
            .astype(BF16)
        )
    low_all = neigh_ref[...] & (LANES - 1)
    for h in range(own_tabs):
        lowd[h] = low_all[:, h * LANES : (h + 1) * LANES]
    slot_iota = lax.broadcasted_iota(jnp.int32, (LANES, atoms), 0).astype(F32).astype(BF16)

    def hot_step(k, carry):
        row = jnp.concatenate([lowd[h, pl.ds(k, 1), :] for h in range(own_tabs)], axis=1)
        row = row.astype(F32).astype(BF16)
        onehot[k] = jnp.where(slot_iota == row, jnp.ones_like(slot_iota), jnp.zeros_like(slot_iota))
        return carry

    lax.fori_loop(0, depth, hot_step, 0, unroll=4)
    space_wait(0, psend, slots)

    def table_of(index):
        t = index >> 7
        return jnp.where(t < own_tabs, t + domains, t - own_tabs)

    idx = neigh_ref[...]
    tab_all = table_of(idx)
    planes = []
    for comp in range(4):
        halves = []
        for h in range(own_tabs):
            lanes = slice(h * LANES, (h + 1) * LANES)
            low, tab = low_all[:, lanes], tab_all[:, lanes]
            out = None
            for t in range(tables):
                source = jnp.broadcast_to(slots[t, comp : comp + 1, :], (depth, LANES))
                got = lane_take(source, low)
                out = got if out is None else jnp.where(tab == t, got, out)
            halves.append(out)
        planes.append(jnp.concatenate(halves, axis=1))
    for h in range(own_tabs):
        lanes = slice(h * LANES, (h + 1) * LANES)
        kindd[h] = planes[3][:, lanes]
        tabd[h] = tab_all[:, lanes]

    def plane_row(ref, k, h):
        return ref[h, pl.ds(k, 1), :]

    def whole_row(ref, k):
        return jnp.concatenate([plane_row(ref, k, h) for h in range(own_tabs)], axis=1)


    def geometry():
        off = [planes[c] - own[c : c + 1, :] for c in range(3)]
        dist = jnp.sqrt(off[0] * off[0] + off[1] * off[1] + off[2] * off[2] + 1.0)
        inv = 1.0 / dist
        return [o * inv for o in off], dist, inv

    u, dist, inv = geometry()
    present = (
        lax.broadcasted_iota(jnp.int32, (depth, atoms), 0) < count_ref[...]
    ).astype(F32)
    scaled = jnp.minimum(dist * (1.0 / RCUT), 1.0)
    arg = math.pi * (scaled - 0.5)
    sq = arg * arg
    cos_y = 1.0
    for n in range(7, 0, -1):
        cos_y = 1.0 - cos_y * sq * (1.0 / ((2 * n - 1) * (2 * n)))
    sin_y = 1.0
    for n in range(6, 0, -1):
        sin_y = 1.0 - sin_y * sq * (1.0 / ((2 * n) * (2 * n + 1)))
    sin_y = sin_y * arg
    sines, cosines = {1: cos_y}, {1: -sin_y}
    for n in range(2, nbasis + 1):
        a, b = n // 2, n - n // 2
        sines[n] = sines[a] * cosines[b] + cosines[a] * sines[b]
        cosines[n] = cosines[a] * cosines[b] - sines[a] * sines[b]
    gap = 1.0 - scaled * scaled
    env = gap * gap * present * inv
    slope = -(4.0 / RCUT) * scaled * gap * present * inv - env * inv

    def strided_put(ref, j, plane):
        for h in range(own_tabs):
            ref[h, pl.ds(j, depth, stride=8), :] = plane[:, h * LANES : (h + 1) * LANES]

    def strided_get(ref, j):
        return jnp.concatenate(
            [ref[h, pl.ds(j, depth, stride=8), :] for h in range(own_tabs)], axis=1
        )

    def rows_get(ref, k):
        rows = pl.ds(pl.multiple_of(k * 8, 8), 8)
        return jnp.concatenate([ref[h, rows, :] for h in range(own_tabs)], axis=1)

    def rows_put(ref, k, value, add):
        rows = pl.ds(pl.multiple_of(k * 8, 8), 8)
        for h in range(own_tabs):
            part = value[:, h * LANES : (h + 1) * LANES]
            ref[h, rows, :] = ref[h, rows, :] + part if add else part

    for n in range(1, nbasis + 1):
        strided_put(bas, n - 1, sines[n] * env)
    ux, uy, uz = u
    harmonic = [
        ROOT3 * ux,
        ROOT3 * uy,
        ROOT3 * uz,
        ROOT15 * ux * uy,
        ROOT15 * uy * uz,
        ROOT15 * ux * uz,
        0.5 * ROOT15 * (ux * ux - uy * uy),
        0.5 * ROOT5 * (2.0 * uz * uz - ux * ux - uy * uy),
    ]
    for m in range(8):
        strided_put(ylm, m, harmonic[m])
    for n in range(1, nbasis + 1):
        strided_put(dbas, n - 1, (n * math.pi / RCUT) * cosines[n] * env + sines[n] * slope)
    for c in range(3):
        geo[c] = u[c]
    geo[3] = inv

    act3b[...] = jnp.zeros_like(act3b)

    def hi_lo_hi(x):
        hi = x.astype(BF16).astype(F32)
        return [hi, x - hi, hi]

    def radial_in(kb, w_in, act):
        xs = []
        for j in range(per):
            k = kb * per + j
            rows = hi_lo_hi(rows_get(bas, k)) + hi_lo_hi(rows_get(dbas, k))
            xs.append(jnp.concatenate(rows, axis=0).astype(BF16))
        for j in range(per):
            pre = mm(w_in, xs[j])
            val, steep = silu_parts(pre[:hidden])
            base = 2 * j * atoms
            act[:, base : base + atoms] = rhs3(val)
            act[:, base + atoms : base + 2 * atoms] = rhs3(steep * pre[hidden:])

    def radial_out(kb, w_out, act, rad, slopes, feature):
        for j in range(per):
            k = kb * per + j
            out = mm(w_out, act[:, 2 * j * atoms : 2 * (j + 1) * atoms])
            val, steep = out[:, :atoms], out[:, atoms:]
            if feature is not None:
                f = jnp.concatenate([feature(k, h) for h in range(own_tabs)], axis=1)
                f = jnp.concatenate([f, f, f], axis=0)
                val, steep = val * f, steep * f
            rad[k] = val
            slopes[k] = steep

    def radial_net(w_in, w_out, rad, slopes, feature):
        def step(p, carry):
            radial_out(jnp.maximum(2 * p - 1, 0), w_out, act3b, rad, slopes, feature)
            radial_in(2 * p, w_in, act3a)
            radial_out(2 * p, w_out, act3a, rad, slopes, feature)
            radial_in(2 * p + 1, w_in, act3b)
            return carry

        lax.fori_loop(0, blocks // 2, step, 0)
        radial_out(blocks - 1, w_out, act3b, rad, slopes, feature)

    group = 16

    def y_row(k, m, h):
        return ylm[h, pl.ds(k * 8 + m - 1, 1), :]

    def amplitudes(amp, rad, feature):
        invs = [[[None] * own_tabs for _ in range(chans // group)] for _ in range(3)]
        for h in range(own_tabs):
            lanes = slice(h * LANES, (h + 1) * LANES)
            for g in range(chans // group):

                def step(k, acc):
                    ws = [
                        rad[k, deg * chans + g * group : deg * chans + (g + 1) * group, lanes]
                        for deg in range(3)
                    ]
                    if feature is not None:
                        f = feature(k, g, h)
                        ws = [w * f for w in ws]
                    out = [acc[0] + ws[0]]
                    for m in range(1, 9):
                        out.append(acc[m] + ws[DEGREE[m]] * y_row(k, m, h))
                    return tuple(out)

                start = tuple(jnp.zeros((group, LANES), F32) for _ in range(9))
                acc = lax.fori_loop(0, depth, step, start, unroll=4)
                sums = [0.0, 0.0, 0.0]
                for m in range(9):
                    amp[m, g * group : (g + 1) * group, lanes] = acc[m]
                    sums[DEGREE[m]] = sums[DEGREE[m]] + acc[m] * acc[m]
                for deg in range(3):
                    invs[deg][g][h] = sums[deg] * norm
        rows = []
        for deg in range(3):
            for g in range(chans // group):
                rows.append(jnp.concatenate(invs[deg][g], axis=1))
        return jnp.concatenate(rows, axis=0)

    def scale_amp(amp, d_inv):
        for m in range(9):
            deg = DEGREE[m]
            amp[m] = amp[m] * d_inv[deg * chans : (deg + 1) * chans] * (2.0 * norm)

    def kind_feature(k, h):
        return jnp.where(plane_row(kindd, k, h) > 0.5, embeds[1], embeds[0])

    def slot_feature(k, g, h):
        return feat2[k, g * group : (g + 1) * group, h * LANES : (h + 1) * LANES]

    radial_net(f1i, f1o, rad1, rad1s, kind_feature)
    inv1 = amplitudes(amp1, rad1, None)
    act1, slope1 = silu_parts(mm(mix_f, rhs3(inv1)))
    own_embed = jnp.where(kind_row > 0.5, embed_t[:, 1:2], embed_t[:, 0:1])
    layer_one = own_embed + act1
    for h in range(own_tabs):
        ftab[domains + h] = layer_one[:, h * LANES : (h + 1) * LANES]
    for t in range(domains):
        row = jnp.broadcast_to(exp_ref[t : t + 1, :], (chans, LANES))
        low = row & (LANES - 1)
        picked = lane_take(ftab[domains], low)
        for h in range(1, own_tabs):
            picked = jnp.where((row >> 7) == h, lane_take(ftab[domains + h], low), picked)
        fsend[t] = picked
    space_start(1, fsend, ftab)
    ftab[dom] = fsend[dom]

    radial_net(f2i, f2o, rad2, rad2s, None)
    space_wait(1, fsend, ftab)

    def gather_step(k, carry):
        low_row = whole_row(lowd, k)
        tab_row = whole_row(tabd, k)
        for h in range(own_tabs):
            lanes = slice(h * LANES, (h + 1) * LANES)
            low = jnp.broadcast_to(low_row[:, lanes], (chans, LANES))
            out = lane_take(ftab[0], low)
            for t in range(1, tables):
                out = jnp.where(tab_row[:, lanes] == t, lane_take(ftab[t], low), out)
            feat2[k, :, lanes] = out
        return carry

    lax.fori_loop(0, depth, gather_step, 0, unroll=4)

    inv2 = amplitudes(amp2, rad2, slot_feature)
    unused, slope_r = silu_parts(mm(read_f, rhs3(inv2)))
    scale_amp(amp2, mm(read_b, rhs3(slope_r * energy_t)))

    sub = lax.broadcasted_iota(jnp.int32, (8, LANES), 0)

    def feature_pass(k):
        d_feats = []
        for h in range(own_tabs):
            lanes = slice(h * LANES, (h + 1) * LANES)
            total = None
            sums = [amp2[0, :, lanes], None, None]
            for m in range(1, 9):
                deg = DEGREE[m]
                term = amp2[m, :, lanes] * y_row(k, m, h)
                sums[deg] = term if sums[deg] is None else sums[deg] + term
            for deg in range(3):
                rows = slice(deg * chans, (deg + 1) * chans)
                if deg:
                    wgrad[k, rows, lanes] = sums[deg]
                part = sums[deg] * rad2[k, rows, lanes]
                total = part if total is None else total + part
            d_feats.append(total)
        return jnp.concatenate(d_feats, axis=1)

    def edge_pass(k, amp, rad, slopes, feature):
        d_ylms, d_rs = [], []
        for h in range(own_tabs):
            lanes = slice(h * LANES, (h + 1) * LANES)
            rads = [rad[k, deg * chans : (deg + 1) * chans, lanes] for deg in range(3)]
            steep = [slopes[k, deg * chans : (deg + 1) * chans, lanes] for deg in range(3)]
            ws = rads
            if feature is not None:
                f = jnp.concatenate([feature(k, g, h) for g in range(chans // group)], axis=0)
                ws = [r * f for r in rads]
            d_ws = [amp[0, :, lanes], None, None]
            if feature is not None:
                for deg in range(1, 3):
                    d_ws[deg] = wgrad[k, deg * chans : (deg + 1) * chans, lanes]
            parts = []
            for m in range(1, 9):
                deg = DEGREE[m]
                da = amp[m, :, lanes]
                if feature is None:
                    term = da * y_row(k, m, h)
                    d_ws[deg] = term if d_ws[deg] is None else d_ws[deg] + term
                parts.append(fold(da * ws[deg]))
            d_ylms.append(rows_to_tile(parts, sub))
            by_r = d_ws[0] * steep[0] + d_ws[1] * steep[1] + d_ws[2] * steep[2]
            if feature is not None:
                by_r = by_r * f
            d_rs.append(fold(by_r))
        return jnp.concatenate(d_ylms, axis=1), d_rs

    def fold(x):
        return (x[0:8] + x[8:16]) + (x[16:24] + x[24:32])

    def distances_put(p, d_rs, add):
        rows = pl.ds(pl.multiple_of(p * 8, 8), 8)
        for h in range(own_tabs):
            tile = rows_to_tile([d[h] for d in d_rs], sub)
            r_grad[h, rows, :] = r_grad[h, rows, :] + tile if add else tile

    acc_g[...] = jnp.zeros_like(acc_g)
    lhs_b[...] = jnp.zeros_like(lhs_b)

    def second_features(kb, lhs):
        for j in range(per):
            k = kb * per + j
            hi, lo = split(feature_pass(k))
            both = jnp.concatenate([hi, lo], axis=0)
            tab_row = whole_row(tabd, k)
            for t in range(tables):
                hit = (tab_row == t).astype(F32).astype(BF16)
                lhs[t * 2 * chans : (t + 1) * 2 * chans, j * atoms : (j + 1) * atoms] = both * hit

    def scatter_block(kb, lhs):
        hot = jnp.concatenate([onehot[kb * per + j] for j in range(per)], axis=1)
        acc_g[...] += mm_nt(lhs[...], hot)

    def second_back(p, carry):
        scatter_block(jnp.maximum(2 * p - 1, 0), lhs_b)
        second_features(2 * p, lhs_a)
        scatter_block(2 * p, lhs_a)
        second_features(2 * p + 1, lhs_b)
        return carry

    lax.fori_loop(0, blocks // 2, second_back, 0)
    scatter_block(blocks - 1, lhs_b)

    def edges_step(amp, rad, slopes, feature, add):
        def step(p, carry):
            d_rs = []
            for j in range(8):
                k = p * 8 + j
                d_ylm, d_r_k = edge_pass(k, amp, rad, slopes, feature)
                rows_put(ylm_grad, k, d_ylm, add)
                d_rs.append(d_r_k)
            distances_put(p, d_rs, add)
            return carry

        lax.fori_loop(0, depth // 8, step, 0)

    def table_grad(t):
        base = t * 2 * chans
        return acc_g[base : base + chans, :] + acc_g[base + chans : base + 2 * chans, :]

    for t in range(domains):
        gsend[t] = table_grad(t)
    space_start(2, gsend, gback)
    gback[dom] = gsend[dom]
    edges_step(amp2, rad2, rad2s, slot_feature, False)
    own_grad = jnp.concatenate([table_grad(domains + h) for h in range(own_tabs)], axis=1)
    space_wait(2, gsend, gback)

    def to_owner(back):
        rows = back.shape[1]
        flat = jnp.concatenate([back[t] for t in range(domains)], axis=1)
        hi = flat.astype(BF16).astype(F32)
        both = jnp.concatenate([hi, flat - hi], axis=0).astype(BF16)
        out = mm_nt(both, onehot_exp[...])
        return out[:rows] + out[rows:]

    d_layer = own_grad + to_owner(gback)
    scale_amp(amp1, mm(mix_b, rhs3(d_layer * slope1)))

    edges_step(amp1, rad1, rad1s, None, True)

    ux, uy, uz = geo[0], geo[1], geo[2]
    d_r = jnp.concatenate([r_grad[h] for h in range(own_tabs)], axis=1)
    dy = [strided_get(ylm_grad, m) for m in range(8)]
    dux = ROOT3 * dy[0] + ROOT15 * (uy * dy[3] + uz * dy[5] + ux * dy[6]) - ROOT5 * (ux * dy[7])
    duy = ROOT3 * dy[1] + ROOT15 * (ux * dy[3] + uz * dy[4] - uy * dy[6]) - ROOT5 * (uy * dy[7])
    duz = ROOT3 * dy[2] + ROOT15 * (uy * dy[4] + ux * dy[5]) + (2.0 * ROOT5) * (uz * dy[7])
    along = d_r - geo[3] * (ux * dux + uy * duy + uz * duz)
    d_off = [geo[3] * d + v * along for d, v in ((dux, ux), (duy, uy), (duz, uz))]
    centre = jnp.concatenate([jnp.sum(d, axis=0, keepdims=True) for d in d_off], axis=0)
    for c in range(3):
        for h in range(own_tabs):
            doff[c, h] = d_off[c][:, h * LANES : (h + 1) * LANES]

    acc_x[...] = jnp.zeros_like(acc_x)

    def force_step(kb, carry):
        for j in range(per):
            k = kb * per + j
            tab_row = whole_row(tabd, k)
            hit = tab_row == lax.broadcasted_iota(jnp.int32, (8, atoms), 0)
            rows = [jnp.where(hit, whole_row(doff.at[c], k), 0.0) for c in range(3)]
            full = jnp.concatenate(rows, axis=0)
            hi = full.astype(BF16).astype(F32)
            lhs_x[:, j * atoms : (j + 1) * atoms] = jnp.concatenate(
                [hi, full - hi], axis=0
            ).astype(BF16)
        hot = jnp.concatenate([onehot[kb * per + j] for j in range(per)], axis=1)
        acc_x[...] += mm_nt(lhs_x[...], hot)
        return carry

    lax.fori_loop(0, depth // per, force_step, 0)
    table_force = [acc_x[c * 8 : (c + 1) * 8, :] + acc_x[24 + c * 8 : 32 + c * 8, :] for c in range(3)]
    pad = jnp.zeros((5, LANES), F32)
    for t in range(domains):
        xsend[t] = jnp.concatenate([f[t : t + 1] for f in table_force] + [pad], axis=0)
    space_start(3, xsend, xback)
    xback[dom] = xsend[dom]
    own_force = jnp.concatenate(
        [
            jnp.concatenate([f[domains + h : domains + h + 1] for f in table_force], axis=0)
            for h in range(own_tabs)
        ],
        axis=1,
    )

    bead_wait(0, qall)
    half_step = 0.5 * beads / 3.0
    partial = mom_ref[...].reshape(3, atoms) - half_step * (own_force - centre)
    wqq, wqp, wpq = circulant_weights(beads)
    q_q = sum(float(wqq[d]) * qall[d] for d in range(beads))
    p_q = sum(float(wpq[d]) * qall[d] for d in range(beads))
    space_wait(3, xsend, xback)
    kicked = partial - half_step * to_owner(xback)[0:3]
    for h in range(own_tabs):
        ptile[4 * h : 4 * h + 3] = kicked[:, h * LANES : (h + 1) * LANES]
        ptile[4 * h + 3 : 4 * h + 4] = zero_row

    def start_p(d, carry):
        bead_copy(1, ptile, pall.at[d], d).start()
        return carry

    lax.fori_loop(1, beads, start_p, 0)
    pall[0] = ptile[...]
    mass = jnp.concatenate(
        [
            jnp.broadcast_to(
                jnp.where(kind_row[:, h * LANES : (h + 1) * LANES] > 0.5, MASS_HYDROGEN, MASS_OXYGEN),
                (4, LANES),
            )
            for h in range(own_tabs)
        ],
        axis=0,
    )

    bead_wait(1, pall)
    q_p = sum(float(wqp[d]) * pall[d] for d in range(beads))
    p_p = sum(float(wqq[d]) * pall[d] for d in range(beads))
    new_q = q_q + q_p / mass
    new_p = p_p - mass * p_q
    for h in range(own_tabs):
        lanes = slice(h * LANES, (h + 1) * LANES)
        out_ref[0:3, 0, lanes] = new_q[4 * h : 4 * h + 3]
        out_ref[3:6, 0, lanes] = new_p[4 * h : 4 * h + 3]


def shards(
    positions,
    momenta,
    species,
    neighbours,
    counts,
    exports,
    embed,
    radial_one_in,
    radial_one_out,
    mix_one,
    radial_two_in,
    radial_two_out,
    readout,
    energy_w,
):
    beads = lax.axis_size("bead")
    domains = lax.axis_size("space")
    depth, atoms = neighbours.shape[1:]
    chans = embed.shape[1]
    nbasis, hidden = radial_one_in.shape
    tables = atoms // LANES + domains
    per = 4
    vmem = pltpu.VMEM
    scratch = [
        vmem((8, LANES), F32),
        vmem((beads, 8, LANES), F32),
        vmem((8, LANES), F32),
        vmem((beads, 8, LANES), F32),
        vmem((domains, 8, LANES), F32),
        vmem((tables, 8, LANES), F32),
        vmem((domains, chans, LANES), F32),
        vmem((tables, chans, LANES), F32),
        vmem((domains, chans, LANES), F32),
        vmem((domains, chans, LANES), F32),
        vmem((domains, 8, LANES), F32),
        vmem((domains, 8, LANES), F32),
        vmem((2, depth * 8, LANES), F32),
        vmem((2, depth * 8, LANES), F32),
        vmem((2, depth * 8, LANES), F32),
        vmem((4, depth, atoms), F32),
        vmem((3, 2, depth, LANES), F32),
        vmem((2, depth, LANES), F32),
        vmem((2, depth, LANES), jnp.int32),
        vmem((2, depth, LANES), jnp.int32),
        vmem((2, chans, LANES), F32),
        vmem((depth, 3 * chans, atoms), F32),
        vmem((depth, 3 * chans, atoms), F32),
        vmem((depth, 3 * chans, atoms), F32),
        vmem((depth, 3 * chans, atoms), F32),
        vmem((depth, 3 * chans, atoms), F32),
        vmem((depth, chans, atoms), F32),
        vmem((9, chans, atoms), F32),
        vmem((9, chans, atoms), F32),
        vmem((depth, LANES, atoms), BF16),
        vmem((atoms, domains * LANES), BF16),
        vmem((tables * 2 * chans, per * atoms), BF16),
        vmem((tables * 2 * chans, per * atoms), BF16),
        vmem((tables * 2 * chans, LANES), F32),
        vmem((48, per * atoms), BF16),
        vmem((48, LANES), F32),
        vmem((2, depth, LANES), F32),
        vmem((2, depth * 8, LANES), F32),
        vmem((3 * hidden, 2 * per * atoms), BF16),
        vmem((3 * hidden, 2 * per * atoms), BF16),
        pltpu.SemaphoreType.DMA((domains + 2,)),
        pltpu.SemaphoreType.DMA((domains + 2,)),
    ]
    whole = pl.BlockSpec(memory_space=pltpu.VMEM)
    moved = pl.pallas_call(
        functools.partial(kernel, beads, domains),
        out_shape=jax.ShapeDtypeStruct((6, 1, atoms), F32),
        in_specs=[whole] * 14,
        out_specs=whole,
        scratch_shapes=scratch,
        compiler_params=pltpu.CompilerParams(
            collective_id=0, has_side_effects=True, vmem_limit_bytes=56 * 1024 * 1024
        ),
    )(
        positions.transpose(1, 0, 2),
        momenta.transpose(1, 0, 2),
        species.reshape(1, atoms),
        neighbours[0],
        counts,
        exports[0, 0],
        embed,
        radial_one_in,
        radial_one_out,
        mix_one.T,
        radial_two_in,
        radial_two_out,
        readout.T,
        energy_w.reshape(1, hidden),
    )
    return moved[:3].transpose(1, 0, 2), moved[3:].transpose(1, 0, 2)


def solution(mesh):
    placed = (
        P("bead", None, "space"),
        P("bead", None, "space"),
        P("space"),
        P("bead", None, "space"),
        P("bead", "space"),
        P("bead", "space", None, None),
        P(),
        P(),
        P(),
        P(),
        P(),
        P(),
        P(),
        P(),
    )
    return jax.shard_map(
        shards,
        mesh=mesh,
        in_specs=placed,
        out_specs=(P("bead", None, "space"), P("bead", None, "space")),
        check_vma=False,
    )
```

```python
import functools
import math

import jax
import jax.numpy as jnp
import numpy as np
from jax import lax
from jax.experimental import pallas as pl
from jax.experimental.pallas import tpu as pltpu
from jax.sharding import PartitionSpec as P

RCUT = 6.0
CYCLE_FREQ = 1.5
MASS_OXYGEN = 15.999
MASS_HYDROGEN = 1.008
LANES = 128
F32 = jnp.float32
BF16 = jnp.bfloat16
MESH = pl.DeviceIdType.MESH
ROOT3 = math.sqrt(3.0)
ROOT5 = math.sqrt(5.0)
ROOT15 = math.sqrt(15.0)
DEGREE = (0, 1, 1, 1, 2, 2, 2, 2, 2)


def circulant_weights(beads):
    dt = beads / 3.0
    k = np.arange(beads)
    w = 2.0 * CYCLE_FREQ * np.sin(np.pi * k / beads)
    cosine = np.cos(w * dt)
    sine = np.sin(w * dt)
    reach = np.where(k == 0, dt, sine / np.where(k == 0, 1.0, w))
    stiff = w * sine
    d = np.arange(beads)
    waves = np.cos(2.0 * np.pi * d[:, None] * k[None, :] / beads) / beads
    return [(waves @ f).astype(np.float32) for f in (cosine, reach, stiff)]


def split(x):
    hi = x.astype(BF16)
    lo = (x - hi.astype(F32)).astype(BF16)
    return hi, lo


def rhs3(x):
    hi, lo = split(x)
    return jnp.concatenate([hi, lo, hi], axis=0)


def lhs3(w):
    hi = w.astype(BF16).astype(F32)
    lo = w - hi
    return jnp.concatenate([hi, hi, lo], axis=1).astype(BF16)


def mm(a, b):
    return jnp.dot(a, b, preferred_element_type=F32)


def mm_nt(a, b):
    return lax.dot_general(a, b, (((1,), (1,)), ((), ())), preferred_element_type=F32)


def lane_take(table, index):
    return jnp.take_along_axis(table, index, axis=1)


def silu_parts(x):
    sig = 0.5 * jnp.tanh(0.5 * x) + 0.5
    val = x * sig
    return val, sig + val * (1.0 - sig)


def rows_to_tile(parts, sub):
    low = sub < 4
    quads = []
    for j in range(4):
        a, b = parts[j], parts[j + 4]
        quads.append(jnp.where(low, a, b) + pltpu.roll(jnp.where(low, b, a), 4, 0))
    even2 = (sub & 2) == 0
    pairs = []
    for j in range(2):
        a, b = quads[j], quads[j + 2]
        pairs.append(jnp.where(even2, a + pltpu.roll(a, 6, 0), b + pltpu.roll(b, 2, 0)))
    even1 = (sub & 1) == 0
    a, b = pairs
    return jnp.where(even1, a + pltpu.roll(a, 7, 0), b + pltpu.roll(b, 1, 0))


def kernel(
    beads,
    domains,
    pos_ref,
    mom_ref,
    kind_ref,
    neigh_ref,
    count_ref,
    exp_ref,
    embed_ref,
    w1i_ref,
    w1o_ref,
    mix_ref,
    w2i_ref,
    w2o_ref,
    read_ref,
    ew_ref,
    out_ref,
    qtile,
    qall,
    ptile,
    pall,
    psend,
    slots,
    fsend,
    ftab,
    gsend,
    gback,
    xsend,
    xback,
    bas,
    dbas,
    ylm,
    geo,
    doff,
    kindd,
    lowd,
    tabd,
    embeds,
    rad1,
    rad1s,
    rad2,
    rad2s,
    wgrad,
    d_inv1,
    feat2,
    amp1,
    amp2,
    onehot,
    onehot_exp,
    lhs_a,
    lhs_b,
    acc_g,
    lhs_x,
    acc_x,
    r_grad,
    ylm_grad,
    act3a,
    act3b,
    send_sem,
    recv_sem,
):
    bead = lax.axis_index("bead")
    dom = lax.axis_index("space")
    depth, atoms = neigh_ref.shape
    chans = embed_ref.shape[1]
    tables = atoms // LANES + domains
    own_tabs = atoms // LANES
    norm = 1.0 / depth
    per = act3a.shape[1] // (2 * atoms)
    blocks = depth // per

    barrier = pltpu.get_barrier_semaphore()
    for d in range(1, domains):
        pl.semaphore_signal(
            barrier, inc=1, device_id=(bead, lax.rem(dom + d, domains)), device_id_type=MESH
        )

    def greet(d, carry):
        pl.semaphore_signal(
            barrier, inc=1, device_id=(lax.rem(bead + d, beads), dom), device_id_type=MESH
        )
        return carry

    lax.fori_loop(1, beads, greet, 0)

    def space_copy(stage, src, dst, peer):
        return pltpu.make_async_remote_copy(
            src_ref=src,
            dst_ref=dst,
            send_sem=send_sem.at[stage],
            recv_sem=recv_sem.at[stage],
            device_id=(bead, peer),
            device_id_type=MESH,
        )

    def space_start(stage, src, dst):
        for d in range(1, domains):
            peer = lax.rem(dom + d, domains)
            space_copy(stage, src.at[peer], dst.at[dom], peer).start()

    def space_wait(stage, src, dst):
        most = pl.ds(0, domains - 1)
        space_copy(stage, src.at[most], dst.at[most], lax.rem(dom + 1, domains)).wait()

    def bead_copy(stage, src, dst, d):
        return pltpu.make_async_remote_copy(
            src_ref=src,
            dst_ref=dst,
            send_sem=send_sem.at[domains + stage],
            recv_sem=recv_sem.at[domains + stage],
            device_id=(lax.rem(bead + d, beads), dom),
            device_id_type=MESH,
        )

    def bead_wait(stage, dst):
        most = pl.ds(1, beads - 1)
        bead_copy(stage, dst.at[most], dst.at[most], 1).wait()

    own = pos_ref[...].reshape(3, atoms)
    kind_row = kind_ref[...].astype(F32)
    zero_row = jnp.zeros((1, LANES), F32)
    for h in range(own_tabs):
        lanes = slice(h * LANES, (h + 1) * LANES)
        slots_h = jnp.concatenate(
            [own[:, lanes], kind_row[:, lanes], zero_row, zero_row, zero_row, zero_row], axis=0
        )
        slots[domains + h] = slots_h
        qtile[4 * h : 4 * h + 4] = slots_h[0:4]
    for t in range(domains):
        row = jnp.broadcast_to(exp_ref[t : t + 1, :], (8, LANES))
        low = row & (LANES - 1)
        picked = lane_take(slots[domains], low)
        for h in range(1, own_tabs):
            picked = jnp.where(
                (row >> 7) == h, lane_take(slots[domains + h], low), picked
            )
        psend[t] = picked

    w1i = w1i_ref[...]
    w1o = w1o_ref[...]
    w2i = w2i_ref[...]
    w2o = w2o_ref[...]
    nbasis, hidden = w1i.shape

    def in_lhs(w):
        wt = w.T
        hi = wt.astype(BF16).astype(F32)
        wide = jnp.concatenate([hi, hi, wt - hi], axis=1)
        none = jnp.zeros_like(wide)
        return jnp.concatenate(
            [jnp.concatenate([wide, none], axis=1), jnp.concatenate([none, wide], axis=1)], axis=0
        ).astype(BF16)

    f1i, f1o = in_lhs(w1i), lhs3(w1o.T)
    f2i, f2o = in_lhs(w2i), lhs3(w2o.T)
    mix_f, mix_b = lhs3(mix_ref[...]), lhs3(mix_ref[...].T)
    read_f, read_b = lhs3(read_ref[...]), lhs3(read_ref[...].T)
    embed_t = embed_ref[...].T
    for kind in range(2):
        embeds[kind] = jnp.broadcast_to(embed_t[:, kind : kind + 1], (chans, LANES))
    energy_t = ew_ref[...].T

    pl.semaphore_wait(barrier, domains - 1 + beads - 1)
    space_start(0, psend, slots)

    def start_q(d, carry):
        bead_copy(0, qtile, qall.at[d], d).start()
        return carry

    lax.fori_loop(1, beads, start_q, 0)
    qall[0] = qtile[...]

    slots[dom] = psend[dom]
    for t in range(domains):
        onehot_exp[:, t * LANES : (t + 1) * LANES] = (
            (lax.broadcasted_iota(jnp.int32, (atoms, LANES), 0) == exp_ref[t : t + 1, :])
            .astype(F32)
            .astype(BF16)
        )
    low_all = neigh_ref[...] & (LANES - 1)
    for h in range(own_tabs):
        lowd[h] = low_all[:, h * LANES : (h + 1) * LANES]
    slot_iota = lax.broadcasted_iota(jnp.int32, (LANES, atoms), 0).astype(F32).astype(BF16)

    def hot_step(k, carry):
        row = jnp.concatenate([lowd[h, pl.ds(k, 1), :] for h in range(own_tabs)], axis=1)
        row = row.astype(F32).astype(BF16)
        onehot[k] = jnp.where(slot_iota == row, jnp.ones_like(slot_iota), jnp.zeros_like(slot_iota))
        return carry

    lax.fori_loop(0, depth, hot_step, 0, unroll=4)
    space_wait(0, psend, slots)

    def table_of(index):
        t = index >> 7
        return jnp.where(t < own_tabs, t + domains, t - own_tabs)

    idx = neigh_ref[...]
    tab_all = table_of(idx)
    planes = []
    for comp in range(4):
        halves = []
        for h in range(own_tabs):
            lanes = slice(h * LANES, (h + 1) * LANES)
            low, tab = low_all[:, lanes], tab_all[:, lanes]
            out = None
            for t in range(tables):
                source = jnp.broadcast_to(slots[t, comp : comp + 1, :], (depth, LANES))
                got = lane_take(source, low)
                out = got if out is None else jnp.where(tab == t, got, out)
            halves.append(out)
        planes.append(jnp.concatenate(halves, axis=1))
    for h in range(own_tabs):
        lanes = slice(h * LANES, (h + 1) * LANES)
        kindd[h] = planes[3][:, lanes]
        tabd[h] = tab_all[:, lanes]

    def plane_row(ref, k, h):
        return ref[h, pl.ds(k, 1), :]

    def whole_row(ref, k):
        return jnp.concatenate([plane_row(ref, k, h) for h in range(own_tabs)], axis=1)


    def geometry():
        off = [planes[c] - own[c : c + 1, :] for c in range(3)]
        dist = jnp.sqrt(off[0] * off[0] + off[1] * off[1] + off[2] * off[2] + 1.0)
        inv = 1.0 / dist
        return [o * inv for o in off], dist, inv

    u, dist, inv = geometry()
    present = (
        lax.broadcasted_iota(jnp.int32, (depth, atoms), 0) < count_ref[...]
    ).astype(F32)
    scaled = jnp.minimum(dist * (1.0 / RCUT), 1.0)
    arg = math.pi * (scaled - 0.5)
    sq = arg * arg
    cos_y = 1.0
    for n in range(7, 0, -1):
        cos_y = 1.0 - cos_y * sq * (1.0 / ((2 * n - 1) * (2 * n)))
    sin_y = 1.0
    for n in range(6, 0, -1):
        sin_y = 1.0 - sin_y * sq * (1.0 / ((2 * n) * (2 * n + 1)))
    sin_y = sin_y * arg
    sines, cosines = {1: cos_y}, {1: -sin_y}
    for n in range(2, nbasis + 1):
        a, b = n // 2, n - n // 2
        sines[n] = sines[a] * cosines[b] + cosines[a] * sines[b]
        cosines[n] = cosines[a] * cosines[b] - sines[a] * sines[b]
    gap = 1.0 - scaled * scaled
    env = gap * gap * present * inv
    slope = -(4.0 / RCUT) * scaled * gap * present * inv - env * inv

    def strided_put(ref, j, plane):
        for h in range(own_tabs):
            ref[h, pl.ds(j, depth, stride=8), :] = plane[:, h * LANES : (h + 1) * LANES]

    def strided_get(ref, j):
        return jnp.concatenate(
            [ref[h, pl.ds(j, depth, stride=8), :] for h in range(own_tabs)], axis=1
        )

    def rows_get(ref, k):
        rows = pl.ds(pl.multiple_of(k * 8, 8), 8)
        return jnp.concatenate([ref[h, rows, :] for h in range(own_tabs)], axis=1)

    def rows_put(ref, k, value, add):
        rows = pl.ds(pl.multiple_of(k * 8, 8), 8)
        for h in range(own_tabs):
            part = value[:, h * LANES : (h + 1) * LANES]
            ref[h, rows, :] = ref[h, rows, :] + part if add else part

    for n in range(1, nbasis + 1):
        strided_put(bas, n - 1, sines[n] * env)
    ux, uy, uz = u
    harmonic = [
        ROOT3 * ux,
        ROOT3 * uy,
        ROOT3 * uz,
        ROOT15 * ux * uy,
        ROOT15 * uy * uz,
        ROOT15 * ux * uz,
        0.5 * ROOT15 * (ux * ux - uy * uy),
        0.5 * ROOT5 * (2.0 * uz * uz - ux * ux - uy * uy),
    ]
    for m in range(8):
        strided_put(ylm, m, harmonic[m])
    for n in range(1, nbasis + 1):
        strided_put(dbas, n - 1, (n * math.pi / RCUT) * cosines[n] * env + sines[n] * slope)
    for c in range(3):
        geo[c] = u[c]
    geo[3] = inv

    act3b[...] = jnp.zeros_like(act3b)

    def hi_lo_hi(x):
        hi = x.astype(BF16).astype(F32)
        return [hi, x - hi, hi]

    def radial_in(kb, w_in, act):
        xs = []
        for j in range(per):
            k = kb * per + j
            rows = hi_lo_hi(rows_get(bas, k)) + hi_lo_hi(rows_get(dbas, k))
            xs.append(jnp.concatenate(rows, axis=0).astype(BF16))
        for j in range(per):
            pre = mm(w_in, xs[j])
            val, steep = silu_parts(pre[:hidden])
            base = 2 * j * atoms
            act[:, base : base + atoms] = rhs3(val)
            act[:, base + atoms : base + 2 * atoms] = rhs3(steep * pre[hidden:])

    def radial_out(kb, w_out, act, rad, slopes, feature):
        for j in range(per):
            k = kb * per + j
            out = mm(w_out, act[:, 2 * j * atoms : 2 * (j + 1) * atoms])
            val, steep = out[:, :atoms], out[:, atoms:]
            if feature is not None:
                f = jnp.concatenate([feature(k, h) for h in range(own_tabs)], axis=1)
                f = jnp.concatenate([f, f, f], axis=0)
                val, steep = val * f, steep * f
            rad[k] = val
            slopes[k] = steep

    def radial_net(w_in, w_out, rad, slopes, feature):
        def step(p, carry):
            radial_out(jnp.maximum(2 * p - 1, 0), w_out, act3b, rad, slopes, feature)
            radial_in(2 * p, w_in, act3a)
            radial_out(2 * p, w_out, act3a, rad, slopes, feature)
            radial_in(2 * p + 1, w_in, act3b)
            return carry

        lax.fori_loop(0, blocks // 2, step, 0)
        radial_out(blocks - 1, w_out, act3b, rad, slopes, feature)

    group = 16

    def y_row(k, m, h):
        return ylm[h, pl.ds(k * 8 + m - 1, 1), :]

    def amplitudes(amp, rad, feature):
        invs = [[[None] * own_tabs for _ in range(chans // group)] for _ in range(3)]
        for h in range(own_tabs):
            lanes = slice(h * LANES, (h + 1) * LANES)
            for g in range(chans // group):

                def step(k, acc):
                    ws = [
                        rad[k, deg * chans + g * group : deg * chans + (g + 1) * group, lanes]
                        for deg in range(3)
                    ]
                    if feature is not None:
                        f = feature(k, g, h)
                        ws = [w * f for w in ws]
                    out = [acc[0] + ws[0]]
                    for m in range(1, 9):
                        out.append(acc[m] + ws[DEGREE[m]] * y_row(k, m, h))
                    return tuple(out)

                start = tuple(jnp.zeros((group, LANES), F32) for _ in range(9))
                acc = lax.fori_loop(0, depth, step, start, unroll=4)
                sums = [0.0, 0.0, 0.0]
                for m in range(9):
                    amp[m, g * group : (g + 1) * group, lanes] = acc[m]
                    sums[DEGREE[m]] = sums[DEGREE[m]] + acc[m] * acc[m]
                for deg in range(3):
                    invs[deg][g][h] = sums[deg] * norm
        rows = []
        for deg in range(3):
            for g in range(chans // group):
                rows.append(jnp.concatenate(invs[deg][g], axis=1))
        return jnp.concatenate(rows, axis=0)

    def scale_amp(amp, d_inv):
        for m in range(9):
            deg = DEGREE[m]
            amp[m] = amp[m] * d_inv[deg * chans : (deg + 1) * chans]

    def kind_feature(k, h):
        return jnp.where(plane_row(kindd, k, h) > 0.5, embeds[1], embeds[0])

    def slot_feature(k, g, h):
        return feat2[k, g * group : (g + 1) * group, h * LANES : (h + 1) * LANES]

    radial_net(f1i, f1o, rad1, rad1s, kind_feature)
    inv1 = amplitudes(amp1, rad1, None)
    act1, slope1 = silu_parts(mm(mix_f, rhs3(inv1)))
    own_embed = jnp.where(kind_row > 0.5, embed_t[:, 1:2], embed_t[:, 0:1])
    layer_one = own_embed + act1
    for h in range(own_tabs):
        ftab[domains + h] = layer_one[:, h * LANES : (h + 1) * LANES]
    for t in range(domains):
        row = jnp.broadcast_to(exp_ref[t : t + 1, :], (chans, LANES))
        low = row & (LANES - 1)
        picked = lane_take(ftab[domains], low)
        for h in range(1, own_tabs):
            picked = jnp.where((row >> 7) == h, lane_take(ftab[domains + h], low), picked)
        fsend[t] = picked
    space_start(1, fsend, ftab)
    ftab[dom] = fsend[dom]

    radial_net(f2i, f2o, rad2, rad2s, None)
    space_wait(1, fsend, ftab)

    def gather_step(k, carry):
        low_row = whole_row(lowd, k)
        tab_row = whole_row(tabd, k)
        for h in range(own_tabs):
            lanes = slice(h * LANES, (h + 1) * LANES)
            low = jnp.broadcast_to(low_row[:, lanes], (chans, LANES))
            out = lane_take(ftab[0], low)
            for t in range(1, tables):
                out = jnp.where(tab_row[:, lanes] == t, lane_take(ftab[t], low), out)
            feat2[k, :, lanes] = out
        return carry

    lax.fori_loop(0, depth, gather_step, 0, unroll=8)

    inv2 = amplitudes(amp2, rad2, slot_feature)
    unused, slope_r = silu_parts(mm(read_f, rhs3(inv2)))
    scale_amp(amp2, mm(read_b, rhs3(slope_r * energy_t)) * (2.0 * norm))

    sub = lax.broadcasted_iota(jnp.int32, (8, LANES), 0)

    def feature_pass(k):
        d_feats = []
        for h in range(own_tabs):
            lanes = slice(h * LANES, (h + 1) * LANES)
            total = None
            sums = [amp2[0, :, lanes], None, None]
            for m in range(1, 9):
                deg = DEGREE[m]
                term = amp2[m, :, lanes] * y_row(k, m, h)
                sums[deg] = term if sums[deg] is None else sums[deg] + term
            for deg in range(3):
                rows = slice(deg * chans, (deg + 1) * chans)
                if deg:
                    wgrad[k, rows, lanes] = sums[deg]
                part = sums[deg] * rad2[k, rows, lanes]
                total = part if total is None else total + part
            d_feats.append(total)
        return jnp.concatenate(d_feats, axis=1)

    def edge_pass(k, amp, rad, slopes, feature):
        d_ylms, d_rs = [], []
        for h in range(own_tabs):
            lanes = slice(h * LANES, (h + 1) * LANES)
            rads = [rad[k, deg * chans : (deg + 1) * chans, lanes] for deg in range(3)]
            steep = [slopes[k, deg * chans : (deg + 1) * chans, lanes] for deg in range(3)]
            ws = rads
            if feature is not None:
                f = jnp.concatenate([feature(k, g, h) for g in range(chans // group)], axis=0)
                ws = [r * f for r in rads]
            parts = []
            for m in range(1, 9):
                parts.append(fold(amp[m, :, lanes] * ws[DEGREE[m]]))
            d_ylms.append(rows_to_tile(parts, sub))
            by_r = None
            for deg in range(3):
                rows = slice(deg * chans, (deg + 1) * chans)
                if feature is None:
                    scale = d_inv1[rows, lanes]
                elif deg == 0:
                    scale = amp[0, :, lanes]
                else:
                    scale = wgrad[k, rows, lanes]
                by_r = scale * steep[deg] if by_r is None else by_r + scale * steep[deg]
            if feature is not None:
                by_r = by_r * f
            d_rs.append(fold(by_r))
        return jnp.concatenate(d_ylms, axis=1), d_rs

    def fold(x):
        return (x[0:8] + x[8:16]) + (x[16:24] + x[24:32])

    def distances_put(p, d_rs, add):
        rows = pl.ds(pl.multiple_of(p * 8, 8), 8)
        for h in range(own_tabs):
            tile = rows_to_tile([d[h] for d in d_rs], sub)
            r_grad[h, rows, :] = r_grad[h, rows, :] + tile if add else tile

    acc_g[...] = jnp.zeros_like(acc_g)
    lhs_b[...] = jnp.zeros_like(lhs_b)

    def second_features(kb, lhs):
        for j in range(per):
            k = kb * per + j
            hi, lo = split(feature_pass(k))
            both = jnp.concatenate([hi, lo], axis=0)
            tab_row = whole_row(tabd, k)
            for t in range(tables):
                hit = (tab_row == t).astype(F32).astype(BF16)
                lhs[t * 2 * chans : (t + 1) * 2 * chans, j * atoms : (j + 1) * atoms] = both * hit

    def scatter_block(kb, lhs):
        hot = jnp.concatenate([onehot[kb * per + j] for j in range(per)], axis=1)
        acc_g[...] += mm_nt(lhs[...], hot)

    def second_back(p, carry):
        scatter_block(jnp.maximum(2 * p - 1, 0), lhs_b)
        second_features(2 * p, lhs_a)
        scatter_block(2 * p, lhs_a)
        second_features(2 * p + 1, lhs_b)
        return carry

    lax.fori_loop(0, blocks // 2, second_back, 0)
    scatter_block(blocks - 1, lhs_b)

    def edges_step(amp, rad, slopes, feature, add):
        def step(p, carry):
            d_rs = []
            for j in range(8):
                k = p * 8 + j
                d_ylm, d_r_k = edge_pass(k, amp, rad, slopes, feature)
                rows_put(ylm_grad, k, d_ylm, add)
                d_rs.append(d_r_k)
            distances_put(p, d_rs, add)
            return carry

        lax.fori_loop(0, depth // 8, step, 0)

    def table_grad(t):
        base = t * 2 * chans
        return acc_g[base : base + chans, :] + acc_g[base + chans : base + 2 * chans, :]

    for t in range(domains):
        gsend[t] = table_grad(t)
    space_start(2, gsend, gback)
    gback[dom] = gsend[dom]
    edges_step(amp2, rad2, rad2s, slot_feature, False)

    def slope_step(k, carry):
        for h in range(own_tabs):
            lanes = slice(h * LANES, (h + 1) * LANES)
            sums = [amp1[0, :, lanes], None, None]
            for m in range(1, 9):
                deg = DEGREE[m]
                term = amp1[m, :, lanes] * y_row(k, m, h)
                sums[deg] = term if sums[deg] is None else sums[deg] + term
            for deg in range(3):
                rows = slice(deg * chans, (deg + 1) * chans)
                rad1s[k, rows, lanes] = rad1s[k, rows, lanes] * sums[deg]
        return carry

    lax.fori_loop(0, depth, slope_step, 0, unroll=4)
    own_grad = jnp.concatenate([table_grad(domains + h) for h in range(own_tabs)], axis=1)
    space_wait(2, gsend, gback)

    def to_owner(back):
        rows = back.shape[1]
        flat = jnp.concatenate([back[t] for t in range(domains)], axis=1)
        hi = flat.astype(BF16).astype(F32)
        both = jnp.concatenate([hi, flat - hi], axis=0).astype(BF16)
        out = mm_nt(both, onehot_exp[...])
        return out[:rows] + out[rows:]

    d_layer = own_grad + to_owner(gback)
    d_inv1[...] = mm(mix_b, rhs3(d_layer * slope1)) * (2.0 * norm)
    scale_amp(amp1, d_inv1[...])

    edges_step(amp1, rad1, rad1s, None, True)

    ux, uy, uz = geo[0], geo[1], geo[2]
    d_r = jnp.concatenate([r_grad[h] for h in range(own_tabs)], axis=1)
    dy = [strided_get(ylm_grad, m) for m in range(8)]
    dux = ROOT3 * dy[0] + ROOT15 * (uy * dy[3] + uz * dy[5] + ux * dy[6]) - ROOT5 * (ux * dy[7])
    duy = ROOT3 * dy[1] + ROOT15 * (ux * dy[3] + uz * dy[4] - uy * dy[6]) - ROOT5 * (uy * dy[7])
    duz = ROOT3 * dy[2] + ROOT15 * (uy * dy[4] + ux * dy[5]) + (2.0 * ROOT5) * (uz * dy[7])
    along = d_r - geo[3] * (ux * dux + uy * duy + uz * duz)
    d_off = [geo[3] * d + v * along for d, v in ((dux, ux), (duy, uy), (duz, uz))]
    centre = jnp.concatenate([jnp.sum(d, axis=0, keepdims=True) for d in d_off], axis=0)
    for c in range(3):
        for h in range(own_tabs):
            doff[c, h] = d_off[c][:, h * LANES : (h + 1) * LANES]

    acc_x[...] = jnp.zeros_like(acc_x)

    def force_step(kb, carry):
        for j in range(per):
            k = kb * per + j
            tab_row = whole_row(tabd, k)
            hit = tab_row == lax.broadcasted_iota(jnp.int32, (8, atoms), 0)
            rows = [jnp.where(hit, whole_row(doff.at[c], k), 0.0) for c in range(3)]
            full = jnp.concatenate(rows, axis=0)
            hi = full.astype(BF16).astype(F32)
            lhs_x[:, j * atoms : (j + 1) * atoms] = jnp.concatenate(
                [hi, full - hi], axis=0
            ).astype(BF16)
        hot = jnp.concatenate([onehot[kb * per + j] for j in range(per)], axis=1)
        acc_x[...] += mm_nt(lhs_x[...], hot)
        return carry

    lax.fori_loop(0, depth // per, force_step, 0)
    table_force = [acc_x[c * 8 : (c + 1) * 8, :] + acc_x[24 + c * 8 : 32 + c * 8, :] for c in range(3)]
    pad = jnp.zeros((5, LANES), F32)
    for t in range(domains):
        xsend[t] = jnp.concatenate([f[t : t + 1] for f in table_force] + [pad], axis=0)
    space_start(3, xsend, xback)
    xback[dom] = xsend[dom]
    own_force = jnp.concatenate(
        [
            jnp.concatenate([f[domains + h : domains + h + 1] for f in table_force], axis=0)
            for h in range(own_tabs)
        ],
        axis=1,
    )

    bead_wait(0, qall)
    half_step = 0.5 * beads / 3.0
    partial = mom_ref[...].reshape(3, atoms) - half_step * (own_force - centre)
    wqq, wqp, wpq = circulant_weights(beads)
    q_q = sum(float(wqq[d]) * qall[d] for d in range(beads))
    p_q = sum(float(wpq[d]) * qall[d] for d in range(beads))
    space_wait(3, xsend, xback)
    kicked = partial - half_step * to_owner(xback)[0:3]
    for h in range(own_tabs):
        ptile[4 * h : 4 * h + 3] = kicked[:, h * LANES : (h + 1) * LANES]
        ptile[4 * h + 3 : 4 * h + 4] = zero_row

    def start_p(d, carry):
        bead_copy(1, ptile, pall.at[d], d).start()
        return carry

    lax.fori_loop(1, beads, start_p, 0)
    pall[0] = ptile[...]
    mass = jnp.concatenate(
        [
            jnp.broadcast_to(
                jnp.where(kind_row[:, h * LANES : (h + 1) * LANES] > 0.5, MASS_HYDROGEN, MASS_OXYGEN),
                (4, LANES),
            )
            for h in range(own_tabs)
        ],
        axis=0,
    )

    bead_wait(1, pall)
    q_p = sum(float(wqp[d]) * pall[d] for d in range(beads))
    p_p = sum(float(wqq[d]) * pall[d] for d in range(beads))
    new_q = q_q + q_p / mass
    new_p = p_p - mass * p_q
    for h in range(own_tabs):
        lanes = slice(h * LANES, (h + 1) * LANES)
        out_ref[0:3, 0, lanes] = new_q[4 * h : 4 * h + 3]
        out_ref[3:6, 0, lanes] = new_p[4 * h : 4 * h + 3]


def shards(
    positions,
    momenta,
    species,
    neighbours,
    counts,
    exports,
    embed,
    radial_one_in,
    radial_one_out,
    mix_one,
    radial_two_in,
    radial_two_out,
    readout,
    energy_w,
):
    beads = lax.axis_size("bead")
    domains = lax.axis_size("space")
    depth, atoms = neighbours.shape[1:]
    chans = embed.shape[1]
    nbasis, hidden = radial_one_in.shape
    tables = atoms // LANES + domains
    per = 4
    vmem = pltpu.VMEM
    scratch = [
        vmem((8, LANES), F32),
        vmem((beads, 8, LANES), F32),
        vmem((8, LANES), F32),
        vmem((beads, 8, LANES), F32),
        vmem((domains, 8, LANES), F32),
        vmem((tables, 8, LANES), F32),
        vmem((domains, chans, LANES), F32),
        vmem((tables, chans, LANES), F32),
        vmem((domains, chans, LANES), F32),
        vmem((domains, chans, LANES), F32),
        vmem((domains, 8, LANES), F32),
        vmem((domains, 8, LANES), F32),
        vmem((2, depth * 8, LANES), F32),
        vmem((2, depth * 8, LANES), F32),
        vmem((2, depth * 8, LANES), F32),
        vmem((4, depth, atoms), F32),
        vmem((3, 2, depth, LANES), F32),
        vmem((2, depth, LANES), F32),
        vmem((2, depth, LANES), jnp.int32),
        vmem((2, depth, LANES), jnp.int32),
        vmem((2, chans, LANES), F32),
        vmem((depth, 3 * chans, atoms), F32),
        vmem((depth, 3 * chans, atoms), F32),
        vmem((depth, 3 * chans, atoms), F32),
        vmem((depth, 3 * chans, atoms), F32),
        vmem((depth, 3 * chans, atoms), F32),
        vmem((3 * chans, atoms), F32),
        vmem((depth, chans, atoms), F32),
        vmem((9, chans, atoms), F32),
        vmem((9, chans, atoms), F32),
        vmem((depth, LANES, atoms), BF16),
        vmem((atoms, domains * LANES), BF16),
        vmem((tables * 2 * chans, per * atoms), BF16),
        vmem((tables * 2 * chans, per * atoms), BF16),
        vmem((tables * 2 * chans, LANES), F32),
        vmem((48, per * atoms), BF16),
        vmem((48, LANES), F32),
        vmem((2, depth, LANES), F32),
        vmem((2, depth * 8, LANES), F32),
        vmem((3 * hidden, 2 * per * atoms), BF16),
        vmem((3 * hidden, 2 * per * atoms), BF16),
        pltpu.SemaphoreType.DMA((domains + 2,)),
        pltpu.SemaphoreType.DMA((domains + 2,)),
    ]
    whole = pl.BlockSpec(memory_space=pltpu.VMEM)
    moved = pl.pallas_call(
        functools.partial(kernel, beads, domains),
        out_shape=jax.ShapeDtypeStruct((6, 1, atoms), F32),
        in_specs=[whole] * 14,
        out_specs=whole,
        scratch_shapes=scratch,
        compiler_params=pltpu.CompilerParams(
            collective_id=0, has_side_effects=True, vmem_limit_bytes=56 * 1024 * 1024
        ),
    )(
        positions.transpose(1, 0, 2),
        momenta.transpose(1, 0, 2),
        species.reshape(1, atoms),
        neighbours[0],
        counts,
        exports[0, 0],
        embed,
        radial_one_in,
        radial_one_out,
        mix_one.T,
        radial_two_in,
        radial_two_out,
        readout.T,
        energy_w.reshape(1, hidden),
    )
    return moved[:3].transpose(1, 0, 2), moved[3:].transpose(1, 0, 2)


def solution(mesh):
    placed = (
        P("bead", None, "space"),
        P("bead", None, "space"),
        P("space"),
        P("bead", None, "space"),
        P("bead", "space"),
        P("bead", "space", None, None),
        P(),
        P(),
        P(),
        P(),
        P(),
        P(),
        P(),
        P(),
    )
    return jax.shard_map(
        shards,
        mesh=mesh,
        in_specs=placed,
        out_specs=(P("bead", None, "space"), P("bead", None, "space")),
        check_vma=False,
    )
```

```python
import functools
import math

import jax
import jax.numpy as jnp
import numpy as np
from jax import lax
from jax.experimental import pallas as pl
from jax.experimental.pallas import tpu as pltpu
from jax.sharding import PartitionSpec as P

RCUT = 6.0
CYCLE_FREQ = 1.5
MASS_OXYGEN = 15.999
MASS_HYDROGEN = 1.008
LANES = 128
F32 = jnp.float32
BF16 = jnp.bfloat16
MESH = pl.DeviceIdType.MESH
ROOT3 = math.sqrt(3.0)
ROOT5 = math.sqrt(5.0)
ROOT15 = math.sqrt(15.0)
DEGREE = (0, 1, 1, 1, 2, 2, 2, 2, 2)


def circulant_weights(beads):
    dt = beads / 3.0
    k = np.arange(beads)
    w = 2.0 * CYCLE_FREQ * np.sin(np.pi * k / beads)
    cosine = np.cos(w * dt)
    sine = np.sin(w * dt)
    reach = np.where(k == 0, dt, sine / np.where(k == 0, 1.0, w))
    stiff = w * sine
    d = np.arange(beads)
    waves = np.cos(2.0 * np.pi * d[:, None] * k[None, :] / beads) / beads
    return [(waves @ f).astype(np.float32) for f in (cosine, reach, stiff)]


def far_first(beads):
    def hops(d):
        return min(d // 8 % 4, 4 - d // 8 % 4) + min(d // 2 % 4, 4 - d // 2 % 4) + 0.5 * (d % 2)

    return sorted(range(1, beads), key=lambda d: (-hops(d), d))


def split(x):
    hi = x.astype(BF16)
    lo = (x - hi.astype(F32)).astype(BF16)
    return hi, lo


def rhs3(x):
    hi, lo = split(x)
    return jnp.concatenate([hi, lo, hi], axis=0)


def lhs3(w):
    hi = w.astype(BF16).astype(F32)
    lo = w - hi
    return jnp.concatenate([hi, hi, lo], axis=1).astype(BF16)


def mm(a, b):
    return jnp.dot(a, b, preferred_element_type=F32)


def mm_nt(a, b):
    return lax.dot_general(a, b, (((1,), (1,)), ((), ())), preferred_element_type=F32)


def lane_take(table, index):
    return jnp.take_along_axis(table, index, axis=1)


def silu_parts(x):
    sig = 0.5 * jnp.tanh(0.5 * x) + 0.5
    val = x * sig
    return val, sig + val * (1.0 - sig)


def rows_to_tile(parts, sub):
    low = sub < 4
    quads = []
    for j in range(4):
        a, b = parts[j], parts[j + 4]
        quads.append(jnp.where(low, a, b) + pltpu.roll(jnp.where(low, b, a), 4, 0))
    even2 = (sub & 2) == 0
    pairs = []
    for j in range(2):
        a, b = quads[j], quads[j + 2]
        pairs.append(jnp.where(even2, a + pltpu.roll(a, 6, 0), b + pltpu.roll(b, 2, 0)))
    even1 = (sub & 1) == 0
    a, b = pairs
    return jnp.where(even1, a + pltpu.roll(a, 7, 0), b + pltpu.roll(b, 1, 0))


def kernel(
    beads,
    domains,
    pos_ref,
    mom_ref,
    kind_ref,
    neigh_ref,
    count_ref,
    exp_ref,
    embed_ref,
    w1i_ref,
    w1o_ref,
    mix_ref,
    w2i_ref,
    w2o_ref,
    read_ref,
    ew_ref,
    out_ref,
    qtile,
    qall,
    ptile,
    pall,
    psend,
    slots,
    fsend,
    ftab,
    gsend,
    gback,
    xsend,
    xback,
    bas,
    dbas,
    ylm,
    geo,
    doff,
    kindd,
    lowd,
    tabd,
    embeds,
    rad1,
    rad1s,
    rad2,
    rad2s,
    wgrad,
    d_inv1,
    feat2,
    amp1,
    amp2,
    onehot,
    onehot_exp,
    lhs_a,
    lhs_b,
    acc_g,
    lhs_x,
    acc_x,
    r_grad,
    ylm_grad,
    act3a,
    act3b,
    send_sem,
    recv_sem,
):
    bead = lax.axis_index("bead")
    dom = lax.axis_index("space")
    depth, atoms = neigh_ref.shape
    chans = embed_ref.shape[1]
    tables = atoms // LANES + domains
    own_tabs = atoms // LANES
    norm = 1.0 / depth
    per = act3a.shape[1] // (2 * atoms)
    blocks = depth // per

    barrier = pltpu.get_barrier_semaphore()
    for d in range(1, domains):
        pl.semaphore_signal(
            barrier, inc=1, device_id=(bead, lax.rem(dom + d, domains)), device_id_type=MESH
        )

    def greet(d, carry):
        pl.semaphore_signal(
            barrier, inc=1, device_id=(lax.rem(bead + d, beads), dom), device_id_type=MESH
        )
        return carry

    lax.fori_loop(1, beads, greet, 0)

    def space_copy(stage, src, dst, peer):
        return pltpu.make_async_remote_copy(
            src_ref=src,
            dst_ref=dst,
            send_sem=send_sem.at[stage],
            recv_sem=recv_sem.at[stage],
            device_id=(bead, peer),
            device_id_type=MESH,
        )

    def space_start(stage, src, dst):
        for d in range(1, domains):
            peer = lax.rem(dom + d, domains)
            space_copy(stage, src.at[peer], dst.at[dom], peer).start()

    def space_wait(stage, src, dst):
        most = pl.ds(0, domains - 1)
        space_copy(stage, src.at[most], dst.at[most], lax.rem(dom + 1, domains)).wait()

    def bead_copy(stage, src, dst, d):
        return pltpu.make_async_remote_copy(
            src_ref=src,
            dst_ref=dst,
            send_sem=send_sem.at[domains + stage],
            recv_sem=recv_sem.at[domains + stage],
            device_id=(lax.rem(bead + d, beads), dom),
            device_id_type=MESH,
        )

    def bead_wait(stage, dst):
        most = pl.ds(1, beads - 1)
        bead_copy(stage, dst.at[most], dst.at[most], 1).wait()

    own = pos_ref[...].reshape(3, atoms)
    kind_row = kind_ref[...].astype(F32)
    zero_row = jnp.zeros((1, LANES), F32)
    for h in range(own_tabs):
        lanes = slice(h * LANES, (h + 1) * LANES)
        slots_h = jnp.concatenate(
            [own[:, lanes], kind_row[:, lanes], zero_row, zero_row, zero_row, zero_row], axis=0
        )
        slots[domains + h] = slots_h
        qtile[4 * h : 4 * h + 4] = slots_h[0:4]
    for t in range(domains):
        row = jnp.broadcast_to(exp_ref[t : t + 1, :], (8, LANES))
        low = row & (LANES - 1)
        picked = lane_take(slots[domains], low)
        for h in range(1, own_tabs):
            picked = jnp.where(
                (row >> 7) == h, lane_take(slots[domains + h], low), picked
            )
        psend[t] = picked

    w1i = w1i_ref[...]
    w1o = w1o_ref[...]
    w2i = w2i_ref[...]
    w2o = w2o_ref[...]
    nbasis, hidden = w1i.shape

    def in_lhs(w):
        wt = w.T
        hi = wt.astype(BF16).astype(F32)
        wide = jnp.concatenate([hi, hi, wt - hi], axis=1)
        none = jnp.zeros_like(wide)
        return jnp.concatenate(
            [jnp.concatenate([wide, none], axis=1), jnp.concatenate([none, wide], axis=1)], axis=0
        ).astype(BF16)

    f1i, f1o = in_lhs(w1i), lhs3(w1o.T)
    f2i, f2o = in_lhs(w2i), lhs3(w2o.T)
    mix_f, mix_b = lhs3(mix_ref[...]), lhs3(mix_ref[...].T)
    read_f, read_b = lhs3(read_ref[...]), lhs3(read_ref[...].T)
    embed_t = embed_ref[...].T
    for kind in range(2):
        embeds[kind] = jnp.broadcast_to(embed_t[:, kind : kind + 1], (chans, LANES))
    energy_t = ew_ref[...].T

    pl.semaphore_wait(barrier, domains - 1 + beads - 1)
    space_start(0, psend, slots)

    def start_q(d, carry):
        bead_copy(0, qtile, qall.at[d], d).start()
        return carry

    lax.fori_loop(1, beads, start_q, 0)
    qall[0] = qtile[...]

    slots[dom] = psend[dom]
    for t in range(domains):
        onehot_exp[:, t * LANES : (t + 1) * LANES] = (
            (lax.broadcasted_iota(jnp.int32, (atoms, LANES), 0) == exp_ref[t : t + 1, :])
            .astype(F32)
            .astype(BF16)
        )
    low_all = neigh_ref[...] & (LANES - 1)
    for h in range(own_tabs):
        lowd[h] = low_all[:, h * LANES : (h + 1) * LANES]
    slot_iota = lax.broadcasted_iota(jnp.int32, (LANES, atoms), 0).astype(F32).astype(BF16)

    def hot_step(k, carry):
        row = jnp.concatenate([lowd[h, pl.ds(k, 1), :] for h in range(own_tabs)], axis=1)
        row = row.astype(F32).astype(BF16)
        onehot[k] = jnp.where(slot_iota == row, jnp.ones_like(slot_iota), jnp.zeros_like(slot_iota))
        return carry

    lax.fori_loop(0, depth, hot_step, 0, unroll=4)
    space_wait(0, psend, slots)

    def table_of(index):
        t = index >> 7
        return jnp.where(t < own_tabs, t + domains, t - own_tabs)

    idx = neigh_ref[...]
    tab_all = table_of(idx)
    pieces = [[[] for _ in range(own_tabs)] for _ in range(4)]
    sources = [
        [jnp.broadcast_to(slots[t, comp : comp + 1, :], (8, LANES)) for t in range(tables)]
        for comp in range(4)
    ]
    for h in range(own_tabs):
        lanes = slice(h * LANES, (h + 1) * LANES)
        for r in range(0, depth, 8):
            low, tab = low_all[r : r + 8, lanes], tab_all[r : r + 8, lanes]
            for comp in range(4):
                out = lane_take(sources[comp][0], low)
                for t in range(1, tables):
                    out = jnp.where(tab == t, lane_take(sources[comp][t], low), out)
                pieces[comp][h].append(out)
    planes = [
        jnp.concatenate([jnp.concatenate(col, axis=0) for col in cols], axis=1) for cols in pieces
    ]
    for h in range(own_tabs):
        lanes = slice(h * LANES, (h + 1) * LANES)
        kindd[h] = planes[3][:, lanes]
        tabd[h] = tab_all[:, lanes]

    def plane_row(ref, k, h):
        return ref[h, pl.ds(k, 1), :]

    def whole_row(ref, k):
        return jnp.concatenate([plane_row(ref, k, h) for h in range(own_tabs)], axis=1)


    def geometry():
        off = [planes[c] - own[c : c + 1, :] for c in range(3)]
        dist = jnp.sqrt(off[0] * off[0] + off[1] * off[1] + off[2] * off[2] + 1.0)
        inv = 1.0 / dist
        return [o * inv for o in off], dist, inv

    u, dist, inv = geometry()
    present = (
        lax.broadcasted_iota(jnp.int32, (depth, atoms), 0) < count_ref[...]
    ).astype(F32)
    scaled = jnp.minimum(dist * (1.0 / RCUT), 1.0)
    arg = math.pi * (scaled - 0.5)
    sq = arg * arg
    cos_y = 1.0
    for n in range(7, 0, -1):
        cos_y = 1.0 - cos_y * sq * (1.0 / ((2 * n - 1) * (2 * n)))
    sin_y = 1.0
    for n in range(6, 0, -1):
        sin_y = 1.0 - sin_y * sq * (1.0 / ((2 * n) * (2 * n + 1)))
    sin_y = sin_y * arg
    sines, cosines = {1: cos_y}, {1: -sin_y}
    for n in range(2, nbasis + 1):
        a, b = n // 2, n - n // 2
        sines[n] = sines[a] * cosines[b] + cosines[a] * sines[b]
        cosines[n] = cosines[a] * cosines[b] - sines[a] * sines[b]
    gap = 1.0 - scaled * scaled
    env = gap * gap * present * inv
    slope = -(4.0 / RCUT) * scaled * gap * present * inv - env * inv

    def strided_put(ref, j, plane):
        for h in range(own_tabs):
            ref[h, pl.ds(j, depth, stride=8), :] = plane[:, h * LANES : (h + 1) * LANES]

    def strided_get(ref, j):
        return jnp.concatenate(
            [ref[h, pl.ds(j, depth, stride=8), :] for h in range(own_tabs)], axis=1
        )

    def rows_get(ref, k):
        rows = pl.ds(pl.multiple_of(k * 8, 8), 8)
        return jnp.concatenate([ref[h, rows, :] for h in range(own_tabs)], axis=1)

    def rows_put(ref, k, value, add):
        rows = pl.ds(pl.multiple_of(k * 8, 8), 8)
        for h in range(own_tabs):
            part = value[:, h * LANES : (h + 1) * LANES]
            ref[h, rows, :] = ref[h, rows, :] + part if add else part

    for n in range(1, nbasis + 1):
        strided_put(bas, n - 1, sines[n] * env)
    ux, uy, uz = u
    harmonic = [
        ROOT3 * ux,
        ROOT3 * uy,
        ROOT3 * uz,
        ROOT15 * ux * uy,
        ROOT15 * uy * uz,
        ROOT15 * ux * uz,
        0.5 * ROOT15 * (ux * ux - uy * uy),
        0.5 * ROOT5 * (2.0 * uz * uz - ux * ux - uy * uy),
    ]
    for m in range(8):
        strided_put(ylm, m, harmonic[m])
    for n in range(1, nbasis + 1):
        strided_put(dbas, n - 1, (n * math.pi / RCUT) * cosines[n] * env + sines[n] * slope)
    for c in range(3):
        geo[c] = u[c]
    geo[3] = inv

    group = 16

    def y_row(k, m, h):
        return ylm[h, pl.ds(k * 8 + m - 1, 1), :]

    def slot_feature(k, g, h):
        return feat2[k, g * group : (g + 1) * group, h * LANES : (h + 1) * LANES]

    def accumulate(amp, ks, rad, feature):
        for h in range(own_tabs):
            lanes = slice(h * LANES, (h + 1) * LANES)
            for g in range(chans // group):
                rows = slice(g * group, (g + 1) * group)
                acc = [amp[m, rows, lanes] for m in range(9)]
                for k in ks:
                    ws = [
                        rad[k, deg * chans + g * group : deg * chans + (g + 1) * group, lanes]
                        for deg in range(3)
                    ]
                    if feature is not None:
                        f = feature(k, g, h)
                        ws = [w * f for w in ws]
                    acc[0] = acc[0] + ws[0]
                    for m in range(1, 9):
                        acc[m] = acc[m] + ws[DEGREE[m]] * y_row(k, m, h)
                for m in range(9):
                    amp[m, rows, lanes] = acc[m]

    def invariants_of(amp):
        sums = [None, None, None]
        for m in range(9):
            square = amp[m] * amp[m]
            deg = DEGREE[m]
            sums[deg] = square if sums[deg] is None else sums[deg] + square
        return jnp.concatenate(sums, axis=0) * norm

    act3b[...] = jnp.zeros_like(act3b)
    amp1[...] = jnp.zeros_like(amp1)
    amp2[...] = jnp.zeros_like(amp2)

    def hi_lo_hi(x):
        hi = x.astype(BF16).astype(F32)
        return [hi, x - hi, hi]

    def radial_in(kb, w_in, act):
        xs = []
        for j in range(per):
            k = kb * per + j
            rows = hi_lo_hi(rows_get(bas, k)) + hi_lo_hi(rows_get(dbas, k))
            xs.append(jnp.concatenate(rows, axis=0).astype(BF16))
        for j in range(per):
            pre = mm(w_in, xs[j])
            val, steep = silu_parts(pre[:hidden])
            base = 2 * j * atoms
            act[:, base : base + atoms] = rhs3(val)
            act[:, base + atoms : base + 2 * atoms] = rhs3(steep * pre[hidden:])

    def radial_out(kb, w_out, act, rad, slopes, feature):
        for j in range(per):
            k = kb * per + j
            out = mm(w_out, act[:, 2 * j * atoms : 2 * (j + 1) * atoms])
            val, steep = out[:, :atoms], out[:, atoms:]
            if feature is not None:
                f = jnp.concatenate([feature(k, h) for h in range(own_tabs)], axis=1)
                f = jnp.concatenate([f, f, f], axis=0)
                val, steep = val * f, steep * f
            rad[k] = val
            slopes[k] = steep

    def radial_net(w_in, w_out, rad, slopes, feature, amp):
        def slots_of(kb):
            return [kb * per + j for j in range(per)]

        def step(p, carry):
            before = jnp.maximum(2 * p - 1, 0)
            radial_out(before, w_out, act3b, rad, slopes, feature)
            radial_in(2 * p, w_in, act3a)
            if amp is not None:
                accumulate(amp, slots_of(before), rad, None)
            radial_out(2 * p, w_out, act3a, rad, slopes, feature)
            radial_in(2 * p + 1, w_in, act3b)
            if amp is not None:
                accumulate(amp, slots_of(2 * p), rad, None)
            return carry

        lax.fori_loop(0, blocks // 2, step, 0)
        radial_out(blocks - 1, w_out, act3b, rad, slopes, feature)
        if amp is not None:
            accumulate(amp, slots_of(blocks - 1), rad, None)

    def scale_amp(amp, d_inv):
        for m in range(9):
            deg = DEGREE[m]
            amp[m] = amp[m] * d_inv[deg * chans : (deg + 1) * chans]

    def kind_feature(k, h):
        return jnp.where(plane_row(kindd, k, h) > 0.5, embeds[1], embeds[0])

    radial_net(f1i, f1o, rad1, rad1s, kind_feature, amp1)
    inv1 = invariants_of(amp1)
    act1, slope1 = silu_parts(mm(mix_f, rhs3(inv1)))
    own_embed = jnp.where(kind_row > 0.5, embed_t[:, 1:2], embed_t[:, 0:1])
    layer_one = own_embed + act1
    for h in range(own_tabs):
        ftab[domains + h] = layer_one[:, h * LANES : (h + 1) * LANES]
    for t in range(domains):
        row = jnp.broadcast_to(exp_ref[t : t + 1, :], (chans, LANES))
        low = row & (LANES - 1)
        picked = lane_take(ftab[domains], low)
        for h in range(1, own_tabs):
            picked = jnp.where((row >> 7) == h, lane_take(ftab[domains + h], low), picked)
        fsend[t] = picked
    space_start(1, fsend, ftab)
    ftab[dom] = fsend[dom]

    radial_net(f2i, f2o, rad2, rad2s, None, None)
    space_wait(1, fsend, ftab)

    many = 16

    def gather_step(kb, carry):
        ks = [kb * many + j for j in range(many)]
        for k in ks:
            low_row = whole_row(lowd, k)
            tab_row = whole_row(tabd, k)
            for h in range(own_tabs):
                lanes = slice(h * LANES, (h + 1) * LANES)
                low = jnp.broadcast_to(low_row[:, lanes], (chans, LANES))
                out = lane_take(ftab[0], low)
                for t in range(1, tables):
                    out = jnp.where(tab_row[:, lanes] == t, lane_take(ftab[t], low), out)
                feat2[k, :, lanes] = out
        accumulate(amp2, ks, rad2, slot_feature)
        return carry

    lax.fori_loop(0, depth // many, gather_step, 0)

    inv2 = invariants_of(amp2)
    unused, slope_r = silu_parts(mm(read_f, rhs3(inv2)))
    scale_amp(amp2, mm(read_b, rhs3(slope_r * energy_t)) * (2.0 * norm))

    sub = lax.broadcasted_iota(jnp.int32, (8, LANES), 0)

    def feature_pass(k):
        d_feats = []
        for h in range(own_tabs):
            lanes = slice(h * LANES, (h + 1) * LANES)
            total = None
            sums = [amp2[0, :, lanes], None, None]
            for m in range(1, 9):
                deg = DEGREE[m]
                term = amp2[m, :, lanes] * y_row(k, m, h)
                sums[deg] = term if sums[deg] is None else sums[deg] + term
            for deg in range(3):
                rows = slice(deg * chans, (deg + 1) * chans)
                if deg:
                    wgrad[k, rows, lanes] = sums[deg]
                part = sums[deg] * rad2[k, rows, lanes]
                total = part if total is None else total + part
            d_feats.append(total)
        return jnp.concatenate(d_feats, axis=1)

    def edge_pass(k, amp, rad, slopes, feature):
        d_ylms, d_rs = [], []
        for h in range(own_tabs):
            lanes = slice(h * LANES, (h + 1) * LANES)
            rads = [rad[k, deg * chans : (deg + 1) * chans, lanes] for deg in range(3)]
            steep = [slopes[k, deg * chans : (deg + 1) * chans, lanes] for deg in range(3)]
            ws = rads
            if feature is not None:
                f = jnp.concatenate([feature(k, g, h) for g in range(chans // group)], axis=0)
                ws = [r * f for r in rads]
            parts = []
            for m in range(1, 9):
                parts.append(fold(amp[m, :, lanes] * ws[DEGREE[m]]))
            d_ylms.append(rows_to_tile(parts, sub))
            by_r = None
            for deg in range(3):
                rows = slice(deg * chans, (deg + 1) * chans)
                if feature is None:
                    scale = d_inv1[rows, lanes]
                elif deg == 0:
                    scale = amp[0, :, lanes]
                else:
                    scale = wgrad[k, rows, lanes]
                by_r = scale * steep[deg] if by_r is None else by_r + scale * steep[deg]
            if feature is not None:
                by_r = by_r * f
            d_rs.append(fold(by_r))
        return jnp.concatenate(d_ylms, axis=1), d_rs

    def fold(x):
        return (x[0:8] + x[8:16]) + (x[16:24] + x[24:32])

    def distances_put(p, d_rs, add):
        rows = pl.ds(pl.multiple_of(p * 8, 8), 8)
        for h in range(own_tabs):
            tile = rows_to_tile([d[h] for d in d_rs], sub)
            r_grad[h, rows, :] = r_grad[h, rows, :] + tile if add else tile

    acc_g[...] = jnp.zeros_like(acc_g)
    lhs_b[...] = jnp.zeros_like(lhs_b)

    def second_features(kb, lhs):
        for j in range(per):
            k = kb * per + j
            hi, lo = split(feature_pass(k))
            both = jnp.concatenate([hi, lo], axis=0)
            tab_row = whole_row(tabd, k)
            for t in range(tables):
                hit = (tab_row == t).astype(F32).astype(BF16)
                lhs[t * 2 * chans : (t + 1) * 2 * chans, j * atoms : (j + 1) * atoms] = both * hit

    def scatter_block(kb, lhs):
        hot = jnp.concatenate([onehot[kb * per + j] for j in range(per)], axis=1)
        acc_g[...] += mm_nt(lhs[...], hot)

    def second_back(p, carry):
        scatter_block(jnp.maximum(2 * p - 1, 0), lhs_b)
        second_features(2 * p, lhs_a)
        scatter_block(2 * p, lhs_a)
        second_features(2 * p + 1, lhs_b)
        return carry

    lax.fori_loop(0, blocks // 2, second_back, 0)
    scatter_block(blocks - 1, lhs_b)

    def edges_step(amp, rad, slopes, feature, add):
        def step(p, carry):
            d_rs = []
            for j in range(8):
                k = p * 8 + j
                d_ylm, d_r_k = edge_pass(k, amp, rad, slopes, feature)
                rows_put(ylm_grad, k, d_ylm, add)
                d_rs.append(d_r_k)
            distances_put(p, d_rs, add)
            return carry

        lax.fori_loop(0, depth // 8, step, 0)

    def table_grad(t):
        base = t * 2 * chans
        return acc_g[base : base + chans, :] + acc_g[base + chans : base + 2 * chans, :]

    for t in range(domains):
        gsend[t] = table_grad(t)
    space_start(2, gsend, gback)
    gback[dom] = gsend[dom]
    edges_step(amp2, rad2, rad2s, slot_feature, False)

    def slope_step(k, carry):
        for h in range(own_tabs):
            lanes = slice(h * LANES, (h + 1) * LANES)
            sums = [amp1[0, :, lanes], None, None]
            for m in range(1, 9):
                deg = DEGREE[m]
                term = amp1[m, :, lanes] * y_row(k, m, h)
                sums[deg] = term if sums[deg] is None else sums[deg] + term
            for deg in range(3):
                rows = slice(deg * chans, (deg + 1) * chans)
                rad1s[k, rows, lanes] = rad1s[k, rows, lanes] * sums[deg]
        return carry

    lax.fori_loop(0, depth, slope_step, 0, unroll=4)
    own_grad = jnp.concatenate([table_grad(domains + h) for h in range(own_tabs)], axis=1)
    space_wait(2, gsend, gback)

    def to_owner(back):
        rows = back.shape[1]
        flat = jnp.concatenate([back[t] for t in range(domains)], axis=1)
        hi = flat.astype(BF16).astype(F32)
        both = jnp.concatenate([hi, flat - hi], axis=0).astype(BF16)
        out = mm_nt(both, onehot_exp[...])
        return out[:rows] + out[rows:]

    d_layer = own_grad + to_owner(gback)
    d_inv1[...] = mm(mix_b, rhs3(d_layer * slope1)) * (2.0 * norm)
    scale_amp(amp1, d_inv1[...])

    edges_step(amp1, rad1, rad1s, None, True)

    ux, uy, uz = geo[0], geo[1], geo[2]
    d_r = jnp.concatenate([r_grad[h] for h in range(own_tabs)], axis=1)
    dy = [strided_get(ylm_grad, m) for m in range(8)]
    dux = ROOT3 * dy[0] + ROOT15 * (uy * dy[3] + uz * dy[5] + ux * dy[6]) - ROOT5 * (ux * dy[7])
    duy = ROOT3 * dy[1] + ROOT15 * (ux * dy[3] + uz * dy[4] - uy * dy[6]) - ROOT5 * (uy * dy[7])
    duz = ROOT3 * dy[2] + ROOT15 * (uy * dy[4] + ux * dy[5]) + (2.0 * ROOT5) * (uz * dy[7])
    along = d_r - geo[3] * (ux * dux + uy * duy + uz * duz)
    d_off = [geo[3] * d + v * along for d, v in ((dux, ux), (duy, uy), (duz, uz))]
    centre = jnp.concatenate([jnp.sum(d, axis=0, keepdims=True) for d in d_off], axis=0)
    for c in range(3):
        for h in range(own_tabs):
            doff[c, h] = d_off[c][:, h * LANES : (h + 1) * LANES]

    acc_x[...] = jnp.zeros_like(acc_x)

    def force_rows(k, carry):
        tab_row = whole_row(tabd, k)
        hit = tab_row == lax.broadcasted_iota(jnp.int32, (8, atoms), 0)
        rows = [jnp.where(hit, whole_row(doff.at[c], k), 0.0) for c in range(3)]
        full = jnp.concatenate(rows, axis=0)
        hi = full.astype(BF16).astype(F32)
        lhs_x[k] = jnp.concatenate([hi, full - hi], axis=0).astype(BF16)
        return carry

    lax.fori_loop(0, depth, force_rows, 0, unroll=4)
    long = 48

    def force_step(kb, carry):
        ks = [kb * long + j for j in range(long)]
        left = jnp.concatenate([lhs_x[k] for k in ks], axis=1)
        hot = jnp.concatenate([onehot[k] for k in ks], axis=1)
        acc_x[...] += mm_nt(left, hot)
        return carry

    lax.fori_loop(0, depth // long, force_step, 0)
    table_force = [acc_x[c * 8 : (c + 1) * 8, :] + acc_x[24 + c * 8 : 32 + c * 8, :] for c in range(3)]
    pad = jnp.zeros((5, LANES), F32)
    for t in range(domains):
        xsend[t] = jnp.concatenate([f[t : t + 1] for f in table_force] + [pad], axis=0)
    space_start(3, xsend, xback)
    xback[dom] = xsend[dom]
    own_force = jnp.concatenate(
        [
            jnp.concatenate([f[domains + h : domains + h + 1] for f in table_force], axis=0)
            for h in range(own_tabs)
        ],
        axis=1,
    )

    bead_wait(0, qall)
    half_step = 0.5 * beads / 3.0
    partial = mom_ref[...].reshape(3, atoms) - half_step * (own_force - centre)
    wqq, wqp, wpq = circulant_weights(beads)
    q_q = sum(float(wqq[d]) * qall[d] for d in range(beads))
    p_q = sum(float(wpq[d]) * qall[d] for d in range(beads))
    space_wait(3, xsend, xback)
    kicked = partial - half_step * to_owner(xback)[0:3]
    for h in range(own_tabs):
        ptile[4 * h : 4 * h + 3] = kicked[:, h * LANES : (h + 1) * LANES]
        ptile[4 * h + 3 : 4 * h + 4] = zero_row

    for d in far_first(beads):
        bead_copy(1, ptile, pall.at[d], d).start()
    pall[0] = ptile[...]
    mass = jnp.concatenate(
        [
            jnp.broadcast_to(
                jnp.where(kind_row[:, h * LANES : (h + 1) * LANES] > 0.5, MASS_HYDROGEN, MASS_OXYGEN),
                (4, LANES),
            )
            for h in range(own_tabs)
        ],
        axis=0,
    )

    bead_wait(1, pall)
    q_p = sum(float(wqp[d]) * pall[d] for d in range(beads))
    p_p = sum(float(wqq[d]) * pall[d] for d in range(beads))
    new_q = q_q + q_p / mass
    new_p = p_p - mass * p_q
    for h in range(own_tabs):
        lanes = slice(h * LANES, (h + 1) * LANES)
        out_ref[0:3, 0, lanes] = new_q[4 * h : 4 * h + 3]
        out_ref[3:6, 0, lanes] = new_p[4 * h : 4 * h + 3]


def shards(
    positions,
    momenta,
    species,
    neighbours,
    counts,
    exports,
    embed,
    radial_one_in,
    radial_one_out,
    mix_one,
    radial_two_in,
    radial_two_out,
    readout,
    energy_w,
):
    beads = lax.axis_size("bead")
    domains = lax.axis_size("space")
    depth, atoms = neighbours.shape[1:]
    chans = embed.shape[1]
    nbasis, hidden = radial_one_in.shape
    tables = atoms // LANES + domains
    per = 4
    vmem = pltpu.VMEM
    scratch = [
        vmem((8, LANES), F32),
        vmem((beads, 8, LANES), F32),
        vmem((8, LANES), F32),
        vmem((beads, 8, LANES), F32),
        vmem((domains, 8, LANES), F32),
        vmem((tables, 8, LANES), F32),
        vmem((domains, chans, LANES), F32),
        vmem((tables, chans, LANES), F32),
        vmem((domains, chans, LANES), F32),
        vmem((domains, chans, LANES), F32),
        vmem((domains, 8, LANES), F32),
        vmem((domains, 8, LANES), F32),
        vmem((2, depth * 8, LANES), F32),
        vmem((2, depth * 8, LANES), F32),
        vmem((2, depth * 8, LANES), F32),
        vmem((4, depth, atoms), F32),
        vmem((3, 2, depth, LANES), F32),
        vmem((2, depth, LANES), F32),
        vmem((2, depth, LANES), jnp.int32),
        vmem((2, depth, LANES), jnp.int32),
        vmem((2, chans, LANES), F32),
        vmem((depth, 3 * chans, atoms), F32),
        vmem((depth, 3 * chans, atoms), F32),
        vmem((depth, 3 * chans, atoms), F32),
        vmem((depth, 3 * chans, atoms), F32),
        vmem((depth, 3 * chans, atoms), F32),
        vmem((3 * chans, atoms), F32),
        vmem((depth, chans, atoms), F32),
        vmem((9, chans, atoms), F32),
        vmem((9, chans, atoms), F32),
        vmem((depth, LANES, atoms), BF16),
        vmem((atoms, domains * LANES), BF16),
        vmem((tables * 2 * chans, per * atoms), BF16),
        vmem((tables * 2 * chans, per * atoms), BF16),
        vmem((tables * 2 * chans, LANES), F32),
        vmem((depth, 48, atoms), BF16),
        vmem((48, LANES), F32),
        vmem((2, depth, LANES), F32),
        vmem((2, depth * 8, LANES), F32),
        vmem((3 * hidden, 2 * per * atoms), BF16),
        vmem((3 * hidden, 2 * per * atoms), BF16),
        pltpu.SemaphoreType.DMA((domains + 2,)),
        pltpu.SemaphoreType.DMA((domains + 2,)),
    ]
    whole = pl.BlockSpec(memory_space=pltpu.VMEM)
    moved = pl.pallas_call(
        functools.partial(kernel, beads, domains),
        out_shape=jax.ShapeDtypeStruct((6, 1, atoms), F32),
        in_specs=[whole] * 14,
        out_specs=whole,
        scratch_shapes=scratch,
        compiler_params=pltpu.CompilerParams(
            collective_id=0, has_side_effects=True, vmem_limit_bytes=56 * 1024 * 1024
        ),
    )(
        positions.transpose(1, 0, 2),
        momenta.transpose(1, 0, 2),
        species.reshape(1, atoms),
        neighbours[0],
        counts,
        exports[0, 0],
        embed,
        radial_one_in,
        radial_one_out,
        mix_one.T,
        radial_two_in,
        radial_two_out,
        readout.T,
        energy_w.reshape(1, hidden),
    )
    return moved[:3].transpose(1, 0, 2), moved[3:].transpose(1, 0, 2)


def solution(mesh):
    placed = (
        P("bead", None, "space"),
        P("bead", None, "space"),
        P("space"),
        P("bead", None, "space"),
        P("bead", "space"),
        P("bead", "space", None, None),
        P(),
        P(),
        P(),
        P(),
        P(),
        P(),
        P(),
        P(),
    )
    return jax.shard_map(
        shards,
        mesh=mesh,
        in_specs=placed,
        out_specs=(P("bead", None, "space"), P("bead", None, "space")),
        check_vma=False,
    )
```

```python
import functools
import math

import jax
import jax.numpy as jnp
import numpy as np
from jax import lax
from jax.experimental import pallas as pl
from jax.experimental.pallas import tpu as pltpu
from jax.sharding import PartitionSpec as P

RCUT = 6.0
CYCLE_FREQ = 1.5
MASS_OXYGEN = 15.999
MASS_HYDROGEN = 1.008
LANES = 128
F32 = jnp.float32
BF16 = jnp.bfloat16
MESH = pl.DeviceIdType.MESH
ROOT3 = math.sqrt(3.0)
ROOT5 = math.sqrt(5.0)
ROOT15 = math.sqrt(15.0)
DEGREE = (0, 1, 1, 1, 2, 2, 2, 2, 2)


def circulant_weights(beads):
    dt = beads / 3.0
    k = np.arange(beads)
    w = 2.0 * CYCLE_FREQ * np.sin(np.pi * k / beads)
    cosine = np.cos(w * dt)
    sine = np.sin(w * dt)
    reach = np.where(k == 0, dt, sine / np.where(k == 0, 1.0, w))
    stiff = w * sine
    d = np.arange(beads)
    waves = np.cos(2.0 * np.pi * d[:, None] * k[None, :] / beads) / beads
    return [(waves @ f).astype(np.float32) for f in (cosine, reach, stiff)]


def far_first(beads):
    def hops(d):
        return min(d // 8 % 4, 4 - d // 8 % 4) + min(d // 2 % 4, 4 - d // 2 % 4) + 0.5 * (d % 2)

    return sorted(range(1, beads), key=lambda d: (-hops(d), d))


def split(x):
    hi = x.astype(BF16)
    lo = (x - hi.astype(F32)).astype(BF16)
    return hi, lo


def rhs3(x):
    hi, lo = split(x)
    return jnp.concatenate([hi, lo, hi], axis=0)


def lhs3(w):
    hi = w.astype(BF16).astype(F32)
    lo = w - hi
    return jnp.concatenate([hi, hi, lo], axis=1).astype(BF16)


def mm(a, b):
    return jnp.dot(a, b, preferred_element_type=F32)


def mm_nt(a, b):
    return lax.dot_general(a, b, (((1,), (1,)), ((), ())), preferred_element_type=F32)


def lane_take(table, index):
    return jnp.take_along_axis(table, index, axis=1)


def silu_parts(x):
    sig = 0.5 * jnp.tanh(0.5 * x) + 0.5
    val = x * sig
    return val, sig + val * (1.0 - sig)


def rows_to_tile(parts, sub):
    low = sub < 4
    quads = []
    for j in range(4):
        a, b = parts[j], parts[j + 4]
        quads.append(jnp.where(low, a, b) + pltpu.roll(jnp.where(low, b, a), 4, 0))
    even2 = (sub & 2) == 0
    pairs = []
    for j in range(2):
        a, b = quads[j], quads[j + 2]
        pairs.append(jnp.where(even2, a + pltpu.roll(a, 6, 0), b + pltpu.roll(b, 2, 0)))
    even1 = (sub & 1) == 0
    a, b = pairs
    return jnp.where(even1, a + pltpu.roll(a, 7, 0), b + pltpu.roll(b, 1, 0))


def kernel(
    beads,
    domains,
    pos_ref,
    mom_ref,
    kind_ref,
    neigh_ref,
    count_ref,
    exp_ref,
    embed_ref,
    w1i_ref,
    w1o_ref,
    mix_ref,
    w2i_ref,
    w2o_ref,
    read_ref,
    ew_ref,
    out_ref,
    qtile,
    qall,
    ptile,
    pall,
    psend,
    slots,
    fsend,
    ftab,
    gsend,
    gback,
    xsend,
    xback,
    bas,
    dbas,
    ylm,
    geo,
    doff,
    kindd,
    lowd,
    tabd,
    embeds,
    rad1,
    rad1s,
    rad2,
    later1,
    later2,
    wgrad,
    d_inv1,
    feat2,
    amp1,
    amp2,
    onehot,
    onehot_exp,
    lhs_a,
    lhs_b,
    acc_g,
    lhs_x,
    acc_x,
    r_grad,
    ylm_grad,
    act3a,
    act3b,
    send_sem,
    recv_sem,
):
    bead = lax.axis_index("bead")
    dom = lax.axis_index("space")
    depth, atoms = neigh_ref.shape
    chans = embed_ref.shape[1]
    tables = atoms // LANES + domains
    own_tabs = atoms // LANES
    norm = 1.0 / depth
    per = act3a.shape[1] // atoms
    blocks = depth // per

    barrier = pltpu.get_barrier_semaphore()
    for d in range(1, domains):
        pl.semaphore_signal(
            barrier, inc=1, device_id=(bead, lax.rem(dom + d, domains)), device_id_type=MESH
        )

    def greet(d, carry):
        pl.semaphore_signal(
            barrier, inc=1, device_id=(lax.rem(bead + d, beads), dom), device_id_type=MESH
        )
        return carry

    lax.fori_loop(1, beads, greet, 0)

    def space_copy(stage, src, dst, peer):
        return pltpu.make_async_remote_copy(
            src_ref=src,
            dst_ref=dst,
            send_sem=send_sem.at[stage],
            recv_sem=recv_sem.at[stage],
            device_id=(bead, peer),
            device_id_type=MESH,
        )

    def space_start(stage, src, dst):
        for d in range(1, domains):
            peer = lax.rem(dom + d, domains)
            space_copy(stage, src.at[peer], dst.at[dom], peer).start()

    def space_wait(stage, src, dst):
        most = pl.ds(0, domains - 1)
        space_copy(stage, src.at[most], dst.at[most], lax.rem(dom + 1, domains)).wait()

    def bead_copy(stage, src, dst, d):
        return pltpu.make_async_remote_copy(
            src_ref=src,
            dst_ref=dst,
            send_sem=send_sem.at[domains + stage],
            recv_sem=recv_sem.at[domains + stage],
            device_id=(lax.rem(bead + d, beads), dom),
            device_id_type=MESH,
        )

    def bead_wait(stage, dst):
        most = pl.ds(1, beads - 1)
        bead_copy(stage, dst.at[most], dst.at[most], 1).wait()

    own = pos_ref[...].reshape(3, atoms)
    kind_row = kind_ref[...].astype(F32)
    zero_row = jnp.zeros((1, LANES), F32)
    for h in range(own_tabs):
        lanes = slice(h * LANES, (h + 1) * LANES)
        slots_h = jnp.concatenate(
            [own[:, lanes], kind_row[:, lanes], zero_row, zero_row, zero_row, zero_row], axis=0
        )
        slots[domains + h] = slots_h
        qtile[4 * h : 4 * h + 4] = slots_h[0:4]
    for t in range(domains):
        row = jnp.broadcast_to(exp_ref[t : t + 1, :], (8, LANES))
        low = row & (LANES - 1)
        picked = lane_take(slots[domains], low)
        for h in range(1, own_tabs):
            picked = jnp.where(
                (row >> 7) == h, lane_take(slots[domains + h], low), picked
            )
        psend[t] = picked

    w1i = w1i_ref[...]
    w1o = w1o_ref[...]
    w2i = w2i_ref[...]
    w2o = w2o_ref[...]
    nbasis, hidden = w1i.shape

    def in_lhs(w):
        wt = w.T
        hi = wt.astype(BF16).astype(F32)
        wide = jnp.concatenate([hi, hi, wt - hi], axis=1)
        none = jnp.zeros_like(wide)
        return jnp.concatenate(
            [jnp.concatenate([wide, none], axis=1), jnp.concatenate([none, wide], axis=1)], axis=0
        ).astype(BF16)

    f1i, f1o = in_lhs(w1i), lhs3(w1o.T)
    f2i, f2o = in_lhs(w2i), lhs3(w2o.T)
    mix_f, mix_b = lhs3(mix_ref[...]), lhs3(mix_ref[...].T)
    read_f, read_b = lhs3(read_ref[...]), lhs3(read_ref[...].T)
    embed_t = embed_ref[...].T
    for kind in range(2):
        embeds[kind] = jnp.broadcast_to(embed_t[:, kind : kind + 1], (chans, LANES))
    energy_t = ew_ref[...].T

    pl.semaphore_wait(barrier, domains - 1 + beads - 1)
    space_start(0, psend, slots)

    def start_q(d, carry):
        bead_copy(0, qtile, qall.at[d], d).start()
        return carry

    lax.fori_loop(1, beads, start_q, 0)
    qall[0] = qtile[...]

    slots[dom] = psend[dom]
    for t in range(domains):
        onehot_exp[:, t * LANES : (t + 1) * LANES] = (
            (lax.broadcasted_iota(jnp.int32, (atoms, LANES), 0) == exp_ref[t : t + 1, :])
            .astype(F32)
            .astype(BF16)
        )
    low_all = neigh_ref[...] & (LANES - 1)
    for h in range(own_tabs):
        lowd[h] = low_all[:, h * LANES : (h + 1) * LANES]
    slot_iota = lax.broadcasted_iota(jnp.int32, (LANES, atoms), 0).astype(F32).astype(BF16)

    def hot_step(k, carry):
        row = jnp.concatenate([lowd[h, pl.ds(k, 1), :] for h in range(own_tabs)], axis=1)
        row = row.astype(F32).astype(BF16)
        onehot[k] = jnp.where(slot_iota == row, jnp.ones_like(slot_iota), jnp.zeros_like(slot_iota))
        return carry

    lax.fori_loop(0, depth, hot_step, 0, unroll=4)
    space_wait(0, psend, slots)

    def table_of(index):
        t = index >> 7
        return jnp.where(t < own_tabs, t + domains, t - own_tabs)

    idx = neigh_ref[...]
    tab_all = table_of(idx)
    pieces = [[[] for _ in range(own_tabs)] for _ in range(4)]
    sources = [
        [jnp.broadcast_to(slots[t, comp : comp + 1, :], (8, LANES)) for t in range(tables)]
        for comp in range(4)
    ]
    for h in range(own_tabs):
        lanes = slice(h * LANES, (h + 1) * LANES)
        for r in range(0, depth, 8):
            low, tab = low_all[r : r + 8, lanes], tab_all[r : r + 8, lanes]
            for comp in range(4):
                out = lane_take(sources[comp][0], low)
                for t in range(1, tables):
                    out = jnp.where(tab == t, lane_take(sources[comp][t], low), out)
                pieces[comp][h].append(out)
    planes = [
        jnp.concatenate([jnp.concatenate(col, axis=0) for col in cols], axis=1) for cols in pieces
    ]
    for h in range(own_tabs):
        lanes = slice(h * LANES, (h + 1) * LANES)
        kindd[h] = planes[3][:, lanes]
        tabd[h] = tab_all[:, lanes]

    def plane_row(ref, k, h):
        return ref[h, pl.ds(k, 1), :]

    def whole_row(ref, k):
        return jnp.concatenate([plane_row(ref, k, h) for h in range(own_tabs)], axis=1)


    def geometry():
        off = [planes[c] - own[c : c + 1, :] for c in range(3)]
        dist = jnp.sqrt(off[0] * off[0] + off[1] * off[1] + off[2] * off[2] + 1.0)
        inv = 1.0 / dist
        return [o * inv for o in off], dist, inv

    u, dist, inv = geometry()
    present = (
        lax.broadcasted_iota(jnp.int32, (depth, atoms), 0) < count_ref[...]
    ).astype(F32)
    scaled = jnp.minimum(dist * (1.0 / RCUT), 1.0)
    arg = math.pi * (scaled - 0.5)
    sq = arg * arg
    cos_y = 1.0
    for n in range(7, 0, -1):
        cos_y = 1.0 - cos_y * sq * (1.0 / ((2 * n - 1) * (2 * n)))
    sin_y = 1.0
    for n in range(6, 0, -1):
        sin_y = 1.0 - sin_y * sq * (1.0 / ((2 * n) * (2 * n + 1)))
    sin_y = sin_y * arg
    sines, cosines = {1: cos_y}, {1: -sin_y}
    for n in range(2, nbasis + 1):
        a, b = n // 2, n - n // 2
        sines[n] = sines[a] * cosines[b] + cosines[a] * sines[b]
        cosines[n] = cosines[a] * cosines[b] - sines[a] * sines[b]
    gap = 1.0 - scaled * scaled
    env = gap * gap * present * inv
    slope = -(4.0 / RCUT) * scaled * gap * present * inv - env * inv

    def strided_put(ref, j, plane):
        for h in range(own_tabs):
            ref[h, pl.ds(j, depth, stride=8), :] = plane[:, h * LANES : (h + 1) * LANES]

    def strided_get(ref, j):
        return jnp.concatenate(
            [ref[h, pl.ds(j, depth, stride=8), :] for h in range(own_tabs)], axis=1
        )

    def rows_get(ref, k):
        rows = pl.ds(pl.multiple_of(k * 8, 8), 8)
        return jnp.concatenate([ref[h, rows, :] for h in range(own_tabs)], axis=1)

    def rows_put(ref, k, value, add):
        rows = pl.ds(pl.multiple_of(k * 8, 8), 8)
        for h in range(own_tabs):
            part = value[:, h * LANES : (h + 1) * LANES]
            ref[h, rows, :] = ref[h, rows, :] + part if add else part

    for n in range(1, nbasis + 1):
        strided_put(bas, n - 1, sines[n] * env)
    ux, uy, uz = u
    harmonic = [
        ROOT3 * ux,
        ROOT3 * uy,
        ROOT3 * uz,
        ROOT15 * ux * uy,
        ROOT15 * uy * uz,
        ROOT15 * ux * uz,
        0.5 * ROOT15 * (ux * ux - uy * uy),
        0.5 * ROOT5 * (2.0 * uz * uz - ux * ux - uy * uy),
    ]
    for m in range(8):
        strided_put(ylm, m, harmonic[m])
    for n in range(1, nbasis + 1):
        strided_put(dbas, n - 1, (n * math.pi / RCUT) * cosines[n] * env + sines[n] * slope)
    for c in range(3):
        geo[c] = u[c]
    geo[3] = inv

    group = 16

    def y_row(k, m, h):
        return ylm[h, pl.ds(k * 8 + m - 1, 1), :]

    def slot_feature(k, g, h):
        return feat2[k, g * group : (g + 1) * group, h * LANES : (h + 1) * LANES]

    def accumulate(amp, ks, rad, feature):
        for h in range(own_tabs):
            lanes = slice(h * LANES, (h + 1) * LANES)
            for g in range(chans // group):
                rows = slice(g * group, (g + 1) * group)
                acc = [amp[m, rows, lanes] for m in range(9)]
                for k in ks:
                    ws = [
                        rad[k, deg * chans + g * group : deg * chans + (g + 1) * group, lanes]
                        for deg in range(3)
                    ]
                    if feature is not None:
                        f = feature(k, g, h)
                        ws = [w * f for w in ws]
                    acc[0] = acc[0] + ws[0]
                    for m in range(1, 9):
                        acc[m] = acc[m] + ws[DEGREE[m]] * y_row(k, m, h)
                for m in range(9):
                    amp[m, rows, lanes] = acc[m]

    def invariants_of(amp):
        sums = [None, None, None]
        for m in range(9):
            square = amp[m] * amp[m]
            deg = DEGREE[m]
            sums[deg] = square if sums[deg] is None else sums[deg] + square
        return jnp.concatenate(sums, axis=0) * norm

    act3b[...] = jnp.zeros_like(act3b)
    amp1[...] = jnp.zeros_like(amp1)
    amp2[...] = jnp.zeros_like(amp2)

    def hi_lo_hi(x):
        hi = x.astype(BF16).astype(F32)
        return [hi, x - hi, hi]

    def radial_in(kb, w_in, act, later):
        xs = []
        for j in range(per):
            k = kb * per + j
            rows = hi_lo_hi(rows_get(bas, k)) + hi_lo_hi(rows_get(dbas, k))
            xs.append(jnp.concatenate(rows, axis=0).astype(BF16))
        for j in range(per):
            pre = mm(w_in, xs[j])
            val, steep = silu_parts(pre[:hidden])
            act[:, j * atoms : (j + 1) * atoms] = rhs3(val)
            later[kb * per + j] = rhs3(steep * pre[hidden:])

    def radial_out(kb, w_out, act, rad, feature):
        for j in range(per):
            k = kb * per + j
            val = mm(w_out, act[:, j * atoms : (j + 1) * atoms])
            rad[k] = val if feature is None else val * feature(k)

    def radial_net(w_in, w_out, rad, later, feature, amp):
        def slots_of(kb):
            return [kb * per + j for j in range(per)]

        def step(p, carry):
            before = jnp.maximum(2 * p - 1, 0)
            radial_out(before, w_out, act3b, rad, feature)
            radial_in(2 * p, w_in, act3a, later)
            if amp is not None:
                accumulate(amp, slots_of(before), rad, None)
            radial_out(2 * p, w_out, act3a, rad, feature)
            radial_in(2 * p + 1, w_in, act3b, later)
            if amp is not None:
                accumulate(amp, slots_of(2 * p), rad, None)
            return carry

        lax.fori_loop(0, blocks // 2, step, 0)
        radial_out(blocks - 1, w_out, act3b, rad, feature)
        if amp is not None:
            accumulate(amp, slots_of(blocks - 1), rad, None)

    def scale_amp(amp, d_inv):
        for m in range(9):
            deg = DEGREE[m]
            amp[m] = amp[m] * d_inv[deg * chans : (deg + 1) * chans]

    def kind_feature(k):
        f = jnp.concatenate(
            [
                jnp.where(plane_row(kindd, k, h) > 0.5, embeds[1], embeds[0])
                for h in range(own_tabs)
            ],
            axis=1,
        )
        return jnp.concatenate([f, f, f], axis=0)

    radial_net(f1i, f1o, rad1, later1, kind_feature, amp1)
    inv1 = invariants_of(amp1)
    act1, slope1 = silu_parts(mm(mix_f, rhs3(inv1)))
    own_embed = jnp.where(kind_row > 0.5, embed_t[:, 1:2], embed_t[:, 0:1])
    layer_one = own_embed + act1
    for h in range(own_tabs):
        ftab[domains + h] = layer_one[:, h * LANES : (h + 1) * LANES]
    for t in range(domains):
        row = jnp.broadcast_to(exp_ref[t : t + 1, :], (chans, LANES))
        low = row & (LANES - 1)
        picked = lane_take(ftab[domains], low)
        for h in range(1, own_tabs):
            picked = jnp.where((row >> 7) == h, lane_take(ftab[domains + h], low), picked)
        fsend[t] = picked
    space_start(1, fsend, ftab)
    ftab[dom] = fsend[dom]

    radial_net(f2i, f2o, rad2, later2, None, None)
    def slope_step(k, carry):
        steep = mm(f1o, later1[k]) * kind_feature(k)
        for h in range(own_tabs):
            lanes = slice(h * LANES, (h + 1) * LANES)
            sums = [amp1[0, :, lanes], None, None]
            for m in range(1, 9):
                deg = DEGREE[m]
                term = amp1[m, :, lanes] * y_row(k, m, h)
                sums[deg] = term if sums[deg] is None else sums[deg] + term
            for deg in range(3):
                rows = slice(deg * chans, (deg + 1) * chans)
                rad1s[k, rows, lanes] = steep[rows, lanes] * sums[deg]
        return carry

    lax.fori_loop(0, 16, slope_step, 0, unroll=8)
    space_wait(1, fsend, ftab)

    many = 16

    def gather_step(kb, carry):
        ks = [kb * many + j for j in range(many)]
        for k in ks:
            low_row = whole_row(lowd, k)
            tab_row = whole_row(tabd, k)
            for h in range(own_tabs):
                lanes = slice(h * LANES, (h + 1) * LANES)
                low = jnp.broadcast_to(low_row[:, lanes], (chans, LANES))
                out = lane_take(ftab[0], low)
                for t in range(1, tables):
                    out = jnp.where(tab_row[:, lanes] == t, lane_take(ftab[t], low), out)
                feat2[k, :, lanes] = out
        accumulate(amp2, ks, rad2, slot_feature)
        return carry

    lax.fori_loop(0, depth // many, gather_step, 0)

    inv2 = invariants_of(amp2)
    unused, slope_r = silu_parts(mm(read_f, rhs3(inv2)))
    scale_amp(amp2, mm(read_b, rhs3(slope_r * energy_t)) * (2.0 * norm))

    sub = lax.broadcasted_iota(jnp.int32, (8, LANES), 0)

    def feature_pass(k):
        d_feats = []
        for h in range(own_tabs):
            lanes = slice(h * LANES, (h + 1) * LANES)
            total = None
            sums = [amp2[0, :, lanes], None, None]
            for m in range(1, 9):
                deg = DEGREE[m]
                term = amp2[m, :, lanes] * y_row(k, m, h)
                sums[deg] = term if sums[deg] is None else sums[deg] + term
            for deg in range(3):
                rows = slice(deg * chans, (deg + 1) * chans)
                if deg:
                    wgrad[k, rows, lanes] = sums[deg]
                part = sums[deg] * rad2[k, rows, lanes]
                total = part if total is None else total + part
            d_feats.append(total)
        return jnp.concatenate(d_feats, axis=1)

    def edge_pass(k, amp, rad, slopes, feature):
        d_ylms, d_rs = [], []
        steep_all = slopes(k)
        for h in range(own_tabs):
            lanes = slice(h * LANES, (h + 1) * LANES)
            rads = [rad[k, deg * chans : (deg + 1) * chans, lanes] for deg in range(3)]
            steep = [steep_all[deg * chans : (deg + 1) * chans, lanes] for deg in range(3)]
            ws = rads
            if feature is not None:
                f = jnp.concatenate([feature(k, g, h) for g in range(chans // group)], axis=0)
                ws = [r * f for r in rads]
            parts = []
            for m in range(1, 9):
                parts.append(fold(amp[m, :, lanes] * ws[DEGREE[m]]))
            d_ylms.append(rows_to_tile(parts, sub))
            by_r = None
            for deg in range(3):
                rows = slice(deg * chans, (deg + 1) * chans)
                if feature is None:
                    scale = d_inv1[rows, lanes]
                elif deg == 0:
                    scale = amp[0, :, lanes]
                else:
                    scale = wgrad[k, rows, lanes]
                by_r = scale * steep[deg] if by_r is None else by_r + scale * steep[deg]
            if feature is not None:
                by_r = by_r * f
            d_rs.append(fold(by_r))
        return jnp.concatenate(d_ylms, axis=1), d_rs

    def fold(x):
        return (x[0:8] + x[8:16]) + (x[16:24] + x[24:32])

    def distances_put(p, d_rs, add):
        rows = pl.ds(pl.multiple_of(p * 8, 8), 8)
        for h in range(own_tabs):
            tile = rows_to_tile([d[h] for d in d_rs], sub)
            r_grad[h, rows, :] = r_grad[h, rows, :] + tile if add else tile

    acc_g[...] = jnp.zeros_like(acc_g)
    lhs_b[...] = jnp.zeros_like(lhs_b)

    def second_features(kb, lhs):
        for j in range(per):
            k = kb * per + j
            hi, lo = split(feature_pass(k))
            both = jnp.concatenate([hi, lo], axis=0)
            tab_row = whole_row(tabd, k)
            for t in range(tables):
                hit = (tab_row == t).astype(F32).astype(BF16)
                lhs[t * 2 * chans : (t + 1) * 2 * chans, j * atoms : (j + 1) * atoms] = both * hit

    def scatter_block(kb, lhs):
        hot = jnp.concatenate([onehot[kb * per + j] for j in range(per)], axis=1)
        acc_g[...] += mm_nt(lhs[...], hot)

    def second_back(p, carry):
        scatter_block(jnp.maximum(2 * p - 1, 0), lhs_b)
        second_features(2 * p, lhs_a)
        scatter_block(2 * p, lhs_a)
        second_features(2 * p + 1, lhs_b)
        return carry

    lax.fori_loop(0, blocks // 2, second_back, 0)
    scatter_block(blocks - 1, lhs_b)

    def edges_step(amp, rad, slopes, feature, add):
        def step(p, carry):
            d_rs = []
            for j in range(8):
                k = p * 8 + j
                d_ylm, d_r_k = edge_pass(k, amp, rad, slopes, feature)
                rows_put(ylm_grad, k, d_ylm, add)
                d_rs.append(d_r_k)
            distances_put(p, d_rs, add)
            return carry

        lax.fori_loop(0, depth // 8, step, 0)

    def table_grad(t):
        base = t * 2 * chans
        return acc_g[base : base + chans, :] + acc_g[base + chans : base + 2 * chans, :]

    for t in range(domains):
        gsend[t] = table_grad(t)
    space_start(2, gsend, gback)
    gback[dom] = gsend[dom]
    edges_step(amp2, rad2, lambda k: mm(f2o, later2[k]), slot_feature, False)

    lax.fori_loop(16, depth, slope_step, 0, unroll=8)
    own_grad = jnp.concatenate([table_grad(domains + h) for h in range(own_tabs)], axis=1)
    space_wait(2, gsend, gback)

    def to_owner(back):
        rows = back.shape[1]
        flat = jnp.concatenate([back[t] for t in range(domains)], axis=1)
        hi = flat.astype(BF16).astype(F32)
        both = jnp.concatenate([hi, flat - hi], axis=0).astype(BF16)
        out = mm_nt(both, onehot_exp[...])
        return out[:rows] + out[rows:]

    d_layer = own_grad + to_owner(gback)
    d_inv1[...] = mm(mix_b, rhs3(d_layer * slope1)) * (2.0 * norm)
    scale_amp(amp1, d_inv1[...])

    edges_step(amp1, rad1, lambda k: rad1s[k], None, True)

    ux, uy, uz = geo[0], geo[1], geo[2]
    d_r = jnp.concatenate([r_grad[h] for h in range(own_tabs)], axis=1)
    dy = [strided_get(ylm_grad, m) for m in range(8)]
    dux = ROOT3 * dy[0] + ROOT15 * (uy * dy[3] + uz * dy[5] + ux * dy[6]) - ROOT5 * (ux * dy[7])
    duy = ROOT3 * dy[1] + ROOT15 * (ux * dy[3] + uz * dy[4] - uy * dy[6]) - ROOT5 * (uy * dy[7])
    duz = ROOT3 * dy[2] + ROOT15 * (uy * dy[4] + ux * dy[5]) + (2.0 * ROOT5) * (uz * dy[7])
    along = d_r - geo[3] * (ux * dux + uy * duy + uz * duz)
    d_off = [geo[3] * d + v * along for d, v in ((dux, ux), (duy, uy), (duz, uz))]
    centre = jnp.concatenate([jnp.sum(d, axis=0, keepdims=True) for d in d_off], axis=0)
    for c in range(3):
        for h in range(own_tabs):
            doff[c, h] = d_off[c][:, h * LANES : (h + 1) * LANES]

    acc_x[...] = jnp.zeros_like(acc_x)

    def force_rows(k, carry):
        tab_row = whole_row(tabd, k)
        hit = tab_row == lax.broadcasted_iota(jnp.int32, (8, atoms), 0)
        rows = [jnp.where(hit, whole_row(doff.at[c], k), 0.0) for c in range(3)]
        full = jnp.concatenate(rows, axis=0)
        hi = full.astype(BF16).astype(F32)
        lhs_x[k] = jnp.concatenate([hi, full - hi], axis=0).astype(BF16)
        return carry

    lax.fori_loop(0, depth, force_rows, 0, unroll=4)
    long = 48

    def force_step(kb, carry):
        ks = [kb * long + j for j in range(long)]
        left = jnp.concatenate([lhs_x[k] for k in ks], axis=1)
        hot = jnp.concatenate([onehot[k] for k in ks], axis=1)
        acc_x[...] += mm_nt(left, hot)
        return carry

    lax.fori_loop(0, depth // long, force_step, 0)
    table_force = [acc_x[c * 8 : (c + 1) * 8, :] + acc_x[24 + c * 8 : 32 + c * 8, :] for c in range(3)]
    pad = jnp.zeros((5, LANES), F32)
    for t in range(domains):
        xsend[t] = jnp.concatenate([f[t : t + 1] for f in table_force] + [pad], axis=0)
    space_start(3, xsend, xback)
    xback[dom] = xsend[dom]
    own_force = jnp.concatenate(
        [
            jnp.concatenate([f[domains + h : domains + h + 1] for f in table_force], axis=0)
            for h in range(own_tabs)
        ],
        axis=1,
    )

    bead_wait(0, qall)
    half_step = 0.5 * beads / 3.0
    partial = mom_ref[...].reshape(3, atoms) - half_step * (own_force - centre)
    wqq, wqp, wpq = circulant_weights(beads)
    q_q = sum(float(wqq[d]) * qall[d] for d in range(beads))
    p_q = sum(float(wpq[d]) * qall[d] for d in range(beads))
    space_wait(3, xsend, xback)
    kicked = partial - half_step * to_owner(xback)[0:3]
    for h in range(own_tabs):
        ptile[4 * h : 4 * h + 3] = kicked[:, h * LANES : (h + 1) * LANES]
        ptile[4 * h + 3 : 4 * h + 4] = zero_row

    for d in far_first(beads):
        bead_copy(1, ptile, pall.at[d], d).start()
    pall[0] = ptile[...]
    mass = jnp.concatenate(
        [
            jnp.broadcast_to(
                jnp.where(kind_row[:, h * LANES : (h + 1) * LANES] > 0.5, MASS_HYDROGEN, MASS_OXYGEN),
                (4, LANES),
            )
            for h in range(own_tabs)
        ],
        axis=0,
    )

    bead_wait(1, pall)
    q_p = sum(float(wqp[d]) * pall[d] for d in range(beads))
    p_p = sum(float(wqq[d]) * pall[d] for d in range(beads))
    new_q = q_q + q_p / mass
    new_p = p_p - mass * p_q
    for h in range(own_tabs):
        lanes = slice(h * LANES, (h + 1) * LANES)
        out_ref[0:3, 0, lanes] = new_q[4 * h : 4 * h + 3]
        out_ref[3:6, 0, lanes] = new_p[4 * h : 4 * h + 3]


def shards(
    positions,
    momenta,
    species,
    neighbours,
    counts,
    exports,
    embed,
    radial_one_in,
    radial_one_out,
    mix_one,
    radial_two_in,
    radial_two_out,
    readout,
    energy_w,
):
    beads = lax.axis_size("bead")
    domains = lax.axis_size("space")
    depth, atoms = neighbours.shape[1:]
    chans = embed.shape[1]
    nbasis, hidden = radial_one_in.shape
    tables = atoms // LANES + domains
    per = 8
    vmem = pltpu.VMEM
    scratch = [
        vmem((8, LANES), F32),
        vmem((beads, 8, LANES), F32),
        vmem((8, LANES), F32),
        vmem((beads, 8, LANES), F32),
        vmem((domains, 8, LANES), F32),
        vmem((tables, 8, LANES), F32),
        vmem((domains, chans, LANES), F32),
        vmem((tables, chans, LANES), F32),
        vmem((domains, chans, LANES), F32),
        vmem((domains, chans, LANES), F32),
        vmem((domains, 8, LANES), F32),
        vmem((domains, 8, LANES), F32),
        vmem((2, depth * 8, LANES), F32),
        vmem((2, depth * 8, LANES), F32),
        vmem((2, depth * 8, LANES), F32),
        vmem((4, depth, atoms), F32),
        vmem((3, 2, depth, LANES), F32),
        vmem((2, depth, LANES), F32),
        vmem((2, depth, LANES), jnp.int32),
        vmem((2, depth, LANES), jnp.int32),
        vmem((2, chans, LANES), F32),
        vmem((depth, 3 * chans, atoms), F32),
        vmem((depth, 3 * chans, atoms), F32),
        vmem((depth, 3 * chans, atoms), F32),
        vmem((depth, 3 * hidden, atoms), BF16),
        vmem((depth, 3 * hidden, atoms), BF16),
        vmem((depth, 3 * chans, atoms), F32),
        vmem((3 * chans, atoms), F32),
        vmem((depth, chans, atoms), F32),
        vmem((9, chans, atoms), F32),
        vmem((9, chans, atoms), F32),
        vmem((depth, LANES, atoms), BF16),
        vmem((atoms, domains * LANES), BF16),
        vmem((tables * 2 * chans, per * atoms), BF16),
        vmem((tables * 2 * chans, per * atoms), BF16),
        vmem((tables * 2 * chans, LANES), F32),
        vmem((depth, 48, atoms), BF16),
        vmem((48, LANES), F32),
        vmem((2, depth, LANES), F32),
        vmem((2, depth * 8, LANES), F32),
        vmem((3 * hidden, per * atoms), BF16),
        vmem((3 * hidden, per * atoms), BF16),
        pltpu.SemaphoreType.DMA((domains + 2,)),
        pltpu.SemaphoreType.DMA((domains + 2,)),
    ]
    whole = pl.BlockSpec(memory_space=pltpu.VMEM)
    moved = pl.pallas_call(
        functools.partial(kernel, beads, domains),
        out_shape=jax.ShapeDtypeStruct((6, 1, atoms), F32),
        in_specs=[whole] * 14,
        out_specs=whole,
        scratch_shapes=scratch,
        compiler_params=pltpu.CompilerParams(
            collective_id=0, has_side_effects=True, vmem_limit_bytes=56 * 1024 * 1024
        ),
    )(
        positions.transpose(1, 0, 2),
        momenta.transpose(1, 0, 2),
        species.reshape(1, atoms),
        neighbours[0],
        counts,
        exports[0, 0],
        embed,
        radial_one_in,
        radial_one_out,
        mix_one.T,
        radial_two_in,
        radial_two_out,
        readout.T,
        energy_w.reshape(1, hidden),
    )
    return moved[:3].transpose(1, 0, 2), moved[3:].transpose(1, 0, 2)


def solution(mesh):
    placed = (
        P("bead", None, "space"),
        P("bead", None, "space"),
        P("space"),
        P("bead", None, "space"),
        P("bead", "space"),
        P("bead", "space", None, None),
        P(),
        P(),
        P(),
        P(),
        P(),
        P(),
        P(),
        P(),
    )
    return jax.shard_map(
        shards,
        mesh=mesh,
        in_specs=placed,
        out_specs=(P("bead", None, "space"), P("bead", None, "space")),
        check_vma=False,
    )
```
